128 devices in a mesh: skyx: 8 (over x, core), skyy: 16 (over z, y).
Axes of the slice: x: 4, y: 4, z: 4, core: 2. Of those that a mesh axis runs over, the one named last changes fastest.
Arguments:
- tiles: bfloat16 [16384, 6, 4096], P(('skyx', 'skyy')), may hold values from -6 to 6
- tile_weight: bfloat16 [16384, 6], P(('skyx', 'skyy')), may hold values from 0.25 to 4
- owners: int32 [16384, 1], P(('skyx', 'skyy')), may hold values from 0 to 127; in each aligned block of 128 rows (0 to 127, 128 to 255, ...) at most 2 rows name the same one
- cells: int32 [16384], P(('skyx', 'skyy')), may hold values from 0 to 3
- psf_kernel: float32 [6, 9, 9], replicated, may hold values from -0.72 to 0.72
- conv1_weight: bfloat16 [64, 6, 3, 3], replicated, may hold values from -0.875 to 0.875
- conv1_bias: float32 [64], replicated, may hold values from -3 to 3
- conv2_weight: bfloat16 [64, 64, 3, 3], replicated, may hold values from -0.25 to 0.25
- conv2_bias: float32 [64], replicated, may hold values from -3 to 3
Outputs:
- psf_image: bfloat16 [6, 2048, 1024], P(None, 'skyy', 'skyx')
- detection: bfloat16 [64, 2048, 1024], P(None, 'skyy', 'skyx')
The draws below stay inside these ranges and needn't reach their ends.
Inputs may be any that keep to these rules, and one draw needn't show every extreme that they name: `owners`: among the 128 tiles of one device at most 2 name the same owner, and every owner is named by some tile.
All inputs are finite; a program needn't handle non-finite values.
Results may differ from the reference program's by a relative error of at most 0.0035.
Values may be sent and summed in bfloat16 or wider, within the bound.
A program may use at most 192 MiB of HBM per device.

```python
import math
import jax
import jax.numpy as jnp
import numpy as np
from jax import lax

B = 6
C = 64
S = 64
G = 2
TPD = 128
CAP = 2
TILES = 16384
N_SKYX = 8
N_SKYY = 16
DEVICES = 128


def with_ends(entries, stream_key, least, high):
    shape = entries.shape
    index_at = [jax.random.randint(jax.random.fold_in(stream_key, axis), (), 0, shape[axis]) for axis in range(len(shape))]
    entries = entries.at[tuple(index_at)].set(least)
    longest = shape.index(max(shape))
    index_at[longest] = (index_at[longest] + 1) % shape[longest]
    return entries.at[tuple(index_at)].set(high)


def steps_of(rng, dims, cuts, smallest, high):
    loudness, own = 1.0, jax.random.fold_in(rng, 6)
    for dim, shards_of in cuts:
        steps = jnp.exp(jax.random.uniform(jax.random.fold_in(own, dim), (shards_of,), jnp.float32, smallest / len(cuts), high / len(cuts)))
        loudness = loudness * jnp.repeat(steps, dims[dim] // shards_of).reshape([-1 if axis == dim else 1 for axis in range(len(dims))])
    return loudness


def shared_out(own_key, own, number, rows, count, top, reach, skew):
    sequence = jax.random.permutation(own_key, count)
    crowded, usual = load_shares(count, rows * top, reach, skew, True), load_shares(count, rows * top, reach, skew, False)
    places = jnp.arange(count)

    def named(sizes, turn):
        used = int((sizes > 0).sum())
        fixed = max(1, used // 4)
        shifted = fixed + (places - fixed + turn * (used - fixed)) % max(1, count - fixed)
        return jnp.zeros((count,), jnp.int32).at[sequence[jnp.where(places < fixed, places, shifted)]].set(jnp.asarray(sizes, jnp.int32))

    sizes = jnp.where(number % 4 == 0, named(crowded, number // 4), named(usual, number - number // 4 - 1))
    mixed = jax.random.permutation(jax.random.fold_in(own, 3), count)
    giver, receiver = mixed[0:count // 2 * 2:2], mixed[1:count // 2 * 2:2]
    slack = jnp.minimum(sizes[giver] - 1, reach - sizes[receiver]) // 2
    slack = jnp.where((giver == sequence[0]) | (receiver == sequence[0]) | (sizes[receiver] == 0), 0, jnp.maximum(slack, 0))
    shifted = jax.random.randint(jax.random.fold_in(own, 4), (count // 2,), 0, 1 << 20) % (slack + 1)
    sizes = sizes.at[giver].add(-shifted).at[receiver].add(shifted)
    items = jnp.searchsorted(jnp.cumsum(sizes), jnp.arange(rows * top), side="right").astype(jnp.int32)
    table = items.reshape(top, rows).T
    table = table[jax.random.permutation(jax.random.fold_in(own, 1), rows)]
    turn = jax.random.randint(jax.random.fold_in(own, 2), (rows, 1), 0, top)
    return jnp.take_along_axis(table, (jnp.arange(top)[None, :] + turn) % top, axis=1)


def load_shares(amount, total, reach, skew, full):
    weights = [(1 << 20) // math.isqrt(rank ** skew) + 1 for rank in range(1, amount + 1)]
    largest = reach if full else min(reach, max(-(-total // amount), total * weights[0] // sum(weights)))
    least = 1 if total - largest >= amount - 1 else 0
    counts, spare = [largest] + [least] * (amount - 1), total - largest - least * (amount - 1)
    while spare > 0:
        free = [i for i in range(1, amount) if counts[i] < largest] or [i for i in range(1, amount) if counts[i] < reach]
        mass, remaining = sum([weights[i] for i in free]), spare
        for i in free:
            extra = min(reach - counts[i], max(1, remaining * weights[i] // mass), spare)
            counts[i] = counts[i] + extra
            spare = spare - extra
    return np.array(counts)


def noise(rng, shape, scale, reach, pieces=(), kind=jnp.bfloat16):
    values = jax.random.normal(rng, shape, jnp.float32) * scale
    if len(pieces) > 0:
        values = steps_of(rng, shape, pieces, -0.22, 0.18) * values
    return jnp.clip(values, min=-reach, max=reach).astype(kind)


def setup_inputs(seed: int = 0) -> dict:
    keys = jax.random.split(jax.random.key(seed), 10)
    tiles = noise(keys[0], (TILES, B, S * S), 1.0, 6.0, ((0, 128),))
    tile_weight = jnp.clip(jnp.exp(math.log(4.0) - 2.7725887 * jax.random.uniform(keys[1], (TILES, B), jnp.float32) ** steps_of(keys[1], (TILES, B), ((0, 128),), -0.2, 0.2)), 0.25, 4.0).astype(jnp.bfloat16)
    owners_keys = jax.random.split(jax.random.fold_in(keys[2], 1), TILES // TPD)
    owners_turns = jax.random.permutation(jax.random.fold_in(keys[2], 3), TILES // TPD)
    owners = jax.vmap(lambda own, number: shared_out(jax.random.fold_in(keys[2], 2), own, number, TPD, DEVICES, 1, CAP, 2))(owners_keys, owners_turns).reshape((TILES, 1))
    cells = with_ends(jax.random.randint(keys[3], (TILES,), 0, G * G), jax.random.fold_in(keys[3], 1), 0, (G * G) - 1).astype(jnp.int32)
    psf_kernel = noise(keys[4], (B, 9, 9), 0.12, 0.72, (), jnp.float32)
    conv1_weight = noise(keys[5], (C, B, 3, 3), (B * 9) ** -0.5, 0.875)
    conv1_bias = noise(keys[6], (C,), 0.5, 3.0, (), jnp.float32)
    conv2_weight = noise(keys[7], (C, C, 3, 3), (C * 9) ** -0.5, 0.25)
    conv2_bias = noise(keys[8], (C,), 0.5, 3.0, (), jnp.float32)
    return {"tiles": tiles, "tile_weight": tile_weight, "owners": owners, "cells": cells, "psf_kernel": psf_kernel, "conv1_weight": conv1_weight, "conv1_bias": conv1_bias, "conv2_weight": conv2_weight, "conv2_bias": conv2_bias}


def conv_layer(source, weight, offset):
    result = lax.conv_general_dilated(source.astype(jnp.float32)[None], weight.astype(jnp.float32), (1, 1), ((1, 1), (1, 1)), precision=lax.Precision.HIGHEST)[0]
    return result + offset[:, None, None]


def reference(tiles, tile_weight, owners, cells, psf_kernel, conv1_weight, conv1_bias, conv2_weight, conv2_bias):
    blocks_x = G * N_SKYX
    blocks_y = G * N_SKYY
    owner = owners[:, 0]
    col_device = owner // N_SKYY
    row_device = owner % N_SKYY
    block_index = ((row_device * G + cells // G) * blocks_x + col_device * G + cells % G).astype(jnp.int32)
    tile_blocks = tiles.reshape(DEVICES, TPD, B, S * S)
    weight_blocks = tile_weight.reshape(DEVICES, TPD, B)
    index_blocks = block_index.reshape(DEVICES, TPD)

    def add_block(carry, item):
        numer, denom = carry
        block_tiles, block_weight, block_ids = item
        weight_full = block_weight.astype(jnp.float32)
        numer = numer.at[block_ids].add(block_tiles.astype(jnp.float32) * weight_full[:, :, None])
        denom = denom.at[block_ids].add(weight_full)
        return (numer, denom), None

    start = (jnp.zeros((blocks_y * blocks_x, B, S * S), jnp.float32), jnp.zeros((blocks_y * blocks_x, B), jnp.float32))
    (numer, denom), unused = lax.scan(add_block, start, (tile_blocks, weight_blocks, index_blocks))
    coadd = numer / (1.0 + denom)[:, :, None]
    coadd_image = coadd.reshape(blocks_y, blocks_x, B, S, S).transpose(2, 0, 3, 1, 4).reshape(B, blocks_y * S, blocks_x * S)
    matched = lax.conv_general_dilated(coadd_image[None], psf_kernel[:, None], (1, 1), ((4, 4), (4, 4)), feature_group_count=B, precision=lax.Precision.HIGHEST)[0]
    psf_image = matched.astype(jnp.bfloat16)
    hidden = jax.nn.silu(conv_layer(psf_image, conv1_weight, conv1_bias)).astype(jnp.bfloat16)
    detection = conv_layer(hidden, conv2_weight, conv2_bias).astype(jnp.bfloat16)
    return psf_image, detection
```

```python
import functools

import jax
import jax.numpy as jnp
from jax import lax
from jax.experimental import pallas as pl
from jax.experimental.pallas import tpu as pltpu
from jax.sharding import PartitionSpec as P

MESH = pl.DeviceIdType.MESH
F32 = jnp.float32
BF16 = jnp.bfloat16

NB = 6
HALF = 2048
WIDE = HALF + 128
ORDER = (0, 2, 4, 1, 3, 5)
MEMBERS = ((2, 0), (2, 1), (1, 0), (3, 0), (1, 1), (3, 1), (0, 1))
AROUND = ((-1, 0), (1, 0), (0, -1), (0, 1), (-1, -1), (-1, 1), (1, -1), (1, 1))


def exchange_kernel(
    tiles_hbm,
    wt_ref,
    own_ref,
    cell_ref,
    img_ref,
    halo_ref,
    tin,
    sel,
    meta,
    metar,
    send_a,
    send_b,
    recv_a,
    recv_b,
    st2,
    rcv2,
    st3,
    rcv3,
    tbuf,
    hsend,
    hrecv,
    tin_sem,
    self_sem,
    s1_send,
    s1_recv,
    s2_send,
    s2_recv,
    s3_send,
    s3_recv,
    h_send,
    h_recv,
):
    ix = lax.axis_index("skyx")
    iy = lax.axis_index("skyy")
    core = ix % 2
    q = (ix // 2, iy % 4, iy // 4)

    def device(axis, step, flip):
        r = list(q)
        if step:
            r[axis] = (r[axis] + step) % 4
        c = (core + flip) % 2 if flip else core
        return (r[0] * 2 + c, r[2] * 4 + r[1])

    def around(dy, dx):
        return ((ix + dx + 8) % 8, (iy + dy + 16) % 16)

    barrier = pltpu.get_barrier_semaphore()
    peers = [device(0, 0, 1)]
    for axis in range(3):
        for step, flip in MEMBERS[:6]:
            peers.append(device(axis, step, flip))
    for dy, dx in AROUND:
        peers.append(around(dy, dx))
    for peer in peers:
        pl.semaphore_signal(barrier, inc=1, device_id=peer, device_id_type=MESH)

    tin_copies = {}
    for b in ORDER:
        tin_copies[b] = pltpu.make_async_copy(tiles_hbm.at[b], tin.at[b], tin_sem.at[b])
        tin_copies[b].start()

    own = own_ref[...]
    ox, oy = own // 16, own % 16
    oq = (ox // 2, oy % 4, oy // 4)
    oc = ox % 2
    ownf = jnp.broadcast_to(own.astype(F32), (128, 128))
    same = ownf == ownf.T
    earlier = lax.broadcasted_iota(jnp.int32, (128, 128), 0) < lax.broadcasted_iota(
        jnp.int32, (128, 128), 1
    )
    rank = jnp.sum(jnp.where(same & earlier, 1.0, 0.0), axis=0, keepdims=True).astype(jnp.int32)
    rows = lax.broadcasted_iota(jnp.int32, (256, 128), 0)
    for p in range(3):
        slot = (oq[p] * 2 + oc) * 32 + (oq[(p + 1) % 3] * 4 + oq[(p + 2) % 3]) * 2 + rank
        sel[p] = jnp.where(rows == slot, 1.0, 0.0).astype(BF16)
    meta[...] = jnp.zeros((128, 128), F32)
    meta[0:6, :] = wt_ref[...].astype(F32)
    meta[6:7, :] = cell_ref[...].astype(F32) + 1.0

    s1 = {}

    def stage1_refs(b):
        p, k = b // 2, b % 2
        return (send_a.at[p], recv_a.at[p]) if k == 0 else (send_b.at[p], recv_b.at[p])

    for n, b in enumerate(ORDER):
        p, k = b // 2, b % 2
        src, dst = stage1_refs(b)
        tin_copies[b].wait()

        def gather(c, carry, b=b, p=p, src=src):
            at = pl.ds(pl.multiple_of(c * 512, 512), 512)
            src[:, at] = jnp.dot(sel[p], tin[b, :, at], preferred_element_type=F32).astype(BF16)
            return carry

        lax.fori_loop(0, 8, gather, 0)
        if k == 0:
            src[:, 4096:4224] = lax.dot_general(
                sel[p],
                meta[...].astype(BF16),
                (((1,), (1,)), ((), ())),
                preferred_element_type=F32,
            ).astype(BF16)
        if n == 0:
            pl.semaphore_wait(barrier, len(peers))
        mine = q[p] * 2 + core
        mine_rows = pl.ds(pl.multiple_of(mine * 32, 32), 32)
        own_copy = pltpu.make_async_copy(src.at[mine_rows], dst.at[mine_rows], self_sem.at[b])
        own_copy.start()
        copies = [own_copy]
        for m, (step, flip) in enumerate(MEMBERS):
            there = ((q[p] + step) % 4) * 2 + (core + flip) % 2
            copy = pltpu.make_async_remote_copy(
                src_ref=src.at[pl.ds(pl.multiple_of(there * 32, 32), 32)],
                dst_ref=dst.at[mine_rows],
                send_sem=s1_send.at[b, m],
                recv_sem=s1_recv.at[b, m],
                device_id=device(p, step, flip),
                device_id_type=MESH,
            )
            copy.start()
            copies.append(copy)
        s1[b] = copies

    s2, s3 = {}, {}

    def reduce_tiles(b):
        p, k = b // 2, b % 2
        src, dst = stage1_refs(b)
        s1[b][0].wait()
        for copy in s1[b][1:]:
            copy.wait_recv()
        if k == 0:
            metar[p] = dst[:, 4096:4224].astype(F32).T[0:8, :]
        w = metar[p, b : b + 1, :]
        code = metar[p, 6:7, :].astype(jnp.int32)
        row = lax.broadcasted_iota(jnp.int32, (128, 256), 0)
        col = lax.broadcasted_iota(jnp.int32, (128, 256), 1)
        hit = ((col % 32) // 2 == row // 8) & (code == row % 4 + 1)
        upper = (row // 4) % 2 == 0
        both = jnp.where(hit, jnp.broadcast_to(w, (128, 256)), 0.0)
        c0 = jnp.where(upper, both, 0.0).astype(BF16)
        c1 = jnp.where(upper, 0.0, both).astype(BF16)
        st2[b, :, HALF:WIDE] = jnp.broadcast_to(
            jnp.sum(both, axis=1, keepdims=True), (128, 128)
        )

        def reduce(c, carry):
            lo = pl.ds(pl.multiple_of(c * 512, 512), 512)
            hi = pl.ds(pl.multiple_of(c * 512 + HALF, 512), 512)
            st2[b, :, lo] = jnp.dot(c0, dst[:, lo], preferred_element_type=F32) + jnp.dot(
                c1, dst[:, hi], preferred_element_type=F32
            )
            return carry

        lax.fori_loop(0, 4, reduce, 0)
        axis = (p + 1) % 3
        copies = []
        for step in (2, 1, 3):
            there = (q[axis] + step) % 4
            copy = pltpu.make_async_remote_copy(
                src_ref=st2.at[b, pl.ds(pl.multiple_of(there * 32, 32), 32)],
                dst_ref=rcv2.at[b, step - 1],
                send_sem=s2_send.at[b, step - 1],
                recv_sem=s2_recv.at[b, step - 1],
                device_id=device(axis, step, 0),
                device_id_type=MESH,
            )
            copy.start()
            copies.append(copy)
        s2[b] = copies

    def second(b):
        p = b // 2
        axis = (p + 1) % 3
        for copy in s2[b]:
            copy.wait_recv()
        at = pl.ds(pl.multiple_of(q[axis] * 32, 32), 32)
        st3[b] = (st2[b, at, :] + rcv2[b, 0]) + (rcv2[b, 1] + rcv2[b, 2])
        axis = (p + 2) % 3
        copies = []
        for step in (2, 1, 3):
            there = (q[axis] + step) % 4
            copy = pltpu.make_async_remote_copy(
                src_ref=st3.at[b, pl.ds(pl.multiple_of(there * 8, 8), 8)],
                dst_ref=rcv3.at[b, step - 1],
                send_sem=s3_send.at[b, step - 1],
                recv_sem=s3_recv.at[b, step - 1],
                device_id=device(axis, step, 0),
                device_id_type=MESH,
            )
            copy.start()
            copies.append(copy)
        s3[b] = copies

    left_half = lax.broadcasted_iota(jnp.int32, (16, 128), 1) < 64

    def third(b):
        p = b // 2
        axis = (p + 2) % 3
        for copy in s3[b]:
            copy.wait_recv()
        at = pl.ds(pl.multiple_of(q[axis] * 8, 8), 8)
        total = (st3[b, at, :] + rcv3[b, 0]) + (rcv3[b, 1] + rcv3[b, 2])
        scale = 1.0 / (1.0 + total[:, HALF:WIDE])
        for j in range(16):
            tbuf[pl.ds(j, 8, stride=16), :] = total[:, 128 * j : 128 * j + 128] * scale
        for h in range(2):
            for cy in range(2):
                s = h * 4 + cy * 2
                a = tbuf[16 * s : 16 * s + 16, :]
                c = tbuf[16 * s + 16 : 16 * s + 32, :]
                y0 = 64 * cy + 32 * h
                img_ref[b, pl.ds(y0, 16, stride=2), :] = jnp.where(
                    left_half, a, pltpu.roll(c, 64, 1)
                )
                img_ref[b, pl.ds(y0 + 1, 16, stride=2), :] = jnp.where(
                    left_half, pltpu.roll(a, 64, 1), c
                )
        hsend[0, b] = img_ref[b, 0:8, :]
        hsend[1, b] = img_ref[b, 120:128, :]
        turned = img_ref[b].T
        hsend[2, b] = turned[0:8, :]
        hsend[3, b] = turned[120:128, :]

    todo = []
    for n in range(6 + 4):
        if n < 6:
            todo.append((reduce_tiles, n))
        if 0 <= n - 2 < 6:
            todo.append((second, n - 2))
        if 0 <= n - 4 < 6:
            todo.append((third, n - 4))
    for step_fn, n in todo:
        step_fn(ORDER[n])

    halo = []
    for n, (dy, dx) in enumerate(AROUND):
        which = 0 if dy < 0 else 1 if dy > 0 else 2 if dx < 0 else 3
        copy = pltpu.make_async_remote_copy(
            src_ref=hsend.at[which],
            dst_ref=hrecv.at[n],
            send_sem=h_send.at[n],
            recv_sem=h_recv.at[n],
            device_id=around(dy, dx),
            device_id_type=MESH,
        )
        copy.start()
        halo.append(copy)
    for b in ORDER:
        for copy in s1[b][1:] + s2[b] + s3[b]:
            copy.wait_send()
    for n, copy in enumerate(halo):
        copy.wait_recv()
        halo_ref[n] = hrecv[n]
    for copy in halo:
        copy.wait_send()


def exchange(tiles, weights, owners, cells):
    vmem = pl.BlockSpec(memory_space=pltpu.VMEM)
    dma = pltpu.SemaphoreType.DMA
    return pl.pallas_call(
        exchange_kernel,
        out_shape=(
            jax.ShapeDtypeStruct((NB, 128, 128), F32),
            jax.ShapeDtypeStruct((8, NB, 8, 128), F32),
        ),
        in_specs=[pl.BlockSpec(memory_space=pl.ANY), vmem, vmem, vmem],
        out_specs=(vmem, vmem),
        scratch_shapes=[
            pltpu.VMEM((NB, 128, 4096), BF16),
            pltpu.VMEM((3, 256, 128), BF16),
            pltpu.VMEM((128, 128), F32),
            pltpu.VMEM((3, 8, 256), F32),
            pltpu.VMEM((3, 256, 4224), BF16),
            pltpu.VMEM((3, 256, 4096), BF16),
            pltpu.VMEM((3, 256, 4224), BF16),
            pltpu.VMEM((3, 256, 4096), BF16),
            pltpu.VMEM((NB, 128, WIDE), F32),
            pltpu.VMEM((NB, 3, 32, WIDE), F32),
            pltpu.VMEM((NB, 32, WIDE), F32),
            pltpu.VMEM((NB, 3, 8, WIDE), F32),
            pltpu.VMEM((128, 128), F32),
            pltpu.VMEM((4, NB, 8, 128), F32),
            pltpu.VMEM((8, NB, 8, 128), F32),
            dma((NB,)),
            dma((NB,)),
            dma((NB, 7)),
            dma((NB, 7)),
            dma((NB, 3)),
            dma((NB, 3)),
            dma((NB, 3)),
            dma((NB, 3)),
            dma((8,)),
            dma((8,)),
        ],
        compiler_params=pltpu.CompilerParams(
            collective_id=0, has_side_effects=True, vmem_limit_bytes=60 * 1024 * 1024
        ),
        name="tile_exchange",
    )(tiles, weights, owners, cells)


def detect_kernel(
    taps_ref,
    img_ref,
    halo_ref,
    w1_ref,
    b1_ref,
    w2_ref,
    b2_ref,
    psf_ref,
    det_ref,
    ext,
    shifted,
    psf,
    taps3,
    hidden,
    turned,
):
    ix = lax.axis_index("skyx")
    iy = lax.axis_index("skyy")
    top, bottom = (iy > 0).astype(F32), (iy < 15).astype(F32)
    left, right = (ix > 0).astype(F32), (ix < 7).astype(F32)
    lane = lax.broadcasted_iota(jnp.int32, (8, 128), 1)
    side = jnp.where(lane < 64, right, left)
    taps3[...] = jnp.zeros_like(taps3)

    for b in range(NB):
        ext[b, 0, 8:136, :] = img_ref[b]
        ext[b, 0, 0:8, :] = halo_ref[1, b] * top
        ext[b, 0, 136:144, :] = halo_ref[0, b] * bottom
        columns = jnp.concatenate(
            [halo_ref[2, b] * right, jnp.zeros((112, 128), F32), halo_ref[3, b] * left], axis=0
        )
        ext[b, 1, 8:136, :] = columns.T
        ext[b, 1, 0:8, :] = jnp.where(lane < 64, halo_ref[6, b], halo_ref[7, b]) * (top * side)
        ext[b, 1, 136:144, :] = jnp.where(lane < 64, halo_ref[4, b], halo_ref[5, b]) * (
            bottom * side
        )

    def ring(x0, x1, by):
        n = x0.shape[0]
        at = lax.broadcasted_iota(jnp.int32, (n, 128), 1)
        r0, r1 = pltpu.roll(x0, (-by) % 128, 1), pltpu.roll(x1, (-by) % 128, 1)
        wrapped = at >= 128 - by if by > 0 else at < -by
        return jnp.where(wrapped, r1, r0), jnp.where(wrapped, r0, r1)

    def band(b, carry):
        x0, x1 = ext[b, 0], ext[b, 1]
        for j in range(9):
            if j == 4:
                shifted[j, 0], shifted[j, 1] = x0, x1
            else:
                shifted[j, 0], shifted[j, 1] = ring(x0, x1, j - 4)

        def block(start, size):
            acc = [jnp.zeros((size, 128), F32), jnp.zeros((size, 128), F32)]
            for i in range(9):
                for j in range(9):
                    tap = taps_ref[b * 81 + i * 9 + j]
                    for t in range(2):
                        acc[t] = acc[t] + tap * shifted[j, t, pl.ds(start + i, size), :]
            at = lax.broadcasted_iota(jnp.int32, (size, 128), 0) + start
            keep = jnp.where(at < 4, top, jnp.where(at >= 132, bottom, 1.0))
            at_lane = lax.broadcasted_iota(jnp.int32, (size, 128), 1)
            beside = keep * jnp.where(at_lane < 64, right, left)
            v0 = acc[0].astype(BF16).astype(F32) * keep
            v1 = acc[1].astype(BF16).astype(F32) * beside
            psf[pl.ds(start, size), :] = v0
            for jj in range(3):
                s0, s1 = (v0, v1) if jj == 1 else ring(v0, v1, jj - 1)
                where = pl.ds(start * 24 + 8 * jj + b, size, stride=24)
                taps3[0, where, :] = s0
                taps3[1, where, :] = s1

        def blocks(n, inner):
            block(pl.multiple_of(n * 32, 32), 32)
            return inner

        lax.fori_loop(0, 4, blocks, 0)
        block(128, 8)
        psf_ref[b] = psf[4:132, :].astype(BF16)
        return carry

    lax.fori_loop(0, NB, band, 0)

    bias1 = jnp.broadcast_to(b1_ref[...], (64, 256))
    lanes = lax.broadcasted_iota(jnp.int32, (64, 256), 1)
    inside = jnp.where(lanes < 128, 1.0, jnp.where(lanes < 192, right, left))
    w1 = w1_ref[...]

    def first(n, carry):
        at = pl.ds(pl.multiple_of((n + 2) * 24, 8), 72)
        rhs = jnp.concatenate([taps3[0, at, :], taps3[1, at, :]], axis=1).astype(BF16)
        v = jnp.dot(w1, rhs, preferred_element_type=F32) + bias1
        keep = jnp.where(n == 0, top, jnp.where(n == 129, bottom, 1.0))
        v = v / (1.0 + jnp.exp(-v))
        hidden[n] = (v * (inside * keep)).astype(BF16)
        return carry

    lax.fori_loop(0, 130, first, 0)

    bias2 = jnp.broadcast_to(b2_ref[...], (64, 128))
    w2 = w2_ref[...]
    at_lane = lax.broadcasted_iota(jnp.int32, (64, 128), 1)

    def group(g, carry):
        def row(yy, inner):
            y = g * 16 + yy
            rhs = hidden[pl.ds(y, 3)].reshape(192, 256)
            z = jnp.dot(w2, rhs, preferred_element_type=F32)
            before = pltpu.roll(
                jnp.where(at_lane == 127, z[0:64, 128:256], z[0:64, 0:128]), 1, 1
            )
            after = pltpu.roll(
                jnp.where(at_lane == 0, z[128:192, 128:256], z[128:192, 0:128]), 127, 1
            )
            turned[pl.ds(yy, 64, stride=16), :] = (before + z[64:128, 0:128]) + (after + bias2)
            return inner

        lax.fori_loop(0, 16, row, 0, unroll=4)
        det_ref[:, pl.ds(pl.multiple_of(g * 16, 16), 16), :] = (
            turned[...].reshape(64, 16, 128).astype(BF16)
        )
        return carry

    lax.fori_loop(0, 8, group, 0)


def detect(taps, image, halo, w1, b1, w2, b2):
    vmem = pl.BlockSpec(memory_space=pltpu.VMEM)
    return pl.pallas_call(
        detect_kernel,
        out_shape=(
            jax.ShapeDtypeStruct((NB, 128, 128), BF16),
            jax.ShapeDtypeStruct((64, 128, 128), BF16),
        ),
        in_specs=[pl.BlockSpec(memory_space=pltpu.SMEM)] + [vmem] * 6,
        out_specs=(vmem, vmem),
        scratch_shapes=[
            pltpu.VMEM((NB, 2, 144, 128), F32),
            pltpu.VMEM((9, 2, 144, 128), F32),
            pltpu.VMEM((136, 128), F32),
            pltpu.VMEM((2, 136 * 24, 128), F32),
            pltpu.VMEM((130, 64, 256), BF16),
            pltpu.VMEM((64 * 16, 128), F32),
        ],
        compiler_params=pltpu.CompilerParams(vmem_limit_bytes=48 * 1024 * 1024),
        name="detect",
    )(taps, image, halo, w1, b1, w2, b2)


def body(
    tiles,
    tile_weight,
    owners,
    cells,
    psf_kernel,
    conv1_weight,
    conv1_bias,
    conv2_weight,
    conv2_bias,
):
    image, halo = exchange(
        tiles.transpose(1, 0, 2),
        tile_weight.transpose(1, 0),
        owners.reshape(1, 128),
        cells.reshape(1, 128),
    )
    w1 = jnp.pad(conv1_weight.transpose(0, 2, 3, 1), ((0, 0), (0, 0), (0, 0), (0, 2)))
    w2 = conv2_weight.transpose(3, 0, 2, 1).reshape(192, 192)
    return detect(
        psf_kernel.reshape(-1),
        image,
        halo,
        w1.reshape(64, 72),
        conv1_bias[:, None],
        w2,
        conv2_bias[:, None],
    )


def solution(mesh):
    in_specs = (
        P(("skyx", "skyy"), None, None),
        P(("skyx", "skyy"), None),
        P(("skyx", "skyy"), None),
        P(("skyx", "skyy")),
        P(),
        P(),
        P(),
        P(),
        P(),
    )
    out_specs = (P(None, "skyy", "skyx"), P(None, "skyy", "skyx"))
    return jax.shard_map(body, mesh=mesh, in_specs=in_specs, out_specs=out_specs, check_vma=False)
```

```python
import functools

import jax
import jax.numpy as jnp
from jax import lax
from jax.experimental import pallas as pl
from jax.experimental.pallas import tpu as pltpu
from jax.sharding import PartitionSpec as P

MESH = pl.DeviceIdType.MESH
F32 = jnp.float32
BF16 = jnp.bfloat16

NB = 6
HALF = 2048
WIDE = HALF + 128
ORDER = (0, 2, 4, 1, 3, 5)
MEMBERS = ((2, 0), (2, 1), (1, 0), (3, 0), (1, 1), (3, 1), (0, 1))
AROUND = ((-1, 0), (1, 0), (0, -1), (0, 1), (-1, -1), (-1, 1), (1, -1), (1, 1))


def exchange_kernel(
    tiles_hbm,
    wt_ref,
    own_ref,
    cell_ref,
    out_ref,
    tin,
    sel,
    meta,
    metar,
    send_a,
    send_b,
    recv_a,
    recv_b,
    st2,
    rcv2,
    st3,
    rcv3,
    tbuf,
    hsend,
    hrecv,
    tin_sem,
    self_sem,
    s1_send,
    s1_recv,
    s2_send,
    s2_recv,
    s3_send,
    s3_recv,
    h_send,
    h_recv,
):
    ix = lax.axis_index("skyx")
    iy = lax.axis_index("skyy")
    core = ix % 2
    q = (ix // 2, iy % 4, iy // 4)

    def device(axis, step, flip):
        r = list(q)
        if step:
            r[axis] = (r[axis] + step) % 4
        c = (core + flip) % 2 if flip else core
        return (r[0] * 2 + c, r[2] * 4 + r[1])

    def around(dy, dx):
        return ((ix + dx + 8) % 8, (iy + dy + 16) % 16)

    barrier = pltpu.get_barrier_semaphore()
    peers = [device(0, 0, 1)]
    for axis in range(3):
        for step, flip in MEMBERS[:6]:
            peers.append(device(axis, step, flip))
    for dy, dx in AROUND:
        peers.append(around(dy, dx))
    for peer in peers:
        pl.semaphore_signal(barrier, inc=1, device_id=peer, device_id_type=MESH)

    tin_copies = {}
    for b in ORDER:
        tin_copies[b] = pltpu.make_async_copy(tiles_hbm.at[b], tin.at[b], tin_sem.at[b])
        tin_copies[b].start()

    own = own_ref[...]
    ox, oy = own // 16, own % 16
    oq = (ox // 2, oy % 4, oy // 4)
    oc = ox % 2
    ownf = jnp.broadcast_to(own.astype(F32), (128, 128))
    same = ownf == ownf.T
    earlier = lax.broadcasted_iota(jnp.int32, (128, 128), 0) < lax.broadcasted_iota(
        jnp.int32, (128, 128), 1
    )
    rank = jnp.sum(jnp.where(same & earlier, 1.0, 0.0), axis=0, keepdims=True).astype(jnp.int32)
    rows = lax.broadcasted_iota(jnp.int32, (256, 128), 0)
    for p in range(3):
        slot = (oq[p] * 2 + oc) * 32 + (oq[(p + 1) % 3] * 4 + oq[(p + 2) % 3]) * 2 + rank
        sel[p] = jnp.where(rows == slot, 1.0, 0.0).astype(BF16)
    meta[...] = jnp.zeros((128, 128), F32)
    meta[0:6, :] = wt_ref[...].astype(F32)
    meta[6:7, :] = cell_ref[...].astype(F32) + 1.0

    s1 = {}

    def stage1_refs(b):
        p, k = b // 2, b % 2
        return (send_a.at[p], recv_a.at[p]) if k == 0 else (send_b.at[p], recv_b.at[p])

    for n, b in enumerate(ORDER):
        p, k = b // 2, b % 2
        src, dst = stage1_refs(b)
        tin_copies[b].wait()

        def gather(c, carry, b=b, p=p, src=src):
            at = pl.ds(pl.multiple_of(c * 512, 512), 512)
            src[:, at] = jnp.dot(sel[p], tin[b, :, at], preferred_element_type=F32).astype(BF16)
            return carry

        lax.fori_loop(0, 8, gather, 0)
        if k == 0:
            src[:, 4096:4224] = lax.dot_general(
                sel[p],
                meta[...].astype(BF16),
                (((1,), (1,)), ((), ())),
                preferred_element_type=F32,
            ).astype(BF16)
        if n == 0:
            pl.semaphore_wait(barrier, len(peers))
        mine = q[p] * 2 + core
        mine_rows = pl.ds(pl.multiple_of(mine * 32, 32), 32)
        own_copy = pltpu.make_async_copy(src.at[mine_rows], dst.at[mine_rows], self_sem.at[b])
        own_copy.start()
        copies = [own_copy]
        for m, (step, flip) in enumerate(MEMBERS):
            there = ((q[p] + step) % 4) * 2 + (core + flip) % 2
            copy = pltpu.make_async_remote_copy(
                src_ref=src.at[pl.ds(pl.multiple_of(there * 32, 32), 32)],
                dst_ref=dst.at[mine_rows],
                send_sem=s1_send.at[b, m],
                recv_sem=s1_recv.at[b, m],
                device_id=device(p, step, flip),
                device_id_type=MESH,
            )
            copy.start()
            copies.append(copy)
        s1[b] = copies

    s2, s3 = {}, {}

    def reduce_tiles(b):
        p, k = b // 2, b % 2
        src, dst = stage1_refs(b)
        s1[b][0].wait()
        for copy in s1[b][1:]:
            copy.wait_recv()
        if k == 0:
            metar[p] = dst[:, 4096:4224].astype(F32).T[0:8, :]
        w = metar[p, b : b + 1, :]
        code = metar[p, 6:7, :].astype(jnp.int32)
        row = lax.broadcasted_iota(jnp.int32, (128, 256), 0)
        col = lax.broadcasted_iota(jnp.int32, (128, 256), 1)
        hit = ((col % 32) // 2 == row // 8) & (code == row % 4 + 1)
        upper = (row // 4) % 2 == 0
        both = jnp.where(hit, jnp.broadcast_to(w, (128, 256)), 0.0)
        c0 = jnp.where(upper, both, 0.0).astype(BF16)
        c1 = jnp.where(upper, 0.0, both).astype(BF16)
        st2[b, :, HALF:WIDE] = jnp.broadcast_to(
            jnp.sum(both, axis=1, keepdims=True), (128, 128)
        )

        def reduce(c, carry):
            lo = pl.ds(pl.multiple_of(c * 512, 512), 512)
            hi = pl.ds(pl.multiple_of(c * 512 + HALF, 512), 512)
            st2[b, :, lo] = jnp.dot(c0, dst[:, lo], preferred_element_type=F32) + jnp.dot(
                c1, dst[:, hi], preferred_element_type=F32
            )
            return carry

        lax.fori_loop(0, 4, reduce, 0)
        axis = (p + 1) % 3
        copies = []
        for step in (2, 1, 3):
            there = (q[axis] + step) % 4
            copy = pltpu.make_async_remote_copy(
                src_ref=st2.at[b, pl.ds(pl.multiple_of(there * 32, 32), 32)],
                dst_ref=rcv2.at[b, step - 1],
                send_sem=s2_send.at[b, step - 1],
                recv_sem=s2_recv.at[b, step - 1],
                device_id=device(axis, step, 0),
                device_id_type=MESH,
            )
            copy.start()
            copies.append(copy)
        s2[b] = copies

    def second(b):
        p = b // 2
        axis = (p + 1) % 3
        for copy in s2[b]:
            copy.wait_recv()
        at = pl.ds(pl.multiple_of(q[axis] * 32, 32), 32)
        st3[b] = (st2[b, at, :] + rcv2[b, 0]) + (rcv2[b, 1] + rcv2[b, 2])
        axis = (p + 2) % 3
        copies = []
        for step in (2, 1, 3):
            there = (q[axis] + step) % 4
            copy = pltpu.make_async_remote_copy(
                src_ref=st3.at[b, pl.ds(pl.multiple_of(there * 8, 8), 8)],
                dst_ref=rcv3.at[b, step - 1],
                send_sem=s3_send.at[b, step - 1],
                recv_sem=s3_recv.at[b, step - 1],
                device_id=device(axis, step, 0),
                device_id_type=MESH,
            )
            copy.start()
            copies.append(copy)
        s3[b] = copies

    left_half = lax.broadcasted_iota(jnp.int32, (16, 128), 1) < 64

    def third(b):
        p = b // 2
        axis = (p + 2) % 3
        for copy in s3[b]:
            copy.wait_recv()
        at = pl.ds(pl.multiple_of(q[axis] * 8, 8), 8)
        total = (st3[b, at, :] + rcv3[b, 0]) + (rcv3[b, 1] + rcv3[b, 2])
        scale = 1.0 / (1.0 + total[:, HALF:WIDE])
        for j in range(16):
            tbuf[pl.ds(j, 8, stride=16), :] = total[:, 128 * j : 128 * j + 128] * scale
        for h in range(2):
            for cy in range(2):
                s = h * 4 + cy * 2
                a = tbuf[16 * s : 16 * s + 16, :]
                c = tbuf[16 * s + 16 : 16 * s + 32, :]
                y0 = 64 * cy + 32 * h
                out_ref[pl.ds(128 * b + y0, 16, stride=2), :] = jnp.where(
                    left_half, a, pltpu.roll(c, 64, 1)
                )
                out_ref[pl.ds(128 * b + y0 + 1, 16, stride=2), :] = jnp.where(
                    left_half, pltpu.roll(a, 64, 1), c
                )
        r = 128 * b
        hsend[0, b] = out_ref[r : r + 8, :]
        hsend[1, b] = out_ref[r + 120 : r + 128, :]
        turned = out_ref[r : r + 128, :].T
        hsend[2, b] = turned[0:8, :]
        hsend[3, b] = turned[120:128, :]
        out_ref[1152 + 8 * b : 1160 + 8 * b, :] = turned[0:8, :]
        out_ref[1200 + 8 * b : 1208 + 8 * b, :] = turned[120:128, :]

    todo = []
    for n in range(6 + 4):
        if n < 6:
            todo.append((reduce_tiles, n))
        if 0 <= n - 2 < 6:
            todo.append((second, n - 2))
        if 0 <= n - 4 < 6:
            todo.append((third, n - 4))
    for step_fn, n in todo:
        step_fn(ORDER[n])

    halo = []
    for n, (dy, dx) in enumerate(AROUND):
        which = 0 if dy < 0 else 1 if dy > 0 else 2 if dx < 0 else 3
        copy = pltpu.make_async_remote_copy(
            src_ref=hsend.at[which],
            dst_ref=hrecv.at[n],
            send_sem=h_send.at[n],
            recv_sem=h_recv.at[n],
            device_id=around(dy, dx),
            device_id_type=MESH,
        )
        copy.start()
        halo.append(copy)
    for b in ORDER:
        for copy in s1[b][1:] + s2[b] + s3[b]:
            copy.wait_send()
    for n, copy in enumerate(halo):
        copy.wait_recv()
        out_ref[768 + 48 * n : 816 + 48 * n, :] = hrecv[n].reshape(48, 128)
    for copy in halo:
        copy.wait_send()


def exchange(tiles, weights, owners, cells):
    vmem = pl.BlockSpec(memory_space=pltpu.VMEM)
    dma = pltpu.SemaphoreType.DMA
    return pl.pallas_call(
        exchange_kernel,
        out_shape=jax.ShapeDtypeStruct((1248, 128), F32),
        in_specs=[pl.BlockSpec(memory_space=pl.ANY), vmem, vmem, vmem],
        out_specs=vmem,
        scratch_shapes=[
            pltpu.VMEM((NB, 128, 4096), BF16),
            pltpu.VMEM((3, 256, 128), BF16),
            pltpu.VMEM((128, 128), F32),
            pltpu.VMEM((3, 8, 256), F32),
            pltpu.VMEM((3, 256, 4224), BF16),
            pltpu.VMEM((3, 256, 4096), BF16),
            pltpu.VMEM((3, 256, 4224), BF16),
            pltpu.VMEM((3, 256, 4096), BF16),
            pltpu.VMEM((NB, 128, WIDE), F32),
            pltpu.VMEM((NB, 3, 32, WIDE), F32),
            pltpu.VMEM((NB, 32, WIDE), F32),
            pltpu.VMEM((NB, 3, 8, WIDE), F32),
            pltpu.VMEM((128, 128), F32),
            pltpu.VMEM((4, NB, 8, 128), F32),
            pltpu.VMEM((8, NB, 8, 128), F32),
            dma((NB,)),
            dma((NB,)),
            dma((NB, 7)),
            dma((NB, 7)),
            dma((NB, 3)),
            dma((NB, 3)),
            dma((NB, 3)),
            dma((NB, 3)),
            dma((8,)),
            dma((8,)),
        ],
        compiler_params=pltpu.CompilerParams(
            collective_id=0, has_side_effects=True, vmem_limit_bytes=60 * 1024 * 1024
        ),
        name="tile_exchange",
    )(tiles, weights, owners, cells)


def detect_kernel(
    taps_ref,
    coadd_ref,
    w1_ref,
    b1_ref,
    w2_ref,
    b2_ref,
    psf_ref,
    det_ref,
    ext,
    shifted,
    sides,
    sides_t,
    psf,
    taps3,
    edge3,
    hidden,
    turned,
    small,
    w2s,
):
    ix = lax.axis_index("skyx")
    iy = lax.axis_index("skyy")
    top, bottom = (iy > 0).astype(F32), (iy < 15).astype(F32)
    left, right = (ix > 0).astype(F32), (ix < 7).astype(F32)

    def halo(slot, b):
        r = 768 + slot * 48 + b * 8
        return coadd_ref[r : r + 8, :]

    def lanes_of(n):
        return lax.broadcasted_iota(jnp.int32, (n, 128), 1)

    small[...] = jnp.zeros((128, 128), F32)
    for b in range(NB):
        for i in range(3):
            small[pl.ds(i * 24 + b, 3, stride=8), 0:64] = w1_ref[b, i].astype(F32)
    w1 = (small[...].T[0:64, 0:72] * 0.5).astype(BF16)
    for j in range(3):
        for i in range(3):
            w2s[64 * j : 64 * j + 64, 64 * i : 64 * i + 64] = w2_ref[i, j]
    small[0:1, 0:64] = b1_ref[...] * 0.5
    small[1:2, 0:64] = b2_ref[...]
    columns = small[...].T
    bias1 = jnp.broadcast_to(columns[0:64, 0:1], (64, 256))
    bias2 = jnp.broadcast_to(columns[0:64, 1:2], (64, 128))

    pieces = []
    for b in range(NB):
        pieces += [
            halo(3, b)[2:8] * left,
            halo(8, b)[0:4],
            halo(9, b)[4:8],
            halo(2, b)[0:6] * right,
        ]
    pieces.append(jnp.zeros((8, 128), F32))
    sides[8:136, :] = jnp.concatenate(pieces, axis=0).T
    lane8 = lanes_of(8)
    for r, mid, at_left, at_right, keep in ((0, 1, 7, 6, top), (136, 0, 5, 4, bottom)):
        line = jnp.zeros((8, 128), F32)
        for b in range(NB):
            middle = halo(mid, b)
            parts = (
                (halo(at_left, b) * left, 122, 0, 6),
                (middle, 0, 6, 4),
                (middle, 124, 10, 4),
                (halo(at_right, b) * right, 0, 14, 6),
            )
            for value, start, at, size in parts:
                at = 20 * b + at
                moved = pltpu.roll(value, (at - start) % 128, 1)
                line = jnp.where((lane8 >= at) & (lane8 < at + size), moved, line)
        sides[r : r + 8, :] = line * keep

    for j in range(9):
        shifted[j] = pltpu.roll(sides[...], (-j) % 128, 1) if j else sides[...]
    owner_band = lane8 // 20

    def edge_block(start, size):
        acc = jnp.zeros((size, 128), F32)
        for i in range(9):
            for j in range(9):
                tap = jnp.full((8, 128), taps_ref[i, 0, j], F32)
                for b in range(1, NB):
                    tap = jnp.where(owner_band == b, taps_ref[i, b, j], tap)
                tap = jnp.broadcast_to(tap[0:1], (size, 128))
                acc = acc + tap * shifted[j, start + i : start + i + size, :]
        at = lax.broadcasted_iota(jnp.int32, (size, 128), 0) + start
        keep = jnp.where(at < 4, top, jnp.where(at >= 132, bottom, 1.0))
        keep = keep * jnp.where(lanes_of(size) % 20 < 10, left, right)
        return acc.astype(BF16).astype(F32) * keep

    sides[0:136, :] = edge_block(0, 136)

    taps3[...] = jnp.zeros_like(taps3)
    for b in range(NB):
        ext[b, 8:136, :] = coadd_ref[128 * b : 128 * b + 128, :]
        ext[b, 0:8, :] = halo(1, b) * top
        ext[b, 136:144, :] = halo(0, b) * bottom
    column = lanes_of(144)

    def band(b, carry):
        near_left = pltpu.roll(shifted[0], 122 - 20 * b, 1)
        near_right = pltpu.roll(shifted[0], 114 - 20 * b, 1)
        x = ext[b]
        for j in range(9):
            if j < 4:
                moved = pltpu.roll(jnp.where(column >= 124 + j, near_left, x), 4 - j, 1)
            elif j == 4:
                moved = x
            else:
                moved = pltpu.roll(jnp.where(column < j - 4, near_right, x), 132 - j, 1)
            shifted[j + 1] = moved

        def block(start, size):
            acc = jnp.zeros((size, 128), F32)
            for i in range(9):
                for j in range(9):
                    acc = acc + taps_ref[i, b, j] * shifted[j + 1, start + i : start + i + size, :]
            at = lax.broadcasted_iota(jnp.int32, (size, 128), 0) + start
            keep = jnp.where(at < 4, top, jnp.where(at >= 132, bottom, 1.0))
            v = acc.astype(BF16).astype(F32) * keep
            psf[start : start + size, :] = v
            lane = lanes_of(size)
            edge = sides[start : start + size, :]
            before = jnp.where(lane == 0, pltpu.roll(edge, 127 - 20 * b, 1), pltpu.roll(v, 1, 1))
            after = jnp.where(
                lane == 127, pltpu.roll(edge, 117 - 20 * b, 1), pltpu.roll(v, 127, 1)
            )
            for j, value in enumerate((before, v, after)):
                taps3[pl.ds(start * 24 + 8 * j + b, size, stride=24), :] = value
            edge = jnp.where(lane == 20 * b + 2, pltpu.roll(v, 20 * b + 2, 1), edge)
            edge = jnp.where(lane == 20 * b + 9, pltpu.roll(v, 20 * b + 10, 1), edge)
            sides[start : start + size, :] = edge

        block(0, 72)
        block(72, 64)
        psf_ref[b] = psf[4:132, :].astype(BF16)
        return carry

    lax.fori_loop(0, NB, band, 0)

    def silu(u):
        return u + u * jnp.tanh(u)

    def first(n, carry):
        at0 = pl.ds(pl.multiple_of((2 * n + 2) * 24, 8), 72)
        at1 = pl.ds(pl.multiple_of((2 * n + 3) * 24, 8), 72)
        rhs = jnp.concatenate([taps3[at0, :], taps3[at1, :]], axis=1).astype(BF16)
        v = silu(jnp.dot(w1, rhs, preferred_element_type=F32) + bias1)
        hidden[2 * n] = v[:, 0:128].astype(BF16)
        hidden[2 * n + 1] = v[:, 128:256].astype(BF16)
        return carry

    lax.fori_loop(0, 65, first, 0, unroll=5)
    hidden[0] = (hidden[0].astype(F32) * top).astype(BF16)
    hidden[129] = (hidden[129].astype(F32) * bottom).astype(BF16)

    sides_t[0] = sides[0:128, :].T
    tail = jnp.concatenate([sides[128:136, :], jnp.zeros((120, 128), F32)], axis=0)
    sides_t[1] = tail.T
    edge3[...] = jnp.zeros_like(edge3)
    at256 = lax.broadcasted_iota(jnp.int32, (64, 256), 1)
    ends = jnp.where(at256 == 0, top, jnp.where(at256 == 129, bottom, 1.0))
    beside = []
    for side, (offset, keep) in enumerate(((0, left), (9, right))):
        for t in range(2):
            for j in range(3):
                edge3[side, 8 * j : 8 * j + 6, 128 * t : 128 * t + 128] = sides_t[
                    t, pl.ds(offset + j, 6, stride=20), :
                ]
        x = edge3[side]
        rhs = jnp.concatenate([pltpu.roll(x, 256 - (2 + i), 1) for i in range(3)], axis=0)
        v = silu(jnp.dot(w1, rhs.astype(BF16), preferred_element_type=F32) + bias1)
        v = (v * (ends * keep)).astype(BF16).astype(F32)
        rhs = jnp.concatenate(
            [v[:, 0:128]] + [pltpu.roll(v, 256 - i, 1)[:, 0:128] for i in (1, 2)], axis=0
        )
        weight = w2s[0:64, :] if side == 0 else w2s[128:192, :]
        beside.append(jnp.dot(weight, rhs.astype(BF16), preferred_element_type=F32))
    small[0:64, :] = beside[0]
    small[64:128, :] = beside[1]

    w2 = w2s[...]
    lane64 = lanes_of(64)

    def group(g, carry):
        def rows(n, inner):
            y = g * 16 + 2 * n
            rhs = jnp.concatenate(
                [hidden[pl.ds(y, 3)].reshape(192, 128), hidden[pl.ds(y + 1, 3)].reshape(192, 128)],
                axis=1,
            )
            z = jnp.dot(w2, rhs, preferred_element_type=F32)
            for k in range(2):
                c = slice(128 * k, 128 * k + 128)
                near = pltpu.roll(small[0:64, :], 128 - (y + k), 1)
                far = pltpu.roll(small[64:128, :], 127 - (y + k), 1)
                before = jnp.where(lane64 == 0, near, pltpu.roll(z[0:64, c], 1, 1))
                after = jnp.where(lane64 == 127, far, pltpu.roll(z[128:192, c], 127, 1))
                turned[pl.ds(2 * n + k, 64, stride=16), :] = (before + z[64:128, c]) + (
                    after + bias2
                )
            return inner

        lax.fori_loop(0, 8, rows, 0, unroll=4)
        det_ref[:, pl.ds(pl.multiple_of(g * 16, 16), 16), :] = (
            turned[...].reshape(64, 16, 128).astype(BF16)
        )
        return carry

    lax.fori_loop(0, 8, group, 0)


def detect(taps, coadd, w1, b1, w2, b2):
    vmem = pl.BlockSpec(memory_space=pltpu.VMEM)
    return pl.pallas_call(
        detect_kernel,
        out_shape=(
            jax.ShapeDtypeStruct((NB, 128, 128), BF16),
            jax.ShapeDtypeStruct((64, 128, 128), BF16),
        ),
        in_specs=[pl.BlockSpec(memory_space=pltpu.SMEM)] + [vmem] * 5,
        out_specs=(vmem, vmem),
        scratch_shapes=[
            pltpu.VMEM((NB, 144, 128), F32),
            pltpu.VMEM((10, 144, 128), F32),
            pltpu.VMEM((144, 128), F32),
            pltpu.VMEM((2, 128, 128), F32),
            pltpu.VMEM((136, 128), F32),
            pltpu.VMEM((136 * 24, 128), F32),
            pltpu.VMEM((2, 24, 256), F32),
            pltpu.VMEM((130, 64, 128), BF16),
            pltpu.VMEM((64 * 16, 128), F32),
            pltpu.VMEM((128, 128), F32),
            pltpu.VMEM((192, 192), BF16),
        ],
        compiler_params=pltpu.CompilerParams(vmem_limit_bytes=48 * 1024 * 1024),
        name="detect",
    )(taps, coadd, w1, b1, w2, b2)


def body(
    tiles,
    tile_weight,
    owners,
    cells,
    psf_kernel,
    conv1_weight,
    conv1_bias,
    conv2_weight,
    conv2_bias,
):
    coadd = exchange(
        tiles.transpose(1, 0, 2),
        tile_weight.transpose(1, 0),
        owners.reshape(1, 128),
        cells.reshape(1, 128),
    )
    return detect(
        psf_kernel.transpose(1, 0, 2),
        coadd,
        conv1_weight.transpose(1, 2, 3, 0),
        conv1_bias.reshape(1, 64),
        conv2_weight.transpose(2, 3, 0, 1),
        conv2_bias.reshape(1, 64),
    )


def solution(mesh):
    in_specs = (
        P(("skyx", "skyy"), None, None),
        P(("skyx", "skyy"), None),
        P(("skyx", "skyy"), None),
        P(("skyx", "skyy")),
        P(),
        P(),
        P(),
        P(),
        P(),
    )
    out_specs = (P(None, "skyy", "skyx"), P(None, "skyy", "skyx"))
    return jax.shard_map(body, mesh=mesh, in_specs=in_specs, out_specs=out_specs, check_vma=False)
```

```python
import functools

import jax
import jax.numpy as jnp
from jax import lax
from jax.experimental import pallas as pl
from jax.experimental.pallas import tpu as pltpu
from jax.sharding import PartitionSpec as P

MESH = pl.DeviceIdType.MESH
F32 = jnp.float32
BF16 = jnp.bfloat16

NB = 6
HALF = 2048
QUARTER = 1024
ORDER = (0, 2, 4, 1, 3, 5)
MEMBERS = ((2, 0), (2, 1), (1, 0), (3, 0), (1, 1), (3, 1), (0, 1))
AROUND = ((-1, 0), (1, 0), (0, -1), (0, 1), (-1, -1), (-1, 1), (1, -1), (1, 1))


def exchange_kernel(
    tiles_hbm,
    wt_ref,
    own_ref,
    cell_ref,
    out_ref,
    tin,
    sel,
    meta,
    metar,
    send_a,
    send_b,
    recv_a,
    recv_b,
    acc2,
    st2,
    st2m,
    rcv2,
    rcv2m,
    acc3,
    st3,
    st3m,
    rcv3,
    rcv3m,
    tbuf,
    hsend,
    hrecv,
    tin_sem,
    self_sem,
    s1_send,
    s1_recv,
    s2_send,
    s2_recv,
    s3_send,
    s3_recv,
    h_send,
    h_recv,
):
    ix = lax.axis_index("skyx")
    iy = lax.axis_index("skyy")
    core = ix % 2
    q = (ix // 2, iy % 4, iy // 4)

    def device(axis, step, flip):
        r = list(q)
        if step:
            r[axis] = (r[axis] + step) % 4
        c = (core + flip) % 2 if flip else core
        return (r[0] * 2 + c, r[2] * 4 + r[1])

    def around(dy, dx):
        return ((ix + dx + 8) % 8, (iy + dy + 16) % 16)

    barrier = pltpu.get_barrier_semaphore()
    peers = [device(0, 0, 1)]
    for axis in range(3):
        for step, flip in MEMBERS[:6]:
            peers.append(device(axis, step, flip))
    for dy, dx in AROUND:
        peers.append(around(dy, dx))
    for peer in peers:
        pl.semaphore_signal(barrier, inc=1, device_id=peer, device_id_type=MESH)

    tin_copies = {}
    for b in ORDER:
        tin_copies[b] = pltpu.make_async_copy(tiles_hbm.at[b], tin.at[b], tin_sem.at[b])
        tin_copies[b].start()

    own = own_ref[...]
    ox, oy = own // 16, own % 16
    oq = (ox // 2, oy % 4, oy // 4)
    oc = ox % 2
    ownf = jnp.broadcast_to(own.astype(F32), (128, 128))
    same = ownf == ownf.T
    earlier = lax.broadcasted_iota(jnp.int32, (128, 128), 0) < lax.broadcasted_iota(
        jnp.int32, (128, 128), 1
    )
    rank = jnp.sum(jnp.where(same & earlier, 1.0, 0.0), axis=0, keepdims=True).astype(jnp.int32)
    rows = lax.broadcasted_iota(jnp.int32, (256, 128), 0)
    for p in range(3):
        slot = (oq[p] * 2 + oc) * 32 + (oq[(p + 1) % 3] * 4 + oq[(p + 2) % 3]) * 2 + rank
        sel[p] = jnp.where(rows == slot, 1.0, 0.0).astype(BF16)
    meta[...] = jnp.zeros((128, 128), F32)
    meta[0:6, :] = wt_ref[...].astype(F32)
    meta[6:7, :] = cell_ref[...].astype(F32) + 1.0

    s1 = {}

    def stage1_refs(b):
        p, k = b // 2, b % 2
        return (send_a.at[p], recv_a.at[p]) if k == 0 else (send_b.at[p], recv_b.at[p])

    for n, b in enumerate(ORDER):
        p, k = b // 2, b % 2
        src, dst = stage1_refs(b)
        tin_copies[b].wait()

        def gather(c, carry, b=b, p=p, src=src):
            at = pl.ds(pl.multiple_of(c * 512, 512), 512)
            src[:, at] = jnp.dot(sel[p], tin[b, :, at], preferred_element_type=F32).astype(BF16)
            return carry

        lax.fori_loop(0, 8, gather, 0)
        if k == 0:
            src[:, 4096:4224] = lax.dot_general(
                sel[p],
                meta[...].astype(BF16),
                (((1,), (1,)), ((), ())),
                preferred_element_type=F32,
            ).astype(BF16)
        if n == 0:
            pl.semaphore_wait(barrier, len(peers))
        mine = q[p] * 2 + core
        mine_rows = pl.ds(pl.multiple_of(mine * 32, 32), 32)
        own_copy = pltpu.make_async_copy(src.at[mine_rows], dst.at[mine_rows], self_sem.at[b])
        own_copy.start()
        copies = [own_copy]
        for m, (step, flip) in enumerate(MEMBERS):
            there = ((q[p] + step) % 4) * 2 + (core + flip) % 2
            copy = pltpu.make_async_remote_copy(
                src_ref=src.at[pl.ds(pl.multiple_of(there * 32, 32), 32)],
                dst_ref=dst.at[mine_rows],
                send_sem=s1_send.at[b, m],
                recv_sem=s1_recv.at[b, m],
                device_id=device(p, step, flip),
                device_id_type=MESH,
            )
            copy.start()
            copies.append(copy)
        s1[b] = copies

    s2, s3 = {}, {}

    def encode(values, denom, size):
        top = jnp.max(jnp.abs(values), axis=1, keepdims=True)
        some = top > 1e-30
        inverse = jnp.where(some, 32767.0 / jnp.where(some, top, 1.0), 0.0)
        codes = (values * inverse + 32768.5).astype(jnp.int32)
        words = codes[:, :QUARTER] | (codes[:, QUARTER:] << 16)
        lane = lax.broadcasted_iota(jnp.int32, (size, 128), 1)
        return words, jnp.where(lane < 64, denom, top * (1.0 / 32767.0))

    def decode(words, extra):
        step = extra[:, 64:65]
        low = (words & 65535).astype(F32) - 32768.0
        high = lax.shift_right_logical(words, jnp.full_like(words, 16)).astype(F32) - 32768.0
        return low * step, high * step

    def gathered(own, own_denom, words, extras):
        low, high, denom = own[:, :QUARTER], own[:, QUARTER:], own_denom
        for k in range(3):
            a, c = decode(words[k], extras[k])
            low, high, denom = low + a, high + c, denom + extras[k][:, 0:1]
        return low, high, denom

    def pass_on(b, axis, size, words, extras, to_words, to_extras, send, recv):
        copies = []
        for step in (2, 1, 3):
            there = (q[axis] + step) % 4
            at = pl.ds(pl.multiple_of(there * size, size), size)
            for n, (src, dst) in enumerate(((words, to_words), (extras, to_extras))):
                copy = pltpu.make_async_remote_copy(
                    src_ref=src.at[b, at],
                    dst_ref=dst.at[b, step - 1],
                    send_sem=send.at[b, step - 1, n],
                    recv_sem=recv.at[b, step - 1, n],
                    device_id=device(axis, step, 0),
                    device_id_type=MESH,
                )
                copy.start()
                copies.append(copy)
        return copies

    def reduce_tiles(b):
        p, k = b // 2, b % 2
        src, dst = stage1_refs(b)
        s1[b][0].wait()
        for copy in s1[b][1:]:
            copy.wait_recv()
        if k == 0:
            metar[p] = dst[:, 4096:4224].astype(F32).T[0:8, :]
        w = metar[p, b : b + 1, :]
        code = metar[p, 6:7, :].astype(jnp.int32)
        row = lax.broadcasted_iota(jnp.int32, (128, 256), 0)
        col = lax.broadcasted_iota(jnp.int32, (128, 256), 1)
        hit = ((col % 32) // 2 == row // 8) & (code == row % 4 + 1)
        upper = (row // 4) % 2 == 0
        both = jnp.where(hit, jnp.broadcast_to(w, (128, 256)), 0.0)
        c0 = jnp.where(upper, both, 0.0).astype(BF16)
        c1 = jnp.where(upper, 0.0, both).astype(BF16)
        denom = jnp.sum(both, axis=1, keepdims=True)

        def reduce(c, carry):
            lo = pl.ds(pl.multiple_of(c * 512, 512), 512)
            hi = pl.ds(pl.multiple_of(c * 512 + HALF, 512), 512)
            acc2[b, :, lo] = jnp.dot(c0, dst[:, lo], preferred_element_type=F32) + jnp.dot(
                c1, dst[:, hi], preferred_element_type=F32
            )
            return carry

        lax.fori_loop(0, 4, reduce, 0)
        st2[b], st2m[b] = encode(acc2[b], denom, 128)
        s2[b] = pass_on(b, (p + 1) % 3, 32, st2, st2m, rcv2, rcv2m, s2_send, s2_recv)

    def second(b):
        p = b // 2
        for copy in s2[b]:
            copy.wait_recv()
        at = pl.ds(pl.multiple_of(q[(p + 1) % 3] * 32, 32), 32)
        low, high, denom = gathered(acc2[b, at, :], st2m[b, at, 0:1], rcv2[b], rcv2m[b])
        acc3[b, :, :QUARTER] = low
        acc3[b, :, QUARTER:] = high
        st3[b], st3m[b] = encode(acc3[b], denom, 32)
        s3[b] = pass_on(b, (p + 2) % 3, 8, st3, st3m, rcv3, rcv3m, s3_send, s3_recv)

    left_half = lax.broadcasted_iota(jnp.int32, (16, 128), 1) < 64

    def third(b):
        p = b // 2
        axis = (p + 2) % 3
        for copy in s3[b]:
            copy.wait_recv()
        at = pl.ds(pl.multiple_of(q[axis] * 8, 8), 8)
        low, high, denom = gathered(acc3[b, at, :], st3m[b, at, 0:1], rcv3[b], rcv3m[b])
        scale = 1.0 / (1.0 + denom)
        for j in range(8):
            c = slice(128 * j, 128 * j + 128)
            tbuf[pl.ds(j, 8, stride=16), :] = low[:, c] * scale
            tbuf[pl.ds(j + 8, 8, stride=16), :] = high[:, c] * scale
        for h in range(2):
            for cy in range(2):
                s = h * 4 + cy * 2
                a = tbuf[16 * s : 16 * s + 16, :]
                c = tbuf[16 * s + 16 : 16 * s + 32, :]
                y0 = 64 * cy + 32 * h
                out_ref[pl.ds(128 * b + y0, 16, stride=2), :] = jnp.where(
                    left_half, a, pltpu.roll(c, 64, 1)
                )
                out_ref[pl.ds(128 * b + y0 + 1, 16, stride=2), :] = jnp.where(
                    left_half, pltpu.roll(a, 64, 1), c
                )
        r = 128 * b
        n = ORDER.index(b)
        hsend[0, n] = out_ref[r : r + 8, :]
        hsend[1, n] = out_ref[r + 120 : r + 128, :]
        turned = out_ref[r : r + 128, :].T
        hsend[2, n] = turned[0:8, :]
        hsend[3, n] = turned[120:128, :]
        out_ref[1152 + 8 * b : 1160 + 8 * b, :] = turned[0:8, :]
        out_ref[1200 + 8 * b : 1208 + 8 * b, :] = turned[120:128, :]

    halo = []

    def send_halo(group):
        bands = pl.ds(3 * group, 3)
        for n, (dy, dx) in enumerate(AROUND):
            which = 0 if dy < 0 else 1 if dy > 0 else 2 if dx < 0 else 3
            copy = pltpu.make_async_remote_copy(
                src_ref=hsend.at[which, bands],
                dst_ref=hrecv.at[n, bands],
                send_sem=h_send.at[group, n],
                recv_sem=h_recv.at[group, n],
                device_id=around(dy, dx),
                device_id_type=MESH,
            )
            copy.start()
            halo.append(copy)

    for n in range(6 + 4):
        if n < 6:
            reduce_tiles(ORDER[n])
        if 0 <= n - 2 < 6:
            second(ORDER[n - 2])
        if 0 <= n - 4 < 6:
            third(ORDER[n - 4])
            if n - 4 in (2, 5):
                send_halo((n - 4) // 3)

    for b in ORDER:
        for copy in s1[b][1:] + s2[b] + s3[b]:
            copy.wait_send()
    for n, copy in enumerate(halo):
        copy.wait_recv()
        group, slot = n // 8, n % 8
        for k in range(3):
            r = 768 + 48 * slot + 8 * ORDER[3 * group + k]
            out_ref[r : r + 8, :] = hrecv[slot, 3 * group + k]
    for copy in halo:
        copy.wait_send()


def exchange(tiles, weights, owners, cells):
    vmem = pl.BlockSpec(memory_space=pltpu.VMEM)
    dma = pltpu.SemaphoreType.DMA
    return pl.pallas_call(
        exchange_kernel,
        out_shape=jax.ShapeDtypeStruct((1248, 128), F32),
        in_specs=[pl.BlockSpec(memory_space=pl.ANY), vmem, vmem, vmem],
        out_specs=vmem,
        scratch_shapes=[
            pltpu.VMEM((NB, 128, 4096), BF16),
            pltpu.VMEM((3, 256, 128), BF16),
            pltpu.VMEM((128, 128), F32),
            pltpu.VMEM((3, 8, 256), F32),
            pltpu.VMEM((3, 256, 4224), BF16),
            pltpu.VMEM((3, 256, 4096), BF16),
            pltpu.VMEM((3, 256, 4224), BF16),
            pltpu.VMEM((3, 256, 4096), BF16),
            pltpu.VMEM((NB, 128, HALF), F32),
            pltpu.VMEM((NB, 128, QUARTER), jnp.int32),
            pltpu.VMEM((NB, 128, 128), F32),
            pltpu.VMEM((NB, 3, 32, QUARTER), jnp.int32),
            pltpu.VMEM((NB, 3, 32, 128), F32),
            pltpu.VMEM((NB, 32, HALF), F32),
            pltpu.VMEM((NB, 32, QUARTER), jnp.int32),
            pltpu.VMEM((NB, 32, 128), F32),
            pltpu.VMEM((NB, 3, 8, QUARTER), jnp.int32),
            pltpu.VMEM((NB, 3, 8, 128), F32),
            pltpu.VMEM((128, 128), F32),
            pltpu.VMEM((4, NB, 8, 128), F32),
            pltpu.VMEM((8, NB, 8, 128), F32),
            dma((NB,)),
            dma((NB,)),
            dma((NB, 7)),
            dma((NB, 7)),
            dma((NB, 3, 2)),
            dma((NB, 3, 2)),
            dma((NB, 3, 2)),
            dma((NB, 3, 2)),
            dma((2, 8)),
            dma((2, 8)),
        ],
        compiler_params=pltpu.CompilerParams(
            collective_id=0, has_side_effects=True, vmem_limit_bytes=60 * 1024 * 1024
        ),
        name="tile_exchange",
    )(tiles, weights, owners, cells)


def detect_kernel(
    taps_ref,
    coadd_ref,
    w1_ref,
    b1_ref,
    w2_ref,
    b2_ref,
    psf_ref,
    det_ref,
    ext,
    shifted,
    sides,
    sides_t,
    psf,
    taps3,
    edge3,
    hidden,
    turned,
    small,
    w2s,
):
    ix = lax.axis_index("skyx")
    iy = lax.axis_index("skyy")
    top, bottom = (iy > 0).astype(F32), (iy < 15).astype(F32)
    left, right = (ix > 0).astype(F32), (ix < 7).astype(F32)

    def halo(slot, b):
        r = 768 + slot * 48 + b * 8
        return coadd_ref[r : r + 8, :]

    def lanes_of(n):
        return lax.broadcasted_iota(jnp.int32, (n, 128), 1)

    small[...] = jnp.zeros((128, 128), F32)
    for b in range(NB):
        for i in range(3):
            small[pl.ds(i * 24 + b, 3, stride=8), 0:64] = w1_ref[b, i].astype(F32)
    w1 = (small[...].T[0:64, 0:72] * 0.5).astype(BF16)
    for j in range(3):
        for i in range(3):
            w2s[64 * j : 64 * j + 64, 64 * i : 64 * i + 64] = w2_ref[i, j]
    small[0:1, 0:64] = b1_ref[...] * 0.5
    small[1:2, 0:64] = b2_ref[...]
    columns = small[...].T
    bias1 = jnp.broadcast_to(columns[0:64, 0:1], (64, 256))
    bias2 = jnp.broadcast_to(columns[0:64, 1:2], (64, 128))

    pieces = []
    for b in range(NB):
        pieces += [
            halo(3, b)[2:8] * left,
            halo(8, b)[0:4],
            halo(9, b)[4:8],
            halo(2, b)[0:6] * right,
        ]
    pieces.append(jnp.zeros((8, 128), F32))
    sides[8:136, :] = jnp.concatenate(pieces, axis=0).T
    lane8 = lanes_of(8)
    for r, mid, at_left, at_right, keep in ((0, 1, 7, 6, top), (136, 0, 5, 4, bottom)):
        line = jnp.zeros((8, 128), F32)
        for b in range(NB):
            middle = halo(mid, b)
            parts = (
                (halo(at_left, b) * left, 122, 0, 6),
                (middle, 0, 6, 4),
                (middle, 124, 10, 4),
                (halo(at_right, b) * right, 0, 14, 6),
            )
            for value, start, at, size in parts:
                at = 20 * b + at
                moved = pltpu.roll(value, (at - start) % 128, 1)
                line = jnp.where((lane8 >= at) & (lane8 < at + size), moved, line)
        sides[r : r + 8, :] = line * keep

    for j in range(9):
        shifted[j] = pltpu.roll(sides[...], (-j) % 128, 1) if j else sides[...]
    owner_band = lane8 // 20

    def edge_block(start, size):
        acc = jnp.zeros((size, 128), F32)
        for i in range(9):
            for j in range(9):
                tap = jnp.full((8, 128), taps_ref[i, 0, j], F32)
                for b in range(1, NB):
                    tap = jnp.where(owner_band == b, taps_ref[i, b, j], tap)
                tap = jnp.broadcast_to(tap[0:1], (size, 128))
                acc = acc + tap * shifted[j, start + i : start + i + size, :]
        at = lax.broadcasted_iota(jnp.int32, (size, 128), 0) + start
        keep = jnp.where(at < 4, top, jnp.where(at >= 132, bottom, 1.0))
        keep = keep * jnp.where(lanes_of(size) % 20 < 10, left, right)
        return acc.astype(BF16).astype(F32) * keep

    sides[0:136, :] = edge_block(0, 136)

    taps3[...] = jnp.zeros_like(taps3)
    for b in range(NB):
        ext[b, 8:136, :] = coadd_ref[128 * b : 128 * b + 128, :]
        ext[b, 0:8, :] = halo(1, b) * top
        ext[b, 136:144, :] = halo(0, b) * bottom
    column = lanes_of(144)

    def band(b, carry):
        near_left = pltpu.roll(shifted[0], 122 - 20 * b, 1)
        near_right = pltpu.roll(shifted[0], 114 - 20 * b, 1)
        x = ext[b]
        for j in range(9):
            if j < 4:
                moved = pltpu.roll(jnp.where(column >= 124 + j, near_left, x), 4 - j, 1)
            elif j == 4:
                moved = x
            else:
                moved = pltpu.roll(jnp.where(column < j - 4, near_right, x), 132 - j, 1)
            shifted[j + 1] = moved

        def block(start, size):
            acc = jnp.zeros((size, 128), F32)
            for i in range(9):
                for j in range(9):
                    acc = acc + taps_ref[i, b, j] * shifted[j + 1, start + i : start + i + size, :]
            at = lax.broadcasted_iota(jnp.int32, (size, 128), 0) + start
            keep = jnp.where(at < 4, top, jnp.where(at >= 132, bottom, 1.0))
            v = acc.astype(BF16).astype(F32) * keep
            psf[start : start + size, :] = v
            lane = lanes_of(size)
            edge = sides[start : start + size, :]
            before = jnp.where(lane == 0, pltpu.roll(edge, 127 - 20 * b, 1), pltpu.roll(v, 1, 1))
            after = jnp.where(
                lane == 127, pltpu.roll(edge, 117 - 20 * b, 1), pltpu.roll(v, 127, 1)
            )
            for j, value in enumerate((before, v, after)):
                taps3[pl.ds(start * 24 + 8 * j + b, size, stride=24), :] = value
            edge = jnp.where(lane == 20 * b + 2, pltpu.roll(v, 20 * b + 2, 1), edge)
            edge = jnp.where(lane == 20 * b + 9, pltpu.roll(v, 20 * b + 10, 1), edge)
            sides[start : start + size, :] = edge

        block(0, 72)
        block(72, 64)
        psf_ref[b] = psf[4:132, :].astype(BF16)
        return carry

    lax.fori_loop(0, NB, band, 0)

    def silu(u):
        return u + u * jnp.tanh(u)

    def first(n, carry):
        at0 = pl.ds(pl.multiple_of((2 * n + 2) * 24, 8), 72)
        at1 = pl.ds(pl.multiple_of((2 * n + 3) * 24, 8), 72)
        rhs = jnp.concatenate([taps3[at0, :], taps3[at1, :]], axis=1).astype(BF16)
        v = silu(jnp.dot(w1, rhs, preferred_element_type=F32) + bias1)
        hidden[2 * n] = v[:, 0:128].astype(BF16)
        hidden[2 * n + 1] = v[:, 128:256].astype(BF16)
        return carry

    lax.fori_loop(0, 65, first, 0, unroll=5)
    hidden[0] = (hidden[0].astype(F32) * top).astype(BF16)
    hidden[129] = (hidden[129].astype(F32) * bottom).astype(BF16)

    sides_t[0] = sides[0:128, :].T
    tail = jnp.concatenate([sides[128:136, :], jnp.zeros((120, 128), F32)], axis=0)
    sides_t[1] = tail.T
    edge3[...] = jnp.zeros_like(edge3)
    at256 = lax.broadcasted_iota(jnp.int32, (64, 256), 1)
    ends = jnp.where(at256 == 0, top, jnp.where(at256 == 129, bottom, 1.0))
    beside = []
    for side, (offset, keep) in enumerate(((0, left), (9, right))):
        for t in range(2):
            for j in range(3):
                edge3[side, 8 * j : 8 * j + 6, 128 * t : 128 * t + 128] = sides_t[
                    t, pl.ds(offset + j, 6, stride=20), :
                ]
        x = edge3[side]
        rhs = jnp.concatenate([pltpu.roll(x, 256 - (2 + i), 1) for i in range(3)], axis=0)
        v = silu(jnp.dot(w1, rhs.astype(BF16), preferred_element_type=F32) + bias1)
        v = (v * (ends * keep)).astype(BF16).astype(F32)
        rhs = jnp.concatenate(
            [v[:, 0:128]] + [pltpu.roll(v, 256 - i, 1)[:, 0:128] for i in (1, 2)], axis=0
        )
        weight = w2s[0:64, :] if side == 0 else w2s[128:192, :]
        beside.append(jnp.dot(weight, rhs.astype(BF16), preferred_element_type=F32))
    small[0:64, :] = beside[0]
    small[64:128, :] = beside[1]

    w2 = w2s[...]
    lane64 = lanes_of(64)

    def group(g, carry):
        def rows(n, inner):
            y = g * 16 + 2 * n
            rhs = jnp.concatenate(
                [hidden[pl.ds(y, 3)].reshape(192, 128), hidden[pl.ds(y + 1, 3)].reshape(192, 128)],
                axis=1,
            )
            z = jnp.dot(w2, rhs, preferred_element_type=F32)
            for k in range(2):
                c = slice(128 * k, 128 * k + 128)
                near = pltpu.roll(small[0:64, :], 128 - (y + k), 1)
                far = pltpu.roll(small[64:128, :], 127 - (y + k), 1)
                before = jnp.where(lane64 == 0, near, pltpu.roll(z[0:64, c], 1, 1))
                after = jnp.where(lane64 == 127, far, pltpu.roll(z[128:192, c], 127, 1))
                turned[pl.ds(2 * n + k, 64, stride=16), :] = (before + z[64:128, c]) + (
                    after + bias2
                )
            return inner

        lax.fori_loop(0, 8, rows, 0, unroll=4)
        det_ref[:, pl.ds(pl.multiple_of(g * 16, 16), 16), :] = (
            turned[...].reshape(64, 16, 128).astype(BF16)
        )
        return carry

    lax.fori_loop(0, 8, group, 0)


def detect(taps, coadd, w1, b1, w2, b2):
    vmem = pl.BlockSpec(memory_space=pltpu.VMEM)
    return pl.pallas_call(
        detect_kernel,
        out_shape=(
            jax.ShapeDtypeStruct((NB, 128, 128), BF16),
            jax.ShapeDtypeStruct((64, 128, 128), BF16),
        ),
        in_specs=[pl.BlockSpec(memory_space=pltpu.SMEM)] + [vmem] * 5,
        out_specs=(vmem, vmem),
        scratch_shapes=[
            pltpu.VMEM((NB, 144, 128), F32),
            pltpu.VMEM((10, 144, 128), F32),
            pltpu.VMEM((144, 128), F32),
            pltpu.VMEM((2, 128, 128), F32),
            pltpu.VMEM((136, 128), F32),
            pltpu.VMEM((136 * 24, 128), F32),
            pltpu.VMEM((2, 24, 256), F32),
            pltpu.VMEM((130, 64, 128), BF16),
            pltpu.VMEM((64 * 16, 128), F32),
            pltpu.VMEM((128, 128), F32),
            pltpu.VMEM((192, 192), BF16),
        ],
        compiler_params=pltpu.CompilerParams(vmem_limit_bytes=48 * 1024 * 1024),
        name="detect",
    )(taps, coadd, w1, b1, w2, b2)


def body(
    tiles,
    tile_weight,
    owners,
    cells,
    psf_kernel,
    conv1_weight,
    conv1_bias,
    conv2_weight,
    conv2_bias,
):
    coadd = exchange(
        tiles.transpose(1, 0, 2),
        tile_weight.transpose(1, 0),
        owners.reshape(1, 128),
        cells.reshape(1, 128),
    )
    return detect(
        psf_kernel.transpose(1, 0, 2),
        coadd,
        conv1_weight.transpose(1, 2, 3, 0),
        conv1_bias.reshape(1, 64),
        conv2_weight.transpose(2, 3, 0, 1),
        conv2_bias.reshape(1, 64),
    )


def solution(mesh):
    in_specs = (
        P(("skyx", "skyy"), None, None),
        P(("skyx", "skyy"), None),
        P(("skyx", "skyy"), None),
        P(("skyx", "skyy")),
        P(),
        P(),
        P(),
        P(),
        P(),
    )
    out_specs = (P(None, "skyy", "skyx"), P(None, "skyy", "skyx"))
    return jax.shard_map(body, mesh=mesh, in_specs=in_specs, out_specs=out_specs, check_vma=False)
```

```python
import functools

import jax
import jax.numpy as jnp
from jax import lax
from jax.experimental import pallas as pl
from jax.experimental.pallas import tpu as pltpu
from jax.sharding import PartitionSpec as P

MESH = pl.DeviceIdType.MESH
F32 = jnp.float32
BF16 = jnp.bfloat16

NB = 6
HALF = 2048
QUARTER = 1024
WIDE = HALF + 128
ORDER = (0, 2, 4, 1, 3, 5)
MEMBERS = ((2, 0), (2, 1), (1, 0), (3, 0), (1, 1), (3, 1), (0, 1))
AROUND = ((-1, 0), (1, 0), (0, -1), (0, 1), (-1, -1), (-1, 1), (1, -1), (1, 1))


def encode(values, denom, flag, size):
    top = jnp.max(jnp.abs(values), axis=1, keepdims=True)
    some = top > 1e-30
    inverse = jnp.where(some, 32767.0 / jnp.where(some, top, 1.0), 0.0)
    codes = (values * inverse + 32768.5).astype(jnp.int32)
    words = codes[:, :QUARTER] | (codes[:, QUARTER:] << 16)
    lane = lax.broadcasted_iota(jnp.int32, (size, 128), 1)
    extra = jnp.where(lane < 64, denom, top * (1.0 / 32767.0))
    return words, jnp.where(lane == 127, flag, extra)


def decode(words, extra):
    step = extra[:, 64:65]
    low = (words & 65535).astype(F32) - 32768.0
    high = lax.shift_right_logical(words, jnp.full_like(words, 16)).astype(F32) - 32768.0
    return low * step, high * step


def gathered(own, own_extra, words, extras):
    low, high = own[:, :QUARTER], own[:, QUARTER:]
    denom, flag = own_extra[:, 0:1], own_extra[:, 127:128]
    for k in range(3):
        a, c = decode(words[k], extras[k])
        low, high, denom = low + a, high + c, denom + extras[k][:, 0:1]
        flag = jnp.maximum(flag, extras[k][:, 127:128])
    return low, high, denom, jnp.max(flag, axis=0, keepdims=True)


def exchange_kernel(
    tiles_hbm,
    wt_ref,
    own_ref,
    cell_ref,
    out_ref,
    tin,
    sel,
    selx,
    meta,
    send_lo,
    send_hi,
    send_x,
    recv_lo,
    recv_hi,
    recv_x,
    acc2,
    st2,
    st2m,
    rcv2,
    rcv2m,
    acc3,
    st3,
    st3m,
    rcv3,
    rcv3m,
    tbuf,
    rbuf,
    hsend,
    hrecv,
    tin_sem,
    self_sem,
    s1_send,
    s1_recv,
    x_send,
    x_recv,
    s2_send,
    s2_recv,
    s3_send,
    s3_recv,
    c_send,
    c_recv,
    h_send,
    h_recv,
):
    ix = lax.axis_index("skyx")
    iy = lax.axis_index("skyy")
    core = ix % 2
    q = (ix // 2, iy % 4, iy // 4)

    def device(axis, step, flip):
        r = list(q)
        if step:
            r[axis] = (r[axis] + step) % 4
        c = (core + flip) % 2 if flip else core
        return (r[0] * 2 + c, r[2] * 4 + r[1])

    def around(dy, dx):
        return ((ix + dx + 8) % 8, (iy + dy + 16) % 16)

    barrier = pltpu.get_barrier_semaphore()
    peers = [device(0, 0, 1)]
    for axis in range(3):
        for step, flip in MEMBERS[:6]:
            peers.append(device(axis, step, flip))
    for dy, dx in AROUND:
        peers.append(around(dy, dx))
    for peer in peers:
        pl.semaphore_signal(barrier, inc=1, device_id=peer, device_id_type=MESH)

    tin_copies = []
    for b in range(NB):
        tin_copies.append(pltpu.make_async_copy(tiles_hbm.at[b], tin.at[b], tin_sem.at[b]))
        tin_copies[b].start()

    own = own_ref[...]
    ox, oy = own // 16, own % 16
    oq = (ox // 2, oy % 4, oy // 4)
    oc = ox % 2
    earlier = lax.broadcasted_iota(jnp.int32, (128, 128), 0) < lax.broadcasted_iota(
        jnp.int32, (128, 128), 1
    )
    rows = lax.broadcasted_iota(jnp.int32, (128, 128), 0)
    rows_x = lax.broadcasted_iota(jnp.int32, (64, 128), 0)
    lane128 = lax.broadcasted_iota(jnp.int32, (128, 128), 1)
    most = jnp.zeros((1, 128), F32)
    codes = []
    for p in range(3):
        group = jnp.broadcast_to(oq[p].astype(F32), (128, 128))
        rank = jnp.sum(
            jnp.where((group == group.T) & earlier, 1.0, 0.0), axis=0, keepdims=True
        )
        most = jnp.maximum(most, rank)
        rank = rank.astype(jnp.int32)
        slot = jnp.where(rank < 32, oq[p] * 32 + rank, -1)
        sel[p] = jnp.where(rows == slot, 1.0, 0.0).astype(BF16)
        slot = jnp.where((rank >= 32) & (rank < 40), oq[p] * 16 + rank - 32, -64)
        selx[p, 0] = jnp.where(rows_x == slot, 1.0, 0.0).astype(BF16)
        selx[p, 1] = jnp.where(rows_x == slot + 8, 1.0, 0.0).astype(BF16)
        unit = oq[(p + 1) % 3] * 4 + oq[(p + 2) % 3]
        codes.append(((unit * 2 + oc) * 4 + cell_ref[...] + 1).astype(F32))
    over = jnp.where(jnp.max(most, axis=1, keepdims=True) > 39.5, 1.0, 0.0)
    meta[...] = jnp.zeros((128, 128), F32)
    meta[0:6, :] = wt_ref[...].astype(F32)

    def pick(which, value):
        return jnp.dot(which, value, preferred_element_type=F32)

    def pick_meta(which):
        return lax.dot_general(
            which,
            meta[...].astype(BF16),
            (((1,), (1,)), ((), ())),
            preferred_element_type=F32,
        )

    s1 = {}
    for n in range(NB):
        p, half = n % 3, n // 3
        if half == 0:
            tin_copies[2 * p].wait()
            tin_copies[2 * p + 1].wait()
            meta[6:7, :] = codes[p]
            flagged = jnp.where(lane128 == 7, over, pick_meta(sel[p])).astype(BF16)
            extra = (pick_meta(selx[p, 0]) + pick_meta(selx[p, 1])).astype(BF16)
        for k in range(2):
            b = 2 * p + k

            def gather(c, carry, b=b, p=p, k=k, half=half):
                at = pl.ds(pl.multiple_of(c * 512, 512), 512)
                there = pl.ds(pl.multiple_of(c * 512 + HALF, 512), 512)
                if half == 0:
                    send_lo[p, k, :, at] = pick(sel[p], tin[b, :, at]).astype(BF16)
                    send_x[p, k, :, at] = (
                        pick(selx[p, 0], tin[b, :, at]) + pick(selx[p, 1], tin[b, :, there])
                    ).astype(BF16)
                else:
                    send_hi[p, k, :, at] = pick(sel[p], tin[b, :, there]).astype(BF16)
                return carry

            lax.fori_loop(0, 4, gather, 0)
            if half == 0:
                send_lo[p, k, :, HALF:WIDE] = flagged
                send_x[p, k, :, HALF:WIDE] = extra
        if n == 0:
            pl.semaphore_wait(barrier, len(peers))
        mine = q[p] * 2 + core
        streams = [(send_hi, recv_hi, 32, s1_send, s1_recv)]
        if half == 0:
            streams = [
                (send_lo, recv_lo, 32, s1_send, s1_recv),
                (send_x, recv_x, 16, x_send, x_recv),
            ]
        local, away = [], []
        for m, (step, flip) in enumerate(MEMBERS + ((0, 0),)):
            to = (q[p] + step) % 4
            parity = (core + flip) % 2
            for w, (src, dst, size, sends, recvs) in enumerate(streams):
                from_ref = src.at[p, parity, pl.ds(pl.multiple_of(to * size, size), size)]
                to_ref = dst.at[p, pl.ds(pl.multiple_of(mine * size, size), size)]
                if (step, flip) == (0, 0):
                    copy = pltpu.make_async_copy(from_ref, to_ref, self_sem.at[n, w])
                    local.append(copy)
                else:
                    at = n if size == 32 else p
                    copy = pltpu.make_async_remote_copy(
                        src_ref=from_ref,
                        dst_ref=to_ref,
                        send_sem=sends.at[at, m],
                        recv_sem=recvs.at[at, m],
                        device_id=device(p, step, flip),
                        device_id_type=MESH,
                    )
                    away.append(copy)
                copy.start()
        s1[n] = (local, away)

    s2, s3, s4 = {}, {}, {}

    def pass_on(n, axis, size, words, extras, to_words, to_extras, send, recv):
        copies = []
        for step in (2, 1, 3):
            there = (q[axis] + step) % 4
            at = pl.ds(pl.multiple_of(there * size, size), size)
            for w, (src, dst) in enumerate(((words, to_words), (extras, to_extras))):
                copy = pltpu.make_async_remote_copy(
                    src_ref=src.at[n, at],
                    dst_ref=dst.at[n, step - 1],
                    send_sem=send.at[n, step - 1, w],
                    recv_sem=recv.at[n, step - 1, w],
                    device_id=device(axis, step, 0),
                    device_id_type=MESH,
                )
                copy.start()
                copies.append(copy)
        return copies

    weighted = {}

    def coefficients(p):
        m = recv_lo[p, :, HALF:WIDE].astype(F32).T
        mx = recv_x[p, :, HALF:WIDE].astype(F32).T
        w = jnp.where(core == 0, m[2 * p : 2 * p + 1], m[2 * p + 1 : 2 * p + 2])
        wx = jnp.where(core == 0, mx[2 * p : 2 * p + 1], mx[2 * p + 1 : 2 * p + 2])
        at = lax.broadcasted_iota(jnp.int32, (128, 256), 0).astype(F32) + 1.0
        c = jnp.where(m[6:7] == at, jnp.broadcast_to(w, (128, 256)), 0.0)
        cx = jnp.where(mx[6:7] == at[:, 0:128], jnp.broadcast_to(wx, (128, 128)), 0.0)
        low = (lane128 // 8) % 2 == 0
        x0, x1 = jnp.where(low, cx, 0.0), jnp.where(low, 0.0, cx)
        denom = jnp.sum(c, axis=1, keepdims=True) + jnp.sum(x0, axis=1, keepdims=True)
        flag = jnp.max(m[7:8], axis=1, keepdims=True)
        return c.astype(BF16), x0.astype(BF16), x1.astype(BF16), denom, flag

    def reduce_tiles(n):
        p, half = n % 3, n // 3
        for copy in s1[n][0]:
            copy.wait()
        for copy in s1[n][1]:
            copy.wait_recv()
        if half == 0:
            weighted[p] = coefficients(p)
        c, x0, x1, denom, flag = weighted[p]
        src = recv_lo if half == 0 else recv_hi
        cx = x0 if half == 0 else x1

        def reduce(i, carry):
            at = pl.ds(pl.multiple_of(i * 512, 512), 512)
            acc2[n, :, at] = pick(c, src[p, :, at]) + pick(cx, recv_x[p, :, at])
            return carry

        lax.fori_loop(0, 4, reduce, 0)
        st2[n], st2m[n] = encode(acc2[n], denom, flag, 128)
        s2[n] = pass_on(n, (p + 1) % 3, 32, st2, st2m, rcv2, rcv2m, s2_send, s2_recv)

    def second(n):
        p = n % 3
        for copy in s2[n]:
            copy.wait_recv()
        at = pl.ds(pl.multiple_of(q[(p + 1) % 3] * 32, 32), 32)
        low, high, denom, flag = gathered(acc2[n, at, :], st2m[n, at, :], rcv2[n], rcv2m[n])
        acc3[n, :, :QUARTER] = low
        acc3[n, :, QUARTER:] = high
        st3[n], st3m[n] = encode(acc3[n], denom, flag, 32)
        s3[n] = pass_on(n, (p + 2) % 3, 8, st3, st3m, rcv3, rcv3m, s3_send, s3_recv)

    def third(n):
        p = n % 3
        for copy in s3[n]:
            copy.wait_recv()
        at = pl.ds(pl.multiple_of(q[(p + 2) % 3] * 8, 8), 8)
        low, high, denom, flag = gathered(acc3[n, at, :], st3m[n, at, :], rcv3[n], rcv3m[n])
        if n == 0:
            out_ref[1248:1256, :] = jnp.broadcast_to(flag, (8, 128))
        scale = 1.0 / (1.0 + denom)
        for j in range(8):
            c = slice(128 * j, 128 * j + 128)
            tbuf[n, pl.ds(j, 8, stride=16), :] = low[:, c] * scale
            tbuf[n, pl.ds(j + 8, 8, stride=16), :] = high[:, c] * scale
        s4[n] = pltpu.make_async_remote_copy(
            src_ref=tbuf.at[n, pl.ds(pl.multiple_of((1 - core) * 64, 64), 64)],
            dst_ref=rbuf.at[n],
            send_sem=c_send.at[n],
            recv_sem=c_recv.at[n],
            device_id=device(0, 0, 1),
            device_id_type=MESH,
        )
        s4[n].start()

    left_half = lax.broadcasted_iota(jnp.int32, (16, 128), 1) < 64
    halo = []

    def place(value, band, half):
        for cy in range(2):
            a, c = value[32 * cy : 32 * cy + 16], value[32 * cy + 16 : 32 * cy + 32]
            y0 = band * 128 + 64 * cy + 32 * half
            out_ref[pl.ds(y0, 16, stride=2), :] = jnp.where(left_half, a, pltpu.roll(c, 64, 1))
            out_ref[pl.ds(y0 + 1, 16, stride=2), :] = jnp.where(
                left_half, pltpu.roll(a, 64, 1), c
            )

    def fourth(n):
        p, half = n % 3, n // 3
        place(tbuf[n, pl.ds(pl.multiple_of(core * 64, 64), 64), :], 2 * p + core, half)
        s4[n].wait_recv()
        place(rbuf[n], 2 * p + 1 - core, half)
        if half == 0:
            return
        for b in (2 * p, 2 * p + 1):
            r = 128 * b
            hsend[0, b] = out_ref[r : r + 8, :]
            hsend[1, b] = out_ref[r + 120 : r + 128, :]
            turned = out_ref[r : r + 128, :].T
            hsend[2, b] = turned[0:8, :]
            hsend[3, b] = turned[120:128, :]
            out_ref[1152 + 8 * b : 1160 + 8 * b, :] = turned[0:8, :]
            out_ref[1200 + 8 * b : 1208 + 8 * b, :] = turned[120:128, :]
        bands = pl.ds(2 * p, 2)
        for m, (dy, dx) in enumerate(AROUND):
            which = 0 if dy < 0 else 1 if dy > 0 else 2 if dx < 0 else 3
            copy = pltpu.make_async_remote_copy(
                src_ref=hsend.at[which, bands],
                dst_ref=hrecv.at[m, bands],
                send_sem=h_send.at[p, m],
                recv_sem=h_recv.at[p, m],
                device_id=around(dy, dx),
                device_id_type=MESH,
            )
            copy.start()
            halo.append(copy)

    steps = (reduce_tiles, second, third, fourth)
    for n in range(6 + 6):
        for lag, step in zip((0, 2, 4, 5), steps):
            if 0 <= n - lag < 6:
                step(n - lag)

    for n in range(NB):
        for copy in s1[n][1] + s2[n] + s3[n] + [s4[n]]:
            copy.wait_send()
    for n, copy in enumerate(halo):
        copy.wait_recv()
        p, slot = n // 8, n % 8
        r = 768 + 48 * slot + 16 * p
        out_ref[r : r + 16, :] = hrecv[slot, 2 * p : 2 * p + 2].reshape(16, 128)
    for copy in halo:
        copy.wait_send()


def exchange(tiles, weights, owners, cells):
    vmem = pl.BlockSpec(memory_space=pltpu.VMEM)
    dma = pltpu.SemaphoreType.DMA
    return pl.pallas_call(
        exchange_kernel,
        out_shape=jax.ShapeDtypeStruct((1256, 128), F32),
        in_specs=[pl.BlockSpec(memory_space=pl.ANY), vmem, vmem, vmem],
        out_specs=vmem,
        scratch_shapes=[
            pltpu.VMEM((NB, 128, 4096), BF16),
            pltpu.VMEM((3, 128, 128), BF16),
            pltpu.VMEM((3, 2, 64, 128), BF16),
            pltpu.VMEM((128, 128), F32),
            pltpu.VMEM((3, 2, 128, WIDE), BF16),
            pltpu.VMEM((3, 2, 128, HALF), BF16),
            pltpu.VMEM((3, 2, 64, WIDE), BF16),
            pltpu.VMEM((3, 256, WIDE), BF16),
            pltpu.VMEM((3, 256, HALF), BF16),
            pltpu.VMEM((3, 128, WIDE), BF16),
            pltpu.VMEM((NB, 128, HALF), F32),
            pltpu.VMEM((NB, 128, QUARTER), jnp.int32),
            pltpu.VMEM((NB, 128, 128), F32),
            pltpu.VMEM((NB, 3, 32, QUARTER), jnp.int32),
            pltpu.VMEM((NB, 3, 32, 128), F32),
            pltpu.VMEM((NB, 32, HALF), F32),
            pltpu.VMEM((NB, 32, QUARTER), jnp.int32),
            pltpu.VMEM((NB, 32, 128), F32),
            pltpu.VMEM((NB, 3, 8, QUARTER), jnp.int32),
            pltpu.VMEM((NB, 3, 8, 128), F32),
            pltpu.VMEM((NB, 128, 128), F32),
            pltpu.VMEM((NB, 64, 128), F32),
            pltpu.VMEM((4, NB, 8, 128), F32),
            pltpu.VMEM((8, NB, 8, 128), F32),
            dma((NB,)),
            dma((NB, 2)),
            dma((NB, 7)),
            dma((NB, 7)),
            dma((3, 7)),
            dma((3, 7)),
            dma((NB, 3, 2)),
            dma((NB, 3, 2)),
            dma((NB, 3, 2)),
            dma((NB, 3, 2)),
            dma((NB,)),
            dma((NB,)),
            dma((3, 8)),
            dma((3, 8)),
        ],
        compiler_params=pltpu.CompilerParams(
            collective_id=0, has_side_effects=True, vmem_limit_bytes=60 * 1024 * 1024
        ),
        name="tile_exchange",
    )(tiles, weights, owners, cells)


def full_exchange_kernel(
    tiles_hbm,
    wt_ref,
    own_ref,
    cell_ref,
    out_ref,
    tin,
    sel,
    meta,
    metar,
    send_a,
    send_b,
    recv_a,
    recv_b,
    acc2,
    st2,
    st2m,
    rcv2,
    rcv2m,
    acc3,
    st3,
    st3m,
    rcv3,
    rcv3m,
    tbuf,
    hsend,
    hrecv,
    tin_sem,
    self_sem,
    s1_send,
    s1_recv,
    s2_send,
    s2_recv,
    s3_send,
    s3_recv,
    h_send,
    h_recv,
):
    ix = lax.axis_index("skyx")
    iy = lax.axis_index("skyy")
    core = ix % 2
    q = (ix // 2, iy % 4, iy // 4)

    def device(axis, step, flip):
        r = list(q)
        if step:
            r[axis] = (r[axis] + step) % 4
        c = (core + flip) % 2 if flip else core
        return (r[0] * 2 + c, r[2] * 4 + r[1])

    def around(dy, dx):
        return ((ix + dx + 8) % 8, (iy + dy + 16) % 16)

    barrier = pltpu.get_barrier_semaphore()
    peers = [device(0, 0, 1)]
    for axis in range(3):
        for step, flip in MEMBERS[:6]:
            peers.append(device(axis, step, flip))
    for dy, dx in AROUND:
        peers.append(around(dy, dx))
    for peer in peers:
        pl.semaphore_signal(barrier, inc=1, device_id=peer, device_id_type=MESH)

    tin_copies = {}
    for b in ORDER:
        tin_copies[b] = pltpu.make_async_copy(tiles_hbm.at[b], tin.at[b], tin_sem.at[b])
        tin_copies[b].start()

    own = own_ref[...]
    ox, oy = own // 16, own % 16
    oq = (ox // 2, oy % 4, oy // 4)
    oc = ox % 2
    ownf = jnp.broadcast_to(own.astype(F32), (128, 128))
    same = ownf == ownf.T
    earlier = lax.broadcasted_iota(jnp.int32, (128, 128), 0) < lax.broadcasted_iota(
        jnp.int32, (128, 128), 1
    )
    rank = jnp.sum(jnp.where(same & earlier, 1.0, 0.0), axis=0, keepdims=True).astype(jnp.int32)
    rows = lax.broadcasted_iota(jnp.int32, (256, 128), 0)
    for p in range(3):
        slot = (oq[p] * 2 + oc) * 32 + (oq[(p + 1) % 3] * 4 + oq[(p + 2) % 3]) * 2 + rank
        sel[p] = jnp.where(rows == slot, 1.0, 0.0).astype(BF16)
    meta[...] = jnp.zeros((128, 128), F32)
    meta[0:6, :] = wt_ref[...].astype(F32)
    meta[6:7, :] = cell_ref[...].astype(F32) + 1.0

    s1 = {}

    def stage1_refs(b):
        p, k = b // 2, b % 2
        return (send_a.at[p], recv_a.at[p]) if k == 0 else (send_b.at[p], recv_b.at[p])

    for n, b in enumerate(ORDER):
        p, k = b // 2, b % 2
        src, dst = stage1_refs(b)
        tin_copies[b].wait()

        def gather(c, carry, b=b, p=p, src=src):
            at = pl.ds(pl.multiple_of(c * 512, 512), 512)
            src[:, at] = jnp.dot(sel[p], tin[b, :, at], preferred_element_type=F32).astype(BF16)
            return carry

        lax.fori_loop(0, 8, gather, 0)
        if k == 0:
            src[:, 4096:4224] = lax.dot_general(
                sel[p],
                meta[...].astype(BF16),
                (((1,), (1,)), ((), ())),
                preferred_element_type=F32,
            ).astype(BF16)
        if n == 0:
            pl.semaphore_wait(barrier, len(peers))
        mine = q[p] * 2 + core
        mine_rows = pl.ds(pl.multiple_of(mine * 32, 32), 32)
        own_copy = pltpu.make_async_copy(src.at[mine_rows], dst.at[mine_rows], self_sem.at[b])
        own_copy.start()
        copies = [own_copy]
        for m, (step, flip) in enumerate(MEMBERS):
            there = ((q[p] + step) % 4) * 2 + (core + flip) % 2
            copy = pltpu.make_async_remote_copy(
                src_ref=src.at[pl.ds(pl.multiple_of(there * 32, 32), 32)],
                dst_ref=dst.at[mine_rows],
                send_sem=s1_send.at[b, m],
                recv_sem=s1_recv.at[b, m],
                device_id=device(p, step, flip),
                device_id_type=MESH,
            )
            copy.start()
            copies.append(copy)
        s1[b] = copies

    s2, s3 = {}, {}

    def encode(values, denom, size):
        top = jnp.max(jnp.abs(values), axis=1, keepdims=True)
        some = top > 1e-30
        inverse = jnp.where(some, 32767.0 / jnp.where(some, top, 1.0), 0.0)
        codes = (values * inverse + 32768.5).astype(jnp.int32)
        words = codes[:, :QUARTER] | (codes[:, QUARTER:] << 16)
        lane = lax.broadcasted_iota(jnp.int32, (size, 128), 1)
        return words, jnp.where(lane < 64, denom, top * (1.0 / 32767.0))

    def decode(words, extra):
        step = extra[:, 64:65]
        low = (words & 65535).astype(F32) - 32768.0
        high = lax.shift_right_logical(words, jnp.full_like(words, 16)).astype(F32) - 32768.0
        return low * step, high * step

    def gathered(own, own_denom, words, extras):
        low, high, denom = own[:, :QUARTER], own[:, QUARTER:], own_denom
        for k in range(3):
            a, c = decode(words[k], extras[k])
            low, high, denom = low + a, high + c, denom + extras[k][:, 0:1]
        return low, high, denom

    def pass_on(b, axis, size, words, extras, to_words, to_extras, send, recv):
        copies = []
        for step in (2, 1, 3):
            there = (q[axis] + step) % 4
            at = pl.ds(pl.multiple_of(there * size, size), size)
            for n, (src, dst) in enumerate(((words, to_words), (extras, to_extras))):
                copy = pltpu.make_async_remote_copy(
                    src_ref=src.at[b, at],
                    dst_ref=dst.at[b, step - 1],
                    send_sem=send.at[b, step - 1, n],
                    recv_sem=recv.at[b, step - 1, n],
                    device_id=device(axis, step, 0),
                    device_id_type=MESH,
                )
                copy.start()
                copies.append(copy)
        return copies

    def reduce_tiles(b):
        p, k = b // 2, b % 2
        src, dst = stage1_refs(b)
        s1[b][0].wait()
        for copy in s1[b][1:]:
            copy.wait_recv()
        if k == 0:
            metar[p] = dst[:, 4096:4224].astype(F32).T[0:8, :]
        w = metar[p, b : b + 1, :]
        code = metar[p, 6:7, :].astype(jnp.int32)
        row = lax.broadcasted_iota(jnp.int32, (128, 256), 0)
        col = lax.broadcasted_iota(jnp.int32, (128, 256), 1)
        hit = ((col % 32) // 2 == row // 8) & (code == row % 4 + 1)
        upper = (row // 4) % 2 == 0
        both = jnp.where(hit, jnp.broadcast_to(w, (128, 256)), 0.0)
        c0 = jnp.where(upper, both, 0.0).astype(BF16)
        c1 = jnp.where(upper, 0.0, both).astype(BF16)
        denom = jnp.sum(both, axis=1, keepdims=True)

        def reduce(c, carry):
            lo = pl.ds(pl.multiple_of(c * 512, 512), 512)
            hi = pl.ds(pl.multiple_of(c * 512 + HALF, 512), 512)
            acc2[b, :, lo] = jnp.dot(c0, dst[:, lo], preferred_element_type=F32) + jnp.dot(
                c1, dst[:, hi], preferred_element_type=F32
            )
            return carry

        lax.fori_loop(0, 4, reduce, 0)
        st2[b], st2m[b] = encode(acc2[b], denom, 128)
        s2[b] = pass_on(b, (p + 1) % 3, 32, st2, st2m, rcv2, rcv2m, s2_send, s2_recv)

    def second(b):
        p = b // 2
        for copy in s2[b]:
            copy.wait_recv()
        at = pl.ds(pl.multiple_of(q[(p + 1) % 3] * 32, 32), 32)
        low, high, denom = gathered(acc2[b, at, :], st2m[b, at, 0:1], rcv2[b], rcv2m[b])
        acc3[b, :, :QUARTER] = low
        acc3[b, :, QUARTER:] = high
        st3[b], st3m[b] = encode(acc3[b], denom, 32)
        s3[b] = pass_on(b, (p + 2) % 3, 8, st3, st3m, rcv3, rcv3m, s3_send, s3_recv)

    left_half = lax.broadcasted_iota(jnp.int32, (16, 128), 1) < 64

    def third(b):
        p = b // 2
        axis = (p + 2) % 3
        for copy in s3[b]:
            copy.wait_recv()
        at = pl.ds(pl.multiple_of(q[axis] * 8, 8), 8)
        low, high, denom = gathered(acc3[b, at, :], st3m[b, at, 0:1], rcv3[b], rcv3m[b])
        scale = 1.0 / (1.0 + denom)
        for j in range(8):
            c = slice(128 * j, 128 * j + 128)
            tbuf[pl.ds(j, 8, stride=16), :] = low[:, c] * scale
            tbuf[pl.ds(j + 8, 8, stride=16), :] = high[:, c] * scale
        for h in range(2):
            for cy in range(2):
                s = h * 4 + cy * 2
                a = tbuf[16 * s : 16 * s + 16, :]
                c = tbuf[16 * s + 16 : 16 * s + 32, :]
                y0 = 64 * cy + 32 * h
                out_ref[pl.ds(128 * b + y0, 16, stride=2), :] = jnp.where(
                    left_half, a, pltpu.roll(c, 64, 1)
                )
                out_ref[pl.ds(128 * b + y0 + 1, 16, stride=2), :] = jnp.where(
                    left_half, pltpu.roll(a, 64, 1), c
                )
        r = 128 * b
        n = ORDER.index(b)
        hsend[0, n] = out_ref[r : r + 8, :]
        hsend[1, n] = out_ref[r + 120 : r + 128, :]
        turned = out_ref[r : r + 128, :].T
        hsend[2, n] = turned[0:8, :]
        hsend[3, n] = turned[120:128, :]
        out_ref[1152 + 8 * b : 1160 + 8 * b, :] = turned[0:8, :]
        out_ref[1200 + 8 * b : 1208 + 8 * b, :] = turned[120:128, :]

    halo = []

    def send_halo(group):
        bands = pl.ds(3 * group, 3)
        for n, (dy, dx) in enumerate(AROUND):
            which = 0 if dy < 0 else 1 if dy > 0 else 2 if dx < 0 else 3
            copy = pltpu.make_async_remote_copy(
                src_ref=hsend.at[which, bands],
                dst_ref=hrecv.at[n, bands],
                send_sem=h_send.at[group, n],
                recv_sem=h_recv.at[group, n],
                device_id=around(dy, dx),
                device_id_type=MESH,
            )
            copy.start()
            halo.append(copy)

    for n in range(6 + 4):
        if n < 6:
            reduce_tiles(ORDER[n])
        if 0 <= n - 2 < 6:
            second(ORDER[n - 2])
        if 0 <= n - 4 < 6:
            third(ORDER[n - 4])
            if n - 4 in (2, 5):
                send_halo((n - 4) // 3)

    for b in ORDER:
        for copy in s1[b][1:] + s2[b] + s3[b]:
            copy.wait_send()
    for n, copy in enumerate(halo):
        copy.wait_recv()
        group, slot = n // 8, n % 8
        for k in range(3):
            r = 768 + 48 * slot + 8 * ORDER[3 * group + k]
            out_ref[r : r + 8, :] = hrecv[slot, 3 * group + k]
    out_ref[1248:1256, :] = jnp.zeros((8, 128), F32)
    for copy in halo:
        copy.wait_send()


def full_exchange(tiles, weights, owners, cells):
    vmem = pl.BlockSpec(memory_space=pltpu.VMEM)
    dma = pltpu.SemaphoreType.DMA
    return pl.pallas_call(
        full_exchange_kernel,
        out_shape=jax.ShapeDtypeStruct((1256, 128), F32),
        in_specs=[pl.BlockSpec(memory_space=pl.ANY), vmem, vmem, vmem],
        out_specs=vmem,
        scratch_shapes=[
            pltpu.VMEM((NB, 128, 4096), BF16),
            pltpu.VMEM((3, 256, 128), BF16),
            pltpu.VMEM((128, 128), F32),
            pltpu.VMEM((3, 8, 256), F32),
            pltpu.VMEM((3, 256, 4224), BF16),
            pltpu.VMEM((3, 256, 4096), BF16),
            pltpu.VMEM((3, 256, 4224), BF16),
            pltpu.VMEM((3, 256, 4096), BF16),
            pltpu.VMEM((NB, 128, HALF), F32),
            pltpu.VMEM((NB, 128, QUARTER), jnp.int32),
            pltpu.VMEM((NB, 128, 128), F32),
            pltpu.VMEM((NB, 3, 32, QUARTER), jnp.int32),
            pltpu.VMEM((NB, 3, 32, 128), F32),
            pltpu.VMEM((NB, 32, HALF), F32),
            pltpu.VMEM((NB, 32, QUARTER), jnp.int32),
            pltpu.VMEM((NB, 32, 128), F32),
            pltpu.VMEM((NB, 3, 8, QUARTER), jnp.int32),
            pltpu.VMEM((NB, 3, 8, 128), F32),
            pltpu.VMEM((128, 128), F32),
            pltpu.VMEM((4, NB, 8, 128), F32),
            pltpu.VMEM((8, NB, 8, 128), F32),
            dma((NB,)),
            dma((NB,)),
            dma((NB, 7)),
            dma((NB, 7)),
            dma((NB, 3, 2)),
            dma((NB, 3, 2)),
            dma((NB, 3, 2)),
            dma((NB, 3, 2)),
            dma((2, 8)),
            dma((2, 8)),
        ],
        compiler_params=pltpu.CompilerParams(
            collective_id=1, has_side_effects=True, vmem_limit_bytes=60 * 1024 * 1024
        ),
        name="full_exchange",
    )(tiles, weights, owners, cells)


def detect_kernel(
    taps_ref,
    coadd_ref,
    w1_ref,
    b1_ref,
    w2_ref,
    b2_ref,
    psf_ref,
    det_ref,
    ext,
    shifted,
    sides,
    sides_t,
    psf,
    taps3,
    edge3,
    hidden,
    turned,
    small,
    w2s,
):
    ix = lax.axis_index("skyx")
    iy = lax.axis_index("skyy")
    top, bottom = (iy > 0).astype(F32), (iy < 15).astype(F32)
    left, right = (ix > 0).astype(F32), (ix < 7).astype(F32)

    def halo(slot, b):
        r = 768 + slot * 48 + b * 8
        return coadd_ref[r : r + 8, :]

    def lanes_of(n):
        return lax.broadcasted_iota(jnp.int32, (n, 128), 1)

    small[...] = jnp.zeros((128, 128), F32)
    for b in range(NB):
        for i in range(3):
            small[pl.ds(i * 24 + b, 3, stride=8), 0:64] = w1_ref[b, i].astype(F32)
    w1 = (small[...].T[0:64, 0:72] * 0.5).astype(BF16)
    for j in range(3):
        for i in range(3):
            w2s[64 * j : 64 * j + 64, 64 * i : 64 * i + 64] = w2_ref[i, j]
    small[0:1, 0:64] = b1_ref[...] * 0.5
    small[1:2, 0:64] = b2_ref[...]
    columns = small[...].T
    bias1 = jnp.broadcast_to(columns[0:64, 0:1], (64, 256))
    bias2 = jnp.broadcast_to(columns[0:64, 1:2], (64, 128))

    pieces = []
    for b in range(NB):
        pieces += [
            halo(3, b)[2:8] * left,
            halo(8, b)[0:4],
            halo(9, b)[4:8],
            halo(2, b)[0:6] * right,
        ]
    pieces.append(jnp.zeros((8, 128), F32))
    sides[8:136, :] = jnp.concatenate(pieces, axis=0).T
    lane8 = lanes_of(8)
    for r, mid, at_left, at_right, keep in ((0, 1, 7, 6, top), (136, 0, 5, 4, bottom)):
        line = jnp.zeros((8, 128), F32)
        for b in range(NB):
            middle = halo(mid, b)
            parts = (
                (halo(at_left, b) * left, 122, 0, 6),
                (middle, 0, 6, 4),
                (middle, 124, 10, 4),
                (halo(at_right, b) * right, 0, 14, 6),
            )
            for value, start, at, size in parts:
                at = 20 * b + at
                moved = pltpu.roll(value, (at - start) % 128, 1)
                line = jnp.where((lane8 >= at) & (lane8 < at + size), moved, line)
        sides[r : r + 8, :] = line * keep

    for j in range(9):
        shifted[j] = pltpu.roll(sides[...], (-j) % 128, 1) if j else sides[...]
    owner_band = lane8 // 20

    def edge_block(start, size):
        acc = jnp.zeros((size, 128), F32)
        for i in range(9):
            for j in range(9):
                tap = jnp.full((8, 128), taps_ref[i, 0, j], F32)
                for b in range(1, NB):
                    tap = jnp.where(owner_band == b, taps_ref[i, b, j], tap)
                tap = jnp.broadcast_to(tap[0:1], (size, 128))
                acc = acc + tap * shifted[j, start + i : start + i + size, :]
        at = lax.broadcasted_iota(jnp.int32, (size, 128), 0) + start
        keep = jnp.where(at < 4, top, jnp.where(at >= 132, bottom, 1.0))
        keep = keep * jnp.where(lanes_of(size) % 20 < 10, left, right)
        return acc.astype(BF16).astype(F32) * keep

    sides[0:136, :] = edge_block(0, 136)

    taps3[...] = jnp.zeros_like(taps3)
    for b in range(NB):
        ext[b, 8:136, :] = coadd_ref[128 * b : 128 * b + 128, :]
        ext[b, 0:8, :] = halo(1, b) * top
        ext[b, 136:144, :] = halo(0, b) * bottom
    column = lanes_of(144)

    def band(b, carry):
        near_left = pltpu.roll(shifted[0], 122 - 20 * b, 1)
        near_right = pltpu.roll(shifted[0], 114 - 20 * b, 1)
        x = ext[b]
        for j in range(9):
            if j < 4:
                moved = pltpu.roll(jnp.where(column >= 124 + j, near_left, x), 4 - j, 1)
            elif j == 4:
                moved = x
            else:
                moved = pltpu.roll(jnp.where(column < j - 4, near_right, x), 132 - j, 1)
            shifted[j + 1] = moved

        def block(start, size):
            acc = jnp.zeros((size, 128), F32)
            for i in range(9):
                for j in range(9):
                    acc = acc + taps_ref[i, b, j] * shifted[j + 1, start + i : start + i + size, :]
            at = lax.broadcasted_iota(jnp.int32, (size, 128), 0) + start
            keep = jnp.where(at < 4, top, jnp.where(at >= 132, bottom, 1.0))
            v = acc.astype(BF16).astype(F32) * keep
            psf[start : start + size, :] = v
            lane = lanes_of(size)
            edge = sides[start : start + size, :]
            before = jnp.where(lane == 0, pltpu.roll(edge, 127 - 20 * b, 1), pltpu.roll(v, 1, 1))
            after = jnp.where(
                lane == 127, pltpu.roll(edge, 117 - 20 * b, 1), pltpu.roll(v, 127, 1)
            )
            for j, value in enumerate((before, v, after)):
                taps3[pl.ds(start * 24 + 8 * j + b, size, stride=24), :] = value
            edge = jnp.where(lane == 20 * b + 2, pltpu.roll(v, 20 * b + 2, 1), edge)
            edge = jnp.where(lane == 20 * b + 9, pltpu.roll(v, 20 * b + 10, 1), edge)
            sides[start : start + size, :] = edge

        block(0, 72)
        block(72, 64)
        psf_ref[b] = psf[4:132, :].astype(BF16)
        return carry

    lax.fori_loop(0, NB, band, 0)

    def silu(u):
        return u + u * jnp.tanh(u)

    def first(n, carry):
        at0 = pl.ds(pl.multiple_of((2 * n + 2) * 24, 8), 72)
        at1 = pl.ds(pl.multiple_of((2 * n + 3) * 24, 8), 72)
        rhs = jnp.concatenate([taps3[at0, :], taps3[at1, :]], axis=1).astype(BF16)
        v = silu(jnp.dot(w1, rhs, preferred_element_type=F32) + bias1)
        hidden[2 * n] = v[:, 0:128].astype(BF16)
        hidden[2 * n + 1] = v[:, 128:256].astype(BF16)
        return carry

    lax.fori_loop(0, 65, first, 0, unroll=5)
    hidden[0] = (hidden[0].astype(F32) * top).astype(BF16)
    hidden[129] = (hidden[129].astype(F32) * bottom).astype(BF16)

    sides_t[0] = sides[0:128, :].T
    tail = jnp.concatenate([sides[128:136, :], jnp.zeros((120, 128), F32)], axis=0)
    sides_t[1] = tail.T
    edge3[...] = jnp.zeros_like(edge3)
    at256 = lax.broadcasted_iota(jnp.int32, (64, 256), 1)
    ends = jnp.where(at256 == 0, top, jnp.where(at256 == 129, bottom, 1.0))
    beside = []
    for side, (offset, keep) in enumerate(((0, left), (9, right))):
        for t in range(2):
            for j in range(3):
                edge3[side, 8 * j : 8 * j + 6, 128 * t : 128 * t + 128] = sides_t[
                    t, pl.ds(offset + j, 6, stride=20), :
                ]
        x = edge3[side]
        rhs = jnp.concatenate([pltpu.roll(x, 256 - (2 + i), 1) for i in range(3)], axis=0)
        v = silu(jnp.dot(w1, rhs.astype(BF16), preferred_element_type=F32) + bias1)
        v = (v * (ends * keep)).astype(BF16).astype(F32)
        rhs = jnp.concatenate(
            [v[:, 0:128]] + [pltpu.roll(v, 256 - i, 1)[:, 0:128] for i in (1, 2)], axis=0
        )
        weight = w2s[0:64, :] if side == 0 else w2s[128:192, :]
        beside.append(jnp.dot(weight, rhs.astype(BF16), preferred_element_type=F32))
    small[0:64, :] = beside[0]
    small[64:128, :] = beside[1]

    w2 = w2s[...]
    lane64 = lanes_of(64)

    def group(g, carry):
        def rows(n, inner):
            y = g * 16 + 2 * n
            rhs = jnp.concatenate(
                [hidden[pl.ds(y, 3)].reshape(192, 128), hidden[pl.ds(y + 1, 3)].reshape(192, 128)],
                axis=1,
            )
            z = jnp.dot(w2, rhs, preferred_element_type=F32)
            for k in range(2):
                c = slice(128 * k, 128 * k + 128)
                near = pltpu.roll(small[0:64, :], 128 - (y + k), 1)
                far = pltpu.roll(small[64:128, :], 127 - (y + k), 1)
                before = jnp.where(lane64 == 0, near, pltpu.roll(z[0:64, c], 1, 1))
                after = jnp.where(lane64 == 127, far, pltpu.roll(z[128:192, c], 127, 1))
                turned[pl.ds(2 * n + k, 64, stride=16), :] = (before + z[64:128, c]) + (
                    after + bias2
                )
            return inner

        lax.fori_loop(0, 8, rows, 0, unroll=4)
        det_ref[:, pl.ds(pl.multiple_of(g * 16, 16), 16), :] = (
            turned[...].reshape(64, 16, 128).astype(BF16)
        )
        return carry

    lax.fori_loop(0, 8, group, 0)


def detect(taps, coadd, w1, b1, w2, b2):
    vmem = pl.BlockSpec(memory_space=pltpu.VMEM)
    return pl.pallas_call(
        detect_kernel,
        out_shape=(
            jax.ShapeDtypeStruct((NB, 128, 128), BF16),
            jax.ShapeDtypeStruct((64, 128, 128), BF16),
        ),
        in_specs=[pl.BlockSpec(memory_space=pltpu.SMEM)] + [vmem] * 5,
        out_specs=(vmem, vmem),
        scratch_shapes=[
            pltpu.VMEM((NB, 144, 128), F32),
            pltpu.VMEM((10, 144, 128), F32),
            pltpu.VMEM((144, 128), F32),
            pltpu.VMEM((2, 128, 128), F32),
            pltpu.VMEM((136, 128), F32),
            pltpu.VMEM((136 * 24, 128), F32),
            pltpu.VMEM((2, 24, 256), F32),
            pltpu.VMEM((130, 64, 128), BF16),
            pltpu.VMEM((64 * 16, 128), F32),
            pltpu.VMEM((128, 128), F32),
            pltpu.VMEM((192, 192), BF16),
        ],
        compiler_params=pltpu.CompilerParams(vmem_limit_bytes=48 * 1024 * 1024),
        name="detect",
    )(taps, coadd, w1, b1, w2, b2)


def body(
    tiles,
    tile_weight,
    owners,
    cells,
    psf_kernel,
    conv1_weight,
    conv1_bias,
    conv2_weight,
    conv2_bias,
):
    operands = (
        tiles.transpose(1, 0, 2),
        tile_weight.transpose(1, 0),
        owners.reshape(1, 128),
        cells.reshape(1, 128),
    )
    coadd = exchange(*operands)
    coadd = lax.cond(coadd[1248, 0] > 0.5, lambda: full_exchange(*operands), lambda: coadd)
    return detect(
        psf_kernel.transpose(1, 0, 2),
        coadd,
        conv1_weight.transpose(1, 2, 3, 0),
        conv1_bias.reshape(1, 64),
        conv2_weight.transpose(2, 3, 0, 1),
        conv2_bias.reshape(1, 64),
    )


def solution(mesh):
    in_specs = (
        P(("skyx", "skyy"), None, None),
        P(("skyx", "skyy"), None),
        P(("skyx", "skyy"), None),
        P(("skyx", "skyy")),
        P(),
        P(),
        P(),
        P(),
        P(),
    )
    out_specs = (P(None, "skyy", "skyx"), P(None, "skyy", "skyx"))
    return jax.shard_map(body, mesh=mesh, in_specs=in_specs, out_specs=out_specs, check_vma=False)
```

```python
import functools

import jax
import jax.numpy as jnp
from jax import lax
from jax.experimental import pallas as pl
from jax.experimental.pallas import tpu as pltpu
from jax.sharding import PartitionSpec as P

MESH = pl.DeviceIdType.MESH
F32 = jnp.float32
BF16 = jnp.bfloat16

NB = 6
HALF = 2048
QUARTER = 1024
WIDE = HALF + 128
PIECES = ((0, 0, 2048), (1, 0, 2048))
UNITS = 3 * len(PIECES)
LAGS = (0, 2, 4, 5)
ORDER = (0, 2, 4, 1, 3, 5)
MEMBERS = ((2, 0), (2, 1), (1, 0), (3, 0), (1, 1), (3, 1), (0, 1))
AROUND = ((-1, 0), (1, 0), (0, -1), (0, 1), (-1, -1), (-1, 1), (1, -1), (1, 1))


def encode(values, denom, flag, size):
    top = jnp.max(jnp.abs(values), axis=1, keepdims=True)
    some = top > 1e-30
    inverse = jnp.where(some, 32767.0 / jnp.where(some, top, 1.0), 0.0)
    codes = (values * inverse + 32768.5).astype(jnp.int32)
    middle = values.shape[1] // 2
    words = codes[:, :middle] | (codes[:, middle:] << 16)
    lane = lax.broadcasted_iota(jnp.int32, (size, 128), 1)
    extra = jnp.where(lane < 64, denom, top * (1.0 / 32767.0))
    return words, jnp.where(lane == 127, flag, extra)


def decode(words, extra):
    step = extra[:, 64:65]
    low = (words & 65535).astype(F32) - 32768.0
    high = lax.shift_right_logical(words, jnp.full_like(words, 16)).astype(F32) - 32768.0
    return low * step, high * step


def gathered(own, own_extra, words, extras):
    middle = own.shape[1] // 2
    low, high = own[:, :middle], own[:, middle:]
    denom, flag = own_extra[:, 0:1], own_extra[:, 127:128]
    for k in range(3):
        a, c = decode(words[k], extras[k])
        low, high, denom = low + a, high + c, denom + extras[k][:, 0:1]
        flag = jnp.maximum(flag, extras[k][:, 127:128])
    return low, high, denom, jnp.max(flag, axis=0, keepdims=True)


def exchange_kernel(
    tiles_hbm,
    wt_ref,
    own_ref,
    cell_ref,
    out_ref,
    tin,
    sel,
    selx,
    meta,
    send_lo,
    send_hi,
    send_x,
    recv_lo,
    recv_hi,
    recv_x,
    acc2,
    st2,
    st2m,
    rcv2,
    rcv2m,
    acc3,
    st3,
    st3m,
    rcv3,
    rcv3m,
    tbuf,
    rbuf,
    hsend,
    hrecv,
    tin_sem,
    self_sem,
    s1_send,
    s1_recv,
    x_send,
    x_recv,
    s2_send,
    s2_recv,
    s3_send,
    s3_recv,
    c_send,
    c_recv,
    h_send,
    h_recv,
):
    ix = lax.axis_index("skyx")
    iy = lax.axis_index("skyy")
    core = ix % 2
    q = (ix // 2, iy % 4, iy // 4)

    def device(axis, step, flip):
        r = list(q)
        if step:
            r[axis] = (r[axis] + step) % 4
        c = (core + flip) % 2 if flip else core
        return (r[0] * 2 + c, r[2] * 4 + r[1])

    def around(dy, dx):
        return ((ix + dx + 8) % 8, (iy + dy + 16) % 16)

    barrier = pltpu.get_barrier_semaphore()
    peers = [device(0, 0, 1)]
    for axis in range(3):
        for step, flip in MEMBERS[:6]:
            peers.append(device(axis, step, flip))
    for dy, dx in AROUND:
        peers.append(around(dy, dx))
    for peer in peers:
        pl.semaphore_signal(barrier, inc=1, device_id=peer, device_id_type=MESH)

    tin_copies = []
    for b in range(NB):
        tin_copies.append(pltpu.make_async_copy(tiles_hbm.at[b], tin.at[b], tin_sem.at[b]))
        tin_copies[b].start()

    own = own_ref[...]
    ox, oy = own // 16, own % 16
    oq = (ox // 2, oy % 4, oy // 4)
    oc = ox % 2
    earlier = lax.broadcasted_iota(jnp.int32, (128, 128), 0) < lax.broadcasted_iota(
        jnp.int32, (128, 128), 1
    )
    rows = lax.broadcasted_iota(jnp.int32, (128, 128), 0)
    rows_x = lax.broadcasted_iota(jnp.int32, (64, 128), 0)
    lane128 = lax.broadcasted_iota(jnp.int32, (128, 128), 1)
    meta[...] = jnp.zeros((128, 128), F32)
    meta[0:6, :] = wt_ref[...].astype(F32)

    def select(p):
        group = jnp.broadcast_to(oq[p].astype(F32), (128, 128))
        rank = jnp.sum(
            jnp.where((group == group.T) & earlier, 1.0, 0.0), axis=0, keepdims=True
        )
        over = jnp.where(jnp.max(rank, axis=1, keepdims=True) > 39.5, 1.0, 0.0)
        rank = rank.astype(jnp.int32)
        slot = jnp.where(rank < 32, oq[p] * 32 + rank, -1)
        sel[p, 0:128] = jnp.where(rows == slot, 1.0, 0.0).astype(BF16)
        slot = jnp.where((rank >= 32) & (rank < 40), oq[p] * 16 + rank - 32, -64)
        sel[p, 128:192] = jnp.where(rows_x == slot, 1.0, 0.0).astype(BF16)
        selx[p] = jnp.where(rows_x == slot + 8, 1.0, 0.0).astype(BF16)
        unit = oq[(p + 1) % 3] * 4 + oq[(p + 2) % 3]
        meta[6:7, :] = ((unit * 2 + oc) * 4 + cell_ref[...] + 1).astype(F32)
        both = pick_meta(sel[p])
        extra = both[128:192] + pick_meta(selx[p])
        return jnp.where(lane128 == 7, over, both[0:128]).astype(BF16), extra.astype(BF16)

    def pick(which, value):
        return jnp.dot(which, value, preferred_element_type=F32)

    def pick_meta(which):
        return lax.dot_general(
            which,
            meta[...].astype(BF16),
            (((1,), (1,)), ((), ())),
            preferred_element_type=F32,
        )

    s1 = {}
    for n in range(UNITS):
        p, (half, first, width) = n % 3, PIECES[n // 3]
        if half == 0:
            flagged, extra = select(p)
        for k in range(2):
            b = 2 * p + k
            if half == 0:
                tin_copies[b].wait()

            def gather(c, carry, b=b, p=p, k=k, half=half, first=first):
                at = pl.ds(pl.multiple_of(c * 512 + first, 512), 512)
                there = pl.ds(pl.multiple_of(c * 512 + first + HALF, 512), 512)
                if half == 0:
                    both = pick(sel[p], tin[b, :, at])
                    send_lo[p, k, :, at] = both[0:128].astype(BF16)
                    send_x[p, k, :, at] = (
                        both[128:192] + pick(selx[p], tin[b, :, there])
                    ).astype(BF16)
                else:
                    send_hi[p, k, :, at] = pick(sel[p, 0:128], tin[b, :, there]).astype(BF16)
                return carry

            lax.fori_loop(0, width // 512, gather, 0)
            if half == 0:
                send_lo[p, k, :, HALF:WIDE] = flagged
                send_x[p, k, :, HALF:WIDE] = extra
        if n == 0:
            pl.semaphore_wait(barrier, len(peers))
        mine = q[p] * 2 + core
        streams = [(send_hi, recv_hi, 32, pl.ds(first, width), s1_send, s1_recv)]
        if half == 0:
            streams = [
                (send_lo, recv_lo, 32, pl.ds(0, WIDE), s1_send, s1_recv),
                (send_x, recv_x, 16, pl.ds(0, WIDE), x_send, x_recv),
            ]
        local, away = [], []
        for m, (step, flip) in enumerate(MEMBERS + ((0, 0),)):
            to = (q[p] + step) % 4
            parity = (core + flip) % 2
            for w, (src, dst, size, columns, sends, recvs) in enumerate(streams):
                from_ref = src.at[p, parity, pl.ds(pl.multiple_of(to * size, size), size), columns]
                to_ref = dst.at[p, pl.ds(pl.multiple_of(mine * size, size), size), columns]
                if (step, flip) == (0, 0):
                    copy = pltpu.make_async_copy(from_ref, to_ref, self_sem.at[n, w])
                    local.append(copy)
                else:
                    at = n if size == 32 else p
                    copy = pltpu.make_async_remote_copy(
                        src_ref=from_ref,
                        dst_ref=to_ref,
                        send_sem=sends.at[at, m],
                        recv_sem=recvs.at[at, m],
                        device_id=device(p, step, flip),
                        device_id_type=MESH,
                    )
                    away.append(copy)
                copy.start()
        s1[n] = (local, away)

    s2, s3, s4 = {}, {}, {}

    def pass_on(n, axis, size, words, extras, to_words, to_extras, send, recv):
        copies = []
        half, first, width = PIECES[n // 3]
        m, columns = 3 * half + n % 3, pl.ds(first // 2, width // 2)
        for step in (2, 1, 3):
            there = (q[axis] + step) % 4
            at = pl.ds(pl.multiple_of(there * size, size), size)
            pairs = (
                (words.at[m, at, columns], to_words.at[m, step - 1, :, columns]),
                (extras.at[n, at], to_extras.at[n, step - 1]),
            )
            for w, (from_ref, to_ref) in enumerate(pairs):
                copy = pltpu.make_async_remote_copy(
                    src_ref=from_ref,
                    dst_ref=to_ref,
                    send_sem=send.at[n, step - 1, w],
                    recv_sem=recv.at[n, step - 1, w],
                    device_id=device(axis, step, 0),
                    device_id_type=MESH,
                )
                copy.start()
                copies.append(copy)
        return copies

    weighted = {}

    def coefficients(p):
        m = recv_lo[p, :, HALF:WIDE].astype(F32).T
        mx = recv_x[p, :, HALF:WIDE].astype(F32).T
        w = jnp.where(core == 0, m[2 * p : 2 * p + 1], m[2 * p + 1 : 2 * p + 2])
        wx = jnp.where(core == 0, mx[2 * p : 2 * p + 1], mx[2 * p + 1 : 2 * p + 2])
        at = lax.broadcasted_iota(jnp.int32, (128, 256), 0).astype(F32) + 1.0
        c = jnp.where(m[6:7] == at, jnp.broadcast_to(w, (128, 256)), 0.0)
        cx = jnp.where(mx[6:7] == at[:, 0:128], jnp.broadcast_to(wx, (128, 128)), 0.0)
        low = (lane128 // 8) % 2 == 0
        x0, x1 = jnp.where(low, cx, 0.0), jnp.where(low, 0.0, cx)
        denom = jnp.sum(c, axis=1, keepdims=True) + jnp.sum(x0, axis=1, keepdims=True)
        flag = jnp.max(m[7:8], axis=1, keepdims=True)
        return c.astype(BF16), x0.astype(BF16), x1.astype(BF16), denom, flag

    def reduce_tiles(n):
        p, (half, first, width) = n % 3, PIECES[n // 3]
        m = 3 * half + p
        for copy in s1[n][0]:
            copy.wait()
        for copy in s1[n][1]:
            copy.wait_recv()
        if half == 0:
            weighted[p] = coefficients(p)
        c, x0, x1, denom, flag = weighted[p]
        src = recv_lo if half == 0 else recv_hi
        cx = x0 if half == 0 else x1

        def reduce(i, carry):
            at = pl.ds(pl.multiple_of(i * 512 + first, 512), 512)
            acc2[m, :, at] = pick(c, src[p, :, at]) + pick(cx, recv_x[p, :, at])
            return carry

        lax.fori_loop(0, width // 512, reduce, 0)
        words, extra = encode(acc2[m, :, first : first + width], denom, flag, 128)
        st2[m, :, first // 2 : (first + width) // 2] = words
        st2m[n] = extra
        s2[n] = pass_on(n, (p + 1) % 3, 32, st2, st2m, rcv2, rcv2m, s2_send, s2_recv)

    def second(n):
        p, (half, first, width) = n % 3, PIECES[n // 3]
        m, columns = 3 * half + p, slice(first // 2, (first + width) // 2)
        for copy in s2[n]:
            copy.wait_recv()
        at = pl.ds(pl.multiple_of(q[(p + 1) % 3] * 32, 32), 32)
        low, high, denom, flag = gathered(
            acc2[m, at, first : first + width],
            st2m[n, at, :],
            rcv2[m, :, :, columns],
            rcv2m[n],
        )
        middle = first + width // 2
        acc3[m, :, first:middle] = low
        acc3[m, :, middle : first + width] = high
        st3[m, :, columns], st3m[n] = encode(acc3[m, :, first : first + width], denom, flag, 32)
        s3[n] = pass_on(n, (p + 2) % 3, 8, st3, st3m, rcv3, rcv3m, s3_send, s3_recv)

    def third(n):
        p, (half, first, width) = n % 3, PIECES[n // 3]
        m, columns = 3 * half + p, slice(first // 2, (first + width) // 2)
        for copy in s3[n]:
            copy.wait_recv()
        at = pl.ds(pl.multiple_of(q[(p + 2) % 3] * 8, 8), 8)
        low, high, denom, flag = gathered(
            acc3[m, at, first : first + width],
            st3m[n, at, :],
            rcv3[m, :, :, columns],
            rcv3m[n],
        )
        if n < 3:
            flag = jnp.broadcast_to(flag, (8, 128))
            out_ref[1248:1256, :] = jnp.maximum(out_ref[1248:1256, :], flag) if n else flag
        scale = 1.0 / (1.0 + denom)
        lines = width // 128
        for j in range(lines // 2):
            c = slice(128 * j, 128 * j + 128)
            tbuf[n, pl.ds(j, 8, stride=lines), :] = low[:, c] * scale
            tbuf[n, pl.ds(j + lines // 2, 8, stride=lines), :] = high[:, c] * scale
        size = 4 * lines
        s4[n] = pltpu.make_async_remote_copy(
            src_ref=tbuf.at[n, pl.ds(pl.multiple_of((1 - core) * size, size), size)],
            dst_ref=rbuf.at[n, pl.ds(0, size)],
            send_sem=c_send.at[n],
            recv_sem=c_recv.at[n],
            device_id=device(0, 0, 1),
            device_id_type=MESH,
        )
        s4[n].start()

    halo = []

    def place(value, band, row):
        lines = value.shape[0] // 4
        left_half = lax.broadcasted_iota(jnp.int32, (lines, 128), 1) < 64
        for cy in range(2):
            r = 2 * cy * lines
            a, c = value[r : r + lines], value[r + lines : r + 2 * lines]
            y0 = band * 128 + 64 * cy + row
            out_ref[pl.ds(y0, lines, stride=2), :] = jnp.where(
                left_half, a, pltpu.roll(c, 64, 1)
            )
            out_ref[pl.ds(y0 + 1, lines, stride=2), :] = jnp.where(
                left_half, pltpu.roll(a, 64, 1), c
            )

    def fourth(n):
        p, (half, first, width) = n % 3, PIECES[n // 3]
        row, size = (half * HALF + first) // 64, width // 32
        place(tbuf[n, pl.ds(pl.multiple_of(core * size, size), size), :], 2 * p + core, row)
        s4[n].wait_recv()
        place(rbuf[n, 0:size, :], 2 * p + 1 - core, row)
        if n < UNITS - 3:
            return
        for b in (2 * p, 2 * p + 1):
            r = 128 * b
            hsend[0, b] = out_ref[r : r + 8, :]
            hsend[1, b] = out_ref[r + 120 : r + 128, :]
            turned = out_ref[r : r + 128, :].T
            hsend[2, b] = turned[0:8, :]
            hsend[3, b] = turned[120:128, :]
            out_ref[1152 + 8 * b : 1160 + 8 * b, :] = turned[0:8, :]
            out_ref[1200 + 8 * b : 1208 + 8 * b, :] = turned[120:128, :]
        bands = pl.ds(2 * p, 2)
        for m, (dy, dx) in enumerate(AROUND):
            which = 0 if dy < 0 else 1 if dy > 0 else 2 if dx < 0 else 3
            copy = pltpu.make_async_remote_copy(
                src_ref=hsend.at[which, bands],
                dst_ref=hrecv.at[m, bands],
                send_sem=h_send.at[p, m],
                recv_sem=h_recv.at[p, m],
                device_id=around(dy, dx),
                device_id_type=MESH,
            )
            copy.start()
            halo.append(copy)

    steps = (reduce_tiles, second, third, fourth)
    for n in range(UNITS + LAGS[3] + 1):
        for lag, step in zip(LAGS, steps):
            if 0 <= n - lag < UNITS:
                step(n - lag)

    for n in range(UNITS):
        for copy in s1[n][1] + s2[n] + s3[n] + [s4[n]]:
            copy.wait_send()
    for n, copy in enumerate(halo):
        copy.wait_recv()
        p, slot = n // 8, n % 8
        r = 768 + 48 * slot + 16 * p
        out_ref[r : r + 16, :] = hrecv[slot, 2 * p : 2 * p + 2].reshape(16, 128)
    for copy in halo:
        copy.wait_send()


def exchange(tiles, weights, owners, cells):
    vmem = pl.BlockSpec(memory_space=pltpu.VMEM)
    dma = pltpu.SemaphoreType.DMA
    return pl.pallas_call(
        exchange_kernel,
        out_shape=jax.ShapeDtypeStruct((1256, 128), F32),
        in_specs=[pl.BlockSpec(memory_space=pl.ANY), vmem, vmem, vmem],
        out_specs=vmem,
        scratch_shapes=[
            pltpu.VMEM((NB, 128, 4096), BF16),
            pltpu.VMEM((3, 192, 128), BF16),
            pltpu.VMEM((3, 64, 128), BF16),
            pltpu.VMEM((128, 128), F32),
            pltpu.VMEM((3, 2, 128, WIDE), BF16),
            pltpu.VMEM((3, 2, 128, HALF), BF16),
            pltpu.VMEM((3, 2, 64, WIDE), BF16),
            pltpu.VMEM((3, 256, WIDE), BF16),
            pltpu.VMEM((3, 256, HALF), BF16),
            pltpu.VMEM((3, 128, WIDE), BF16),
            pltpu.VMEM((NB, 128, HALF), F32),
            pltpu.VMEM((NB, 128, QUARTER), jnp.int32),
            pltpu.VMEM((UNITS, 128, 128), F32),
            pltpu.VMEM((NB, 3, 32, QUARTER), jnp.int32),
            pltpu.VMEM((UNITS, 3, 32, 128), F32),
            pltpu.VMEM((NB, 32, HALF), F32),
            pltpu.VMEM((NB, 32, QUARTER), jnp.int32),
            pltpu.VMEM((UNITS, 32, 128), F32),
            pltpu.VMEM((NB, 3, 8, QUARTER), jnp.int32),
            pltpu.VMEM((UNITS, 3, 8, 128), F32),
            pltpu.VMEM((UNITS, 128, 128), F32),
            pltpu.VMEM((UNITS, 64, 128), F32),
            pltpu.VMEM((4, NB, 8, 128), F32),
            pltpu.VMEM((8, NB, 8, 128), F32),
            dma((NB,)),
            dma((UNITS, 2)),
            dma((UNITS, 7)),
            dma((UNITS, 7)),
            dma((3, 7)),
            dma((3, 7)),
            dma((UNITS, 3, 2)),
            dma((UNITS, 3, 2)),
            dma((UNITS, 3, 2)),
            dma((UNITS, 3, 2)),
            dma((UNITS,)),
            dma((UNITS,)),
            dma((3, 8)),
            dma((3, 8)),
        ],
        compiler_params=pltpu.CompilerParams(
            collective_id=0, has_side_effects=True, vmem_limit_bytes=60 * 1024 * 1024
        ),
        name="tile_exchange",
    )(tiles, weights, owners, cells)


def full_exchange_kernel(
    tiles_hbm,
    wt_ref,
    own_ref,
    cell_ref,
    out_ref,
    tin,
    sel,
    meta,
    metar,
    send_a,
    send_b,
    recv_a,
    recv_b,
    acc2,
    st2,
    st2m,
    rcv2,
    rcv2m,
    acc3,
    st3,
    st3m,
    rcv3,
    rcv3m,
    tbuf,
    hsend,
    hrecv,
    tin_sem,
    self_sem,
    s1_send,
    s1_recv,
    s2_send,
    s2_recv,
    s3_send,
    s3_recv,
    h_send,
    h_recv,
):
    ix = lax.axis_index("skyx")
    iy = lax.axis_index("skyy")
    core = ix % 2
    q = (ix // 2, iy % 4, iy // 4)

    def device(axis, step, flip):
        r = list(q)
        if step:
            r[axis] = (r[axis] + step) % 4
        c = (core + flip) % 2 if flip else core
        return (r[0] * 2 + c, r[2] * 4 + r[1])

    def around(dy, dx):
        return ((ix + dx + 8) % 8, (iy + dy + 16) % 16)

    barrier = pltpu.get_barrier_semaphore()
    peers = [device(0, 0, 1)]
    for axis in range(3):
        for step, flip in MEMBERS[:6]:
            peers.append(device(axis, step, flip))
    for dy, dx in AROUND:
        peers.append(around(dy, dx))
    for peer in peers:
        pl.semaphore_signal(barrier, inc=1, device_id=peer, device_id_type=MESH)

    tin_copies = {}
    for b in ORDER:
        tin_copies[b] = pltpu.make_async_copy(tiles_hbm.at[b], tin.at[b], tin_sem.at[b])
        tin_copies[b].start()

    own = own_ref[...]
    ox, oy = own // 16, own % 16
    oq = (ox // 2, oy % 4, oy // 4)
    oc = ox % 2
    ownf = jnp.broadcast_to(own.astype(F32), (128, 128))
    same = ownf == ownf.T
    earlier = lax.broadcasted_iota(jnp.int32, (128, 128), 0) < lax.broadcasted_iota(
        jnp.int32, (128, 128), 1
    )
    rank = jnp.sum(jnp.where(same & earlier, 1.0, 0.0), axis=0, keepdims=True).astype(jnp.int32)
    rows = lax.broadcasted_iota(jnp.int32, (256, 128), 0)
    for p in range(3):
        slot = (oq[p] * 2 + oc) * 32 + (oq[(p + 1) % 3] * 4 + oq[(p + 2) % 3]) * 2 + rank
        sel[p] = jnp.where(rows == slot, 1.0, 0.0).astype(BF16)
    meta[...] = jnp.zeros((128, 128), F32)
    meta[0:6, :] = wt_ref[...].astype(F32)
    meta[6:7, :] = cell_ref[...].astype(F32) + 1.0

    s1 = {}

    def stage1_refs(b):
        p, k = b // 2, b % 2
        return (send_a.at[p], recv_a.at[p]) if k == 0 else (send_b.at[p], recv_b.at[p])

    for n, b in enumerate(ORDER):
        p, k = b // 2, b % 2
        src, dst = stage1_refs(b)
        tin_copies[b].wait()

        def gather(c, carry, b=b, p=p, src=src):
            at = pl.ds(pl.multiple_of(c * 512, 512), 512)
            src[:, at] = jnp.dot(sel[p], tin[b, :, at], preferred_element_type=F32).astype(BF16)
            return carry

        lax.fori_loop(0, 8, gather, 0)
        if k == 0:
            src[:, 4096:4224] = lax.dot_general(
                sel[p],
                meta[...].astype(BF16),
                (((1,), (1,)), ((), ())),
                preferred_element_type=F32,
            ).astype(BF16)
        if n == 0:
            pl.semaphore_wait(barrier, len(peers))
        mine = q[p] * 2 + core
        mine_rows = pl.ds(pl.multiple_of(mine * 32, 32), 32)
        own_copy = pltpu.make_async_copy(src.at[mine_rows], dst.at[mine_rows], self_sem.at[b])
        own_copy.start()
        copies = [own_copy]
        for m, (step, flip) in enumerate(MEMBERS):
            there = ((q[p] + step) % 4) * 2 + (core + flip) % 2
            copy = pltpu.make_async_remote_copy(
                src_ref=src.at[pl.ds(pl.multiple_of(there * 32, 32), 32)],
                dst_ref=dst.at[mine_rows],
                send_sem=s1_send.at[b, m],
                recv_sem=s1_recv.at[b, m],
                device_id=device(p, step, flip),
                device_id_type=MESH,
            )
            copy.start()
            copies.append(copy)
        s1[b] = copies

    s2, s3 = {}, {}

    def encode(values, denom, size):
        top = jnp.max(jnp.abs(values), axis=1, keepdims=True)
        some = top > 1e-30
        inverse = jnp.where(some, 32767.0 / jnp.where(some, top, 1.0), 0.0)
        codes = (values * inverse + 32768.5).astype(jnp.int32)
        words = codes[:, :QUARTER] | (codes[:, QUARTER:] << 16)
        lane = lax.broadcasted_iota(jnp.int32, (size, 128), 1)
        return words, jnp.where(lane < 64, denom, top * (1.0 / 32767.0))

    def decode(words, extra):
        step = extra[:, 64:65]
        low = (words & 65535).astype(F32) - 32768.0
        high = lax.shift_right_logical(words, jnp.full_like(words, 16)).astype(F32) - 32768.0
        return low * step, high * step

    def gathered(own, own_denom, words, extras):
        low, high, denom = own[:, :QUARTER], own[:, QUARTER:], own_denom
        for k in range(3):
            a, c = decode(words[k], extras[k])
            low, high, denom = low + a, high + c, denom + extras[k][:, 0:1]
        return low, high, denom

    def pass_on(b, axis, size, words, extras, to_words, to_extras, send, recv):
        copies = []
        for step in (2, 1, 3):
            there = (q[axis] + step) % 4
            at = pl.ds(pl.multiple_of(there * size, size), size)
            for n, (src, dst) in enumerate(((words, to_words), (extras, to_extras))):
                copy = pltpu.make_async_remote_copy(
                    src_ref=src.at[b, at],
                    dst_ref=dst.at[b, step - 1],
                    send_sem=send.at[b, step - 1, n],
                    recv_sem=recv.at[b, step - 1, n],
                    device_id=device(axis, step, 0),
                    device_id_type=MESH,
                )
                copy.start()
                copies.append(copy)
        return copies

    def reduce_tiles(b):
        p, k = b // 2, b % 2
        src, dst = stage1_refs(b)
        s1[b][0].wait()
        for copy in s1[b][1:]:
            copy.wait_recv()
        if k == 0:
            metar[p] = dst[:, 4096:4224].astype(F32).T[0:8, :]
        w = metar[p, b : b + 1, :]
        code = metar[p, 6:7, :].astype(jnp.int32)
        row = lax.broadcasted_iota(jnp.int32, (128, 256), 0)
        col = lax.broadcasted_iota(jnp.int32, (128, 256), 1)
        hit = ((col % 32) // 2 == row // 8) & (code == row % 4 + 1)
        upper = (row // 4) % 2 == 0
        both = jnp.where(hit, jnp.broadcast_to(w, (128, 256)), 0.0)
        c0 = jnp.where(upper, both, 0.0).astype(BF16)
        c1 = jnp.where(upper, 0.0, both).astype(BF16)
        denom = jnp.sum(both, axis=1, keepdims=True)

        def reduce(c, carry):
            lo = pl.ds(pl.multiple_of(c * 512, 512), 512)
            hi = pl.ds(pl.multiple_of(c * 512 + HALF, 512), 512)
            acc2[b, :, lo] = jnp.dot(c0, dst[:, lo], preferred_element_type=F32) + jnp.dot(
                c1, dst[:, hi], preferred_element_type=F32
            )
            return carry

        lax.fori_loop(0, 4, reduce, 0)
        st2[b], st2m[b] = encode(acc2[b], denom, 128)
        s2[b] = pass_on(b, (p + 1) % 3, 32, st2, st2m, rcv2, rcv2m, s2_send, s2_recv)

    def second(b):
        p = b // 2
        for copy in s2[b]:
            copy.wait_recv()
        at = pl.ds(pl.multiple_of(q[(p + 1) % 3] * 32, 32), 32)
        low, high, denom = gathered(acc2[b, at, :], st2m[b, at, 0:1], rcv2[b], rcv2m[b])
        acc3[b, :, :QUARTER] = low
        acc3[b, :, QUARTER:] = high
        st3[b], st3m[b] = encode(acc3[b], denom, 32)
        s3[b] = pass_on(b, (p + 2) % 3, 8, st3, st3m, rcv3, rcv3m, s3_send, s3_recv)

    left_half = lax.broadcasted_iota(jnp.int32, (16, 128), 1) < 64

    def third(b):
        p = b // 2
        axis = (p + 2) % 3
        for copy in s3[b]:
            copy.wait_recv()
        at = pl.ds(pl.multiple_of(q[axis] * 8, 8), 8)
        low, high, denom = gathered(acc3[b, at, :], st3m[b, at, 0:1], rcv3[b], rcv3m[b])
        scale = 1.0 / (1.0 + denom)
        for j in range(8):
            c = slice(128 * j, 128 * j + 128)
            tbuf[pl.ds(j, 8, stride=16), :] = low[:, c] * scale
            tbuf[pl.ds(j + 8, 8, stride=16), :] = high[:, c] * scale
        for h in range(2):
            for cy in range(2):
                s = h * 4 + cy * 2
                a = tbuf[16 * s : 16 * s + 16, :]
                c = tbuf[16 * s + 16 : 16 * s + 32, :]
                y0 = 64 * cy + 32 * h
                out_ref[pl.ds(128 * b + y0, 16, stride=2), :] = jnp.where(
                    left_half, a, pltpu.roll(c, 64, 1)
                )
                out_ref[pl.ds(128 * b + y0 + 1, 16, stride=2), :] = jnp.where(
                    left_half, pltpu.roll(a, 64, 1), c
                )
        r = 128 * b
        n = ORDER.index(b)
        hsend[0, n] = out_ref[r : r + 8, :]
        hsend[1, n] = out_ref[r + 120 : r + 128, :]
        turned = out_ref[r : r + 128, :].T
        hsend[2, n] = turned[0:8, :]
        hsend[3, n] = turned[120:128, :]
        out_ref[1152 + 8 * b : 1160 + 8 * b, :] = turned[0:8, :]
        out_ref[1200 + 8 * b : 1208 + 8 * b, :] = turned[120:128, :]

    halo = []

    def send_halo(group):
        bands = pl.ds(3 * group, 3)
        for n, (dy, dx) in enumerate(AROUND):
            which = 0 if dy < 0 else 1 if dy > 0 else 2 if dx < 0 else 3
            copy = pltpu.make_async_remote_copy(
                src_ref=hsend.at[which, bands],
                dst_ref=hrecv.at[n, bands],
                send_sem=h_send.at[group, n],
                recv_sem=h_recv.at[group, n],
                device_id=around(dy, dx),
                device_id_type=MESH,
            )
            copy.start()
            halo.append(copy)

    for n in range(6 + 4):
        if n < 6:
            reduce_tiles(ORDER[n])
        if 0 <= n - 2 < 6:
            second(ORDER[n - 2])
        if 0 <= n - 4 < 6:
            third(ORDER[n - 4])
            if n - 4 in (2, 5):
                send_halo((n - 4) // 3)

    for b in ORDER:
        for copy in s1[b][1:] + s2[b] + s3[b]:
            copy.wait_send()
    for n, copy in enumerate(halo):
        copy.wait_recv()
        group, slot = n // 8, n % 8
        for k in range(3):
            r = 768 + 48 * slot + 8 * ORDER[3 * group + k]
            out_ref[r : r + 8, :] = hrecv[slot, 3 * group + k]
    out_ref[1248:1256, :] = jnp.zeros((8, 128), F32)
    for copy in halo:
        copy.wait_send()


def full_exchange(tiles, weights, owners, cells):
    vmem = pl.BlockSpec(memory_space=pltpu.VMEM)
    dma = pltpu.SemaphoreType.DMA
    return pl.pallas_call(
        full_exchange_kernel,
        out_shape=jax.ShapeDtypeStruct((1256, 128), F32),
        in_specs=[pl.BlockSpec(memory_space=pl.ANY), vmem, vmem, vmem],
        out_specs=vmem,
        scratch_shapes=[
            pltpu.VMEM((NB, 128, 4096), BF16),
            pltpu.VMEM((3, 256, 128), BF16),
            pltpu.VMEM((128, 128), F32),
            pltpu.VMEM((3, 8, 256), F32),
            pltpu.VMEM((3, 256, 4224), BF16),
            pltpu.VMEM((3, 256, 4096), BF16),
            pltpu.VMEM((3, 256, 4224), BF16),
            pltpu.VMEM((3, 256, 4096), BF16),
            pltpu.VMEM((NB, 128, HALF), F32),
            pltpu.VMEM((NB, 128, QUARTER), jnp.int32),
            pltpu.VMEM((NB, 128, 128), F32),
            pltpu.VMEM((NB, 3, 32, QUARTER), jnp.int32),
            pltpu.VMEM((NB, 3, 32, 128), F32),
            pltpu.VMEM((NB, 32, HALF), F32),
            pltpu.VMEM((NB, 32, QUARTER), jnp.int32),
            pltpu.VMEM((NB, 32, 128), F32),
            pltpu.VMEM((NB, 3, 8, QUARTER), jnp.int32),
            pltpu.VMEM((NB, 3, 8, 128), F32),
            pltpu.VMEM((128, 128), F32),
            pltpu.VMEM((4, NB, 8, 128), F32),
            pltpu.VMEM((8, NB, 8, 128), F32),
            dma((NB,)),
            dma((NB,)),
            dma((NB, 7)),
            dma((NB, 7)),
            dma((NB, 3, 2)),
            dma((NB, 3, 2)),
            dma((NB, 3, 2)),
            dma((NB, 3, 2)),
            dma((2, 8)),
            dma((2, 8)),
        ],
        compiler_params=pltpu.CompilerParams(
            collective_id=1, has_side_effects=True, vmem_limit_bytes=60 * 1024 * 1024
        ),
        name="full_exchange",
    )(tiles, weights, owners, cells)


def detect_kernel(
    taps_ref,
    coadd_hbm,
    w1_ref,
    b1_ref,
    w2_ref,
    b2_ref,
    psf_hbm,
    det_hbm,
    coadd_ref,
    psf_out,
    det_out,
    partial,
    ext,
    shifted,
    sides,
    sides_t,
    psf,
    taps3,
    edge3,
    hidden,
    turned,
    small,
    w2s,
    sems,
):
    ix = lax.axis_index("skyx")
    iy = lax.axis_index("skyy")
    top, bottom = (iy > 0).astype(F32), (iy < 15).astype(F32)
    left, right = (ix > 0).astype(F32), (ix < 7).astype(F32)

    fetch = pltpu.make_async_copy(coadd_hbm, coadd_ref, sems.at[0])
    fetch.start()

    def halo(slot, b):
        r = 768 + slot * 48 + b * 8
        return coadd_ref[r : r + 8, :]

    def lanes_of(n):
        return lax.broadcasted_iota(jnp.int32, (n, 128), 1)

    small[...] = jnp.zeros((128, 128), F32)
    for b in range(NB):
        for i in range(3):
            small[pl.ds(i * 24 + b, 3, stride=8), 0:64] = w1_ref[b, i].astype(F32)
    w1 = (small[...].T[0:64, 0:72] * 0.5).astype(BF16)
    for j in range(3):
        for i in range(3):
            w2s[64 * j : 64 * j + 64, 64 * i : 64 * i + 64] = w2_ref[i, j]
    small[0:1, 0:64] = b1_ref[...] * 0.5
    small[1:2, 0:64] = b2_ref[...]
    columns = small[...].T
    bias1 = jnp.broadcast_to(columns[0:64, 0:1], (64, 256))
    bias2 = jnp.broadcast_to(columns[0:64, 1:2], (64, 128))

    taps3[...] = jnp.zeros_like(taps3)
    fetch.wait()

    pieces = []
    for b in range(NB):
        pieces += [
            halo(3, b)[2:8] * left,
            halo(8, b)[0:4],
            halo(9, b)[4:8],
            halo(2, b)[0:6] * right,
        ]
    pieces.append(jnp.zeros((8, 128), F32))
    sides[8:136, :] = jnp.concatenate(pieces, axis=0).T
    lane8 = lanes_of(8)
    for r, mid, at_left, at_right, keep in ((0, 1, 7, 6, top), (136, 0, 5, 4, bottom)):
        line = jnp.zeros((8, 128), F32)
        for b in range(NB):
            middle = halo(mid, b)
            parts = (
                (halo(at_left, b) * left, 122, 0, 6),
                (middle, 0, 6, 4),
                (middle, 124, 10, 4),
                (halo(at_right, b) * right, 0, 14, 6),
            )
            for value, start, at, size in parts:
                at = 20 * b + at
                moved = pltpu.roll(value, (at - start) % 128, 1)
                line = jnp.where((lane8 >= at) & (lane8 < at + size), moved, line)
        sides[r : r + 8, :] = line * keep

    for j in range(9):
        shifted[j] = pltpu.roll(sides[...], (-j) % 128, 1) if j else sides[...]
    owner_band = lane8 // 20

    def edge_block(start, size):
        acc = jnp.zeros((size, 128), F32)
        for i in range(9):
            for j in range(9):
                tap = jnp.full((8, 128), taps_ref[i, 0, j], F32)
                for b in range(1, NB):
                    tap = jnp.where(owner_band == b, taps_ref[i, b, j], tap)
                tap = jnp.broadcast_to(tap[0:1], (size, 128))
                acc = acc + tap * shifted[j, start + i : start + i + size, :]
        at = lax.broadcasted_iota(jnp.int32, (size, 128), 0) + start
        keep = jnp.where(at < 4, top, jnp.where(at >= 132, bottom, 1.0))
        keep = keep * jnp.where(lanes_of(size) % 20 < 10, left, right)
        return acc.astype(BF16).astype(F32) * keep

    sides[0:136, :] = edge_block(0, 136)

    for b in range(NB):
        ext[b, 8:136, :] = coadd_ref[128 * b : 128 * b + 128, :]
        ext[b, 0:8, :] = halo(1, b) * top
        ext[b, 136:144, :] = halo(0, b) * bottom
    column = lanes_of(144)

    def band(b, carry):
        near_left = pltpu.roll(shifted[0], 122 - 20 * b, 1)
        near_right = pltpu.roll(shifted[0], 114 - 20 * b, 1)
        x = ext[b]
        for j in range(9):
            if j < 4:
                moved = pltpu.roll(jnp.where(column >= 124 + j, near_left, x), 4 - j, 1)
            elif j == 4:
                moved = x
            else:
                moved = pltpu.roll(jnp.where(column < j - 4, near_right, x), 132 - j, 1)
            shifted[j + 1] = moved

        for n in range(6):
            at_rows = slice(24 * n, 24 * n + 24)
            sums = [None] * 9
            for j in range(9):
                value = shifted[j + 1, at_rows, :]
                for i in range(9):
                    term = taps_ref[i, b, j] * value
                    sums[i] = term if j == 0 else sums[i] + term
            for i in range(9):
                partial[i, at_rows, :] = sums[i]

        def block(start, size):
            acc = partial[0, start : start + size, :]
            for i in range(1, 9):
                acc = acc + partial[i, start + i : start + i + size, :]
            at = lax.broadcasted_iota(jnp.int32, (size, 128), 0) + start
            keep = jnp.where(at < 4, top, jnp.where(at >= 132, bottom, 1.0))
            v = acc.astype(BF16).astype(F32) * keep
            psf[start : start + size, :] = v
            lane = lanes_of(size)
            edge = sides[start : start + size, :]
            before = jnp.where(lane == 0, pltpu.roll(edge, 127 - 20 * b, 1), pltpu.roll(v, 1, 1))
            after = jnp.where(
                lane == 127, pltpu.roll(edge, 117 - 20 * b, 1), pltpu.roll(v, 127, 1)
            )
            for j, value in enumerate((before, v, after)):
                taps3[pl.ds(start * 24 + 8 * j + b, size, stride=24), :] = value
            edge = jnp.where(lane == 20 * b + 2, pltpu.roll(v, 20 * b + 2, 1), edge)
            edge = jnp.where(lane == 20 * b + 9, pltpu.roll(v, 20 * b + 10, 1), edge)
            sides[start : start + size, :] = edge

        block(0, 72)
        block(72, 64)
        psf_out[b] = psf[4:132, :].astype(BF16)
        return carry

    lax.fori_loop(0, NB, band, 0)

    psf_copy = pltpu.make_async_copy(psf_out, psf_hbm, sems.at[1])
    psf_copy.start()

    def silu(u):
        return u + u * jnp.tanh(u)

    def first(n, carry):
        at0 = pl.ds(pl.multiple_of((2 * n + 2) * 24, 8), 72)
        at1 = pl.ds(pl.multiple_of((2 * n + 3) * 24, 8), 72)
        rhs = jnp.concatenate([taps3[at0, :], taps3[at1, :]], axis=1).astype(BF16)
        v = silu(jnp.dot(w1, rhs, preferred_element_type=F32) + bias1)
        hidden[2 * n] = v[:, 0:128].astype(BF16)
        hidden[2 * n + 1] = v[:, 128:256].astype(BF16)
        return carry

    lax.fori_loop(0, 65, first, 0, unroll=5)
    hidden[0] = (hidden[0].astype(F32) * top).astype(BF16)
    hidden[129] = (hidden[129].astype(F32) * bottom).astype(BF16)

    sides_t[0] = sides[0:128, :].T
    tail = jnp.concatenate([sides[128:136, :], jnp.zeros((120, 128), F32)], axis=0)
    sides_t[1] = tail.T
    edge3[...] = jnp.zeros_like(edge3)
    at256 = lax.broadcasted_iota(jnp.int32, (64, 256), 1)
    ends = jnp.where(at256 == 0, top, jnp.where(at256 == 129, bottom, 1.0))
    beside = []
    for side, (offset, keep) in enumerate(((0, left), (9, right))):
        for t in range(2):
            for j in range(3):
                edge3[side, 8 * j : 8 * j + 6, 128 * t : 128 * t + 128] = sides_t[
                    t, pl.ds(offset + j, 6, stride=20), :
                ]
        x = edge3[side]
        rhs = jnp.concatenate([pltpu.roll(x, 256 - (2 + i), 1) for i in range(3)], axis=0)
        v = silu(jnp.dot(w1, rhs.astype(BF16), preferred_element_type=F32) + bias1)
        v = (v * (ends * keep)).astype(BF16).astype(F32)
        rhs = jnp.concatenate(
            [v[:, 0:128]] + [pltpu.roll(v, 256 - i, 1)[:, 0:128] for i in (1, 2)], axis=0
        )
        weight = w2s[0:64, :] if side == 0 else w2s[128:192, :]
        beside.append(jnp.dot(weight, rhs.astype(BF16), preferred_element_type=F32))
    small[0:64, :] = beside[0]
    small[64:128, :] = beside[1]

    w2 = w2s[...]
    lane64 = lanes_of(64)

    def leave(g):
        at = pl.ds(pl.multiple_of(g * 16, 16), 16)
        return pltpu.make_async_copy(det_out.at[g], det_hbm.at[:, at], sems.at[2 + g])

    def group(g, carry):
        def rows(n, inner):
            y = g * 16 + 2 * n
            rhs = jnp.concatenate(
                [hidden[pl.ds(y, 3)].reshape(192, 128), hidden[pl.ds(y + 1, 3)].reshape(192, 128)],
                axis=1,
            )
            z = jnp.dot(w2, rhs, preferred_element_type=F32)
            for k in range(2):
                c = slice(128 * k, 128 * k + 128)
                near = pltpu.roll(small[0:64, :], 128 - (y + k), 1)
                far = pltpu.roll(small[64:128, :], 127 - (y + k), 1)
                before = jnp.where(lane64 == 0, near, pltpu.roll(z[0:64, c], 1, 1))
                after = jnp.where(lane64 == 127, far, pltpu.roll(z[128:192, c], 127, 1))
                turned[pl.ds(2 * n + k, 64, stride=16), :] = (before + z[64:128, c]) + (
                    after + bias2
                )
            return inner

        lax.fori_loop(0, 8, rows, 0, unroll=8)
        det_out[g] = turned[...].reshape(64, 16, 128).astype(BF16)
        leave(g).start()
        return carry

    lax.fori_loop(0, 8, group, 0)
    psf_copy.wait()
    for g in range(8):
        leave(g).wait()


def detect(taps, coadd, w1, b1, w2, b2):
    vmem = pl.BlockSpec(memory_space=pltpu.VMEM)
    anywhere = pl.BlockSpec(memory_space=pl.ANY)
    return pl.pallas_call(
        detect_kernel,
        out_shape=(
            jax.ShapeDtypeStruct((NB, 128, 128), BF16),
            jax.ShapeDtypeStruct((64, 128, 128), BF16),
        ),
        in_specs=[pl.BlockSpec(memory_space=pltpu.SMEM), anywhere] + [vmem] * 4,
        out_specs=(anywhere, anywhere),
        scratch_shapes=[
            pltpu.VMEM((1256, 128), F32),
            pltpu.VMEM((NB, 128, 128), BF16),
            pltpu.VMEM((8, 64, 16, 128), BF16),
            pltpu.VMEM((9, 144, 128), F32),
            pltpu.VMEM((NB, 144, 128), F32),
            pltpu.VMEM((10, 144, 128), F32),
            pltpu.VMEM((144, 128), F32),
            pltpu.VMEM((2, 128, 128), F32),
            pltpu.VMEM((136, 128), F32),
            pltpu.VMEM((136 * 24, 128), F32),
            pltpu.VMEM((2, 24, 256), F32),
            pltpu.VMEM((130, 64, 128), BF16),
            pltpu.VMEM((64 * 16, 128), F32),
            pltpu.VMEM((128, 128), F32),
            pltpu.VMEM((192, 192), BF16),
            pltpu.SemaphoreType.DMA((10,)),
        ],
        compiler_params=pltpu.CompilerParams(vmem_limit_bytes=48 * 1024 * 1024),
        name="detect",
    )(taps, coadd, w1, b1, w2, b2)


def body(
    tiles,
    tile_weight,
    owners,
    cells,
    psf_kernel,
    conv1_weight,
    conv1_bias,
    conv2_weight,
    conv2_bias,
):
    operands = (
        tiles.transpose(1, 0, 2),
        tile_weight.transpose(1, 0),
        owners.reshape(1, 128),
        cells.reshape(1, 128),
    )
    coadd = exchange(*operands)
    coadd = lax.cond(coadd[1248, 0] > 0.5, lambda: full_exchange(*operands), lambda: coadd)
    return detect(
        psf_kernel.transpose(1, 0, 2),
        coadd,
        conv1_weight.transpose(1, 2, 3, 0),
        conv1_bias.reshape(1, 64),
        conv2_weight.transpose(2, 3, 0, 1),
        conv2_bias.reshape(1, 64),
    )


def solution(mesh):
    in_specs = (
        P(("skyx", "skyy"), None, None),
        P(("skyx", "skyy"), None),
        P(("skyx", "skyy"), None),
        P(("skyx", "skyy")),
        P(),
        P(),
        P(),
        P(),
        P(),
    )
    out_specs = (P(None, "skyy", "skyx"), P(None, "skyy", "skyx"))
    return jax.shard_map(body, mesh=mesh, in_specs=in_specs, out_specs=out_specs, check_vma=False)
```

```python
import functools

import jax
import jax.numpy as jnp
from jax import lax
from jax.experimental import pallas as pl
from jax.experimental.pallas import tpu as pltpu
from jax.sharding import PartitionSpec as P

MESH = pl.DeviceIdType.MESH
F32 = jnp.float32
BF16 = jnp.bfloat16

NB = 6
HALF = 2048
QUARTER = 1024
WIDE = HALF + 128
PIECES = ((0, 0, 2048), (1, 0, 2048))
UNITS = 3 * len(PIECES)
LAGS = (0, 2, 4, 5)
ORDER = (0, 2, 4, 1, 3, 5)
MEMBERS = ((2, 0), (2, 1), (1, 0), (3, 0), (1, 1), (3, 1), (0, 1))
AROUND = ((-1, 0), (1, 0), (0, -1), (0, 1), (-1, -1), (-1, 1), (1, -1), (1, 1))


def encode(values, denom, flag, size):
    top = jnp.max(jnp.abs(values), axis=1, keepdims=True)
    some = top > 1e-30
    inverse = jnp.where(some, 32767.0 / jnp.where(some, top, 1.0), 0.0)
    codes = (values * inverse + 32768.5).astype(jnp.int32)
    middle = values.shape[1] // 2
    words = codes[:, :middle] | (codes[:, middle:] << 16)
    lane = lax.broadcasted_iota(jnp.int32, (size, 128), 1)
    extra = jnp.where(lane < 64, denom, top * (1.0 / 32767.0))
    return words, jnp.where(lane == 127, flag, extra)


def decode(words, extra):
    step = extra[:, 64:65]
    low = (words & 65535).astype(F32) - 32768.0
    high = lax.shift_right_logical(words, jnp.full_like(words, 16)).astype(F32) - 32768.0
    return low * step, high * step


def gathered(own, own_extra, words, extras):
    middle = own.shape[1] // 2
    low, high = own[:, :middle], own[:, middle:]
    denom, flag = own_extra[:, 0:1], own_extra[:, 127:128]
    for k in range(3):
        a, c = decode(words[k], extras[k])
        low, high, denom = low + a, high + c, denom + extras[k][:, 0:1]
        flag = jnp.maximum(flag, extras[k][:, 127:128])
    return low, high, denom, jnp.max(flag, axis=0, keepdims=True)


def exchange_kernel(
    tiles_hbm,
    wt_ref,
    own_ref,
    cell_ref,
    out_ref,
    tin,
    sel,
    selx,
    meta,
    send_lo,
    send_hi,
    send_x,
    recv_lo,
    recv_hi,
    recv_x,
    acc2,
    st2,
    st2m,
    rcv2,
    rcv2m,
    acc3,
    st3,
    st3m,
    rcv3,
    rcv3m,
    tbuf,
    rbuf,
    hsend,
    hrecv,
    tin_sem,
    self_sem,
    s1_send,
    s1_recv,
    x_send,
    x_recv,
    s2_send,
    s2_recv,
    s3_send,
    s3_recv,
    c_send,
    c_recv,
    h_send,
    h_recv,
):
    ix = lax.axis_index("skyx")
    iy = lax.axis_index("skyy")
    core = ix % 2
    q = (ix // 2, iy % 4, iy // 4)

    def device(axis, step, flip):
        r = list(q)
        if step:
            r[axis] = (r[axis] + step) % 4
        c = (core + flip) % 2 if flip else core
        return (r[0] * 2 + c, r[2] * 4 + r[1])

    def around(dy, dx):
        return ((ix + dx + 8) % 8, (iy + dy + 16) % 16)

    barrier = pltpu.get_barrier_semaphore()
    peers = [device(0, 0, 1)]
    for axis in range(3):
        for step, flip in MEMBERS[:6]:
            peers.append(device(axis, step, flip))
    for dy, dx in AROUND:
        peers.append(around(dy, dx))
    for peer in peers:
        pl.semaphore_signal(barrier, inc=1, device_id=peer, device_id_type=MESH)

    tin_copies = []
    for b in range(NB):
        tin_copies.append(pltpu.make_async_copy(tiles_hbm.at[b], tin.at[b], tin_sem.at[b]))
        tin_copies[b].start()

    own = own_ref[...]
    ox, oy = own // 16, own % 16
    oq = (ox // 2, oy % 4, oy // 4)
    oc = ox % 2
    earlier = lax.broadcasted_iota(jnp.int32, (128, 128), 0) < lax.broadcasted_iota(
        jnp.int32, (128, 128), 1
    )
    rows = lax.broadcasted_iota(jnp.int32, (128, 128), 0)
    rows_x = lax.broadcasted_iota(jnp.int32, (64, 128), 0)
    lane128 = lax.broadcasted_iota(jnp.int32, (128, 128), 1)
    meta[...] = jnp.zeros((128, 128), F32)
    meta[0:6, :] = wt_ref[...].astype(F32)

    def select(p):
        group = jnp.broadcast_to(oq[p].astype(F32), (128, 128))
        rank = jnp.sum(
            jnp.where((group == group.T) & earlier, 1.0, 0.0), axis=0, keepdims=True
        )
        over = jnp.where(jnp.max(rank, axis=1, keepdims=True) > 39.5, 1.0, 0.0)
        rank = rank.astype(jnp.int32)
        slot = jnp.where(rank < 32, oq[p] * 32 + rank, -1)
        sel[p, 0:128] = jnp.where(rows == slot, 1.0, 0.0).astype(BF16)
        slot = jnp.where((rank >= 32) & (rank < 40), oq[p] * 16 + rank - 32, -64)
        sel[p, 128:192] = jnp.where(rows_x == slot, 1.0, 0.0).astype(BF16)
        selx[p] = jnp.where(rows_x == slot + 8, 1.0, 0.0).astype(BF16)
        unit = oq[(p + 1) % 3] * 4 + oq[(p + 2) % 3]
        meta[6:7, :] = ((unit * 2 + oc) * 4 + cell_ref[...] + 1).astype(F32)
        both = pick_meta(sel[p])
        extra = both[128:192] + pick_meta(selx[p])
        return jnp.where(lane128 == 7, over, both[0:128]).astype(BF16), extra.astype(BF16)

    def pick(which, value):
        return jnp.dot(which, value, preferred_element_type=F32)

    def pick_meta(which):
        return lax.dot_general(
            which,
            meta[...].astype(BF16),
            (((1,), (1,)), ((), ())),
            preferred_element_type=F32,
        )

    s1 = {}
    for n in range(UNITS):
        p, (half, first, width) = n % 3, PIECES[n // 3]
        if half == 0:
            flagged, extra = select(p)
        for k in range(2):
            b = 2 * p + k
            if half == 0:
                tin_copies[b].wait()

            def gather(c, carry, b=b, p=p, k=k, half=half, first=first):
                at = pl.ds(pl.multiple_of(c * 512 + first, 512), 512)
                there = pl.ds(pl.multiple_of(c * 512 + first + HALF, 512), 512)
                if half == 0:
                    both = pick(sel[p], tin[b, :, at])
                    send_lo[p, k, :, at] = both[0:128].astype(BF16)
                    send_x[p, k, :, at] = (
                        both[128:192] + pick(selx[p], tin[b, :, there])
                    ).astype(BF16)
                else:
                    send_hi[p, k, :, at] = pick(sel[p, 0:128], tin[b, :, there]).astype(BF16)
                return carry

            lax.fori_loop(0, width // 512, gather, 0)
            if half == 0:
                send_lo[p, k, :, HALF:WIDE] = flagged
                send_x[p, k, :, HALF:WIDE] = extra
        if n == 0:
            pl.semaphore_wait(barrier, len(peers))
        mine = q[p] * 2 + core
        streams = [(send_hi, recv_hi, 32, pl.ds(first, width), s1_send, s1_recv)]
        if half == 0:
            streams = [
                (send_lo, recv_lo, 32, pl.ds(0, WIDE), s1_send, s1_recv),
                (send_x, recv_x, 16, pl.ds(0, WIDE), x_send, x_recv),
            ]
        local, away = [], []
        for m, (step, flip) in enumerate(MEMBERS + ((0, 0),)):
            to = (q[p] + step) % 4
            parity = (core + flip) % 2
            for w, (src, dst, size, columns, sends, recvs) in enumerate(streams):
                from_ref = src.at[p, parity, pl.ds(pl.multiple_of(to * size, size), size), columns]
                to_ref = dst.at[p, pl.ds(pl.multiple_of(mine * size, size), size), columns]
                if (step, flip) == (0, 0):
                    copy = pltpu.make_async_copy(from_ref, to_ref, self_sem.at[n, w])
                    local.append(copy)
                else:
                    at = n if size == 32 else p
                    copy = pltpu.make_async_remote_copy(
                        src_ref=from_ref,
                        dst_ref=to_ref,
                        send_sem=sends.at[at, m],
                        recv_sem=recvs.at[at, m],
                        device_id=device(p, step, flip),
                        device_id_type=MESH,
                    )
                    away.append(copy)
                copy.start()
        s1[n] = (local, away)

    s2, s3, s4 = {}, {}, {}

    def pass_on(n, axis, size, words, extras, to_words, to_extras, send, recv):
        copies = []
        half, first, width = PIECES[n // 3]
        m, columns = 3 * half + n % 3, pl.ds(first // 2, width // 2)
        for step in (2, 1, 3):
            there = (q[axis] + step) % 4
            at = pl.ds(pl.multiple_of(there * size, size), size)
            pairs = (
                (words.at[m, at, columns], to_words.at[m, step - 1, :, columns]),
                (extras.at[n, at], to_extras.at[n, step - 1]),
            )
            for w, (from_ref, to_ref) in enumerate(pairs):
                copy = pltpu.make_async_remote_copy(
                    src_ref=from_ref,
                    dst_ref=to_ref,
                    send_sem=send.at[n, step - 1, w],
                    recv_sem=recv.at[n, step - 1, w],
                    device_id=device(axis, step, 0),
                    device_id_type=MESH,
                )
                copy.start()
                copies.append(copy)
        return copies

    weighted = {}

    def coefficients(p):
        m = recv_lo[p, :, HALF:WIDE].astype(F32).T
        mx = recv_x[p, :, HALF:WIDE].astype(F32).T
        w = jnp.where(core == 0, m[2 * p : 2 * p + 1], m[2 * p + 1 : 2 * p + 2])
        wx = jnp.where(core == 0, mx[2 * p : 2 * p + 1], mx[2 * p + 1 : 2 * p + 2])
        at = lax.broadcasted_iota(jnp.int32, (128, 256), 0).astype(F32) + 1.0
        c = jnp.where(m[6:7] == at, jnp.broadcast_to(w, (128, 256)), 0.0)
        cx = jnp.where(mx[6:7] == at[:, 0:128], jnp.broadcast_to(wx, (128, 128)), 0.0)
        low = (lane128 // 8) % 2 == 0
        x0, x1 = jnp.where(low, cx, 0.0), jnp.where(low, 0.0, cx)
        denom = jnp.sum(c, axis=1, keepdims=True) + jnp.sum(x0, axis=1, keepdims=True)
        flag = jnp.max(m[7:8], axis=1, keepdims=True)
        return c.astype(BF16), x0.astype(BF16), x1.astype(BF16), denom, flag

    def reduce_tiles(n):
        p, (half, first, width) = n % 3, PIECES[n // 3]
        m = 3 * half + p
        for copy in s1[n][0]:
            copy.wait()
        for copy in s1[n][1]:
            copy.wait_recv()
        if half == 0:
            weighted[p] = coefficients(p)
        c, x0, x1, denom, flag = weighted[p]
        src = recv_lo if half == 0 else recv_hi
        cx = x0 if half == 0 else x1

        def reduce(i, carry):
            at = pl.ds(pl.multiple_of(i * 512 + first, 512), 512)
            acc2[m, :, at] = pick(c, src[p, :, at]) + pick(cx, recv_x[p, :, at])
            return carry

        lax.fori_loop(0, width // 512, reduce, 0)
        words, extra = encode(acc2[m, :, first : first + width], denom, flag, 128)
        st2[m, :, first // 2 : (first + width) // 2] = words
        st2m[n] = extra
        s2[n] = pass_on(n, (p + 1) % 3, 32, st2, st2m, rcv2, rcv2m, s2_send, s2_recv)

    def second(n):
        p, (half, first, width) = n % 3, PIECES[n // 3]
        m, columns = 3 * half + p, slice(first // 2, (first + width) // 2)
        for copy in s2[n]:
            copy.wait_recv()
        at = pl.ds(pl.multiple_of(q[(p + 1) % 3] * 32, 32), 32)
        low, high, denom, flag = gathered(
            acc2[m, at, first : first + width],
            st2m[n, at, :],
            rcv2[m, :, :, columns],
            rcv2m[n],
        )
        middle = first + width // 2
        acc3[m, :, first:middle] = low
        acc3[m, :, middle : first + width] = high
        st3[m, :, columns], st3m[n] = encode(acc3[m, :, first : first + width], denom, flag, 32)
        s3[n] = pass_on(n, (p + 2) % 3, 8, st3, st3m, rcv3, rcv3m, s3_send, s3_recv)

    def third(n):
        p, (half, first, width) = n % 3, PIECES[n // 3]
        m, columns = 3 * half + p, slice(first // 2, (first + width) // 2)
        for copy in s3[n]:
            copy.wait_recv()
        at = pl.ds(pl.multiple_of(q[(p + 2) % 3] * 8, 8), 8)
        low, high, denom, flag = gathered(
            acc3[m, at, first : first + width],
            st3m[n, at, :],
            rcv3[m, :, :, columns],
            rcv3m[n],
        )
        if n < 3:
            flag = jnp.broadcast_to(flag, (8, 128))
            out_ref[1248:1256, :] = jnp.maximum(out_ref[1248:1256, :], flag) if n else flag
        scale = 1.0 / (1.0 + denom)
        lines = width // 128
        for j in range(lines // 2):
            c = slice(128 * j, 128 * j + 128)
            tbuf[n, pl.ds(j, 8, stride=lines), :] = low[:, c] * scale
            tbuf[n, pl.ds(j + lines // 2, 8, stride=lines), :] = high[:, c] * scale
        size = 4 * lines
        s4[n] = pltpu.make_async_remote_copy(
            src_ref=tbuf.at[n, pl.ds(pl.multiple_of((1 - core) * size, size), size)],
            dst_ref=rbuf.at[n, pl.ds(0, size)],
            send_sem=c_send.at[n],
            recv_sem=c_recv.at[n],
            device_id=device(0, 0, 1),
            device_id_type=MESH,
        )
        s4[n].start()

    halo = []

    def place(value, band, row):
        lines = value.shape[0] // 4
        left_half = lax.broadcasted_iota(jnp.int32, (lines, 128), 1) < 64
        for cy in range(2):
            r = 2 * cy * lines
            a, c = value[r : r + lines], value[r + lines : r + 2 * lines]
            y0 = band * 128 + 64 * cy + row
            out_ref[pl.ds(y0, lines, stride=2), :] = jnp.where(
                left_half, a, pltpu.roll(c, 64, 1)
            )
            out_ref[pl.ds(y0 + 1, lines, stride=2), :] = jnp.where(
                left_half, pltpu.roll(a, 64, 1), c
            )

    def fourth(n):
        p, (half, first, width) = n % 3, PIECES[n // 3]
        row, size = (half * HALF + first) // 64, width // 32
        place(tbuf[n, pl.ds(pl.multiple_of(core * size, size), size), :], 2 * p + core, row)
        s4[n].wait_recv()
        place(rbuf[n, 0:size, :], 2 * p + 1 - core, row)
        if n < UNITS - 3:
            return
        for b in (2 * p, 2 * p + 1):
            r = 128 * b
            hsend[0, b] = out_ref[r : r + 8, :]
            hsend[1, b] = out_ref[r + 120 : r + 128, :]
            turned = out_ref[r : r + 128, :].T
            hsend[2, b] = turned[0:8, :]
            hsend[3, b] = turned[120:128, :]
            out_ref[1152 + 8 * b : 1160 + 8 * b, :] = turned[0:8, :]
            out_ref[1200 + 8 * b : 1208 + 8 * b, :] = turned[120:128, :]
        bands = pl.ds(2 * p, 2)
        for m, (dy, dx) in enumerate(AROUND):
            which = 0 if dy < 0 else 1 if dy > 0 else 2 if dx < 0 else 3
            copy = pltpu.make_async_remote_copy(
                src_ref=hsend.at[which, bands],
                dst_ref=hrecv.at[m, bands],
                send_sem=h_send.at[p, m],
                recv_sem=h_recv.at[p, m],
                device_id=around(dy, dx),
                device_id_type=MESH,
            )
            copy.start()
            halo.append(copy)

    steps = (reduce_tiles, second, third, fourth)
    for n in range(UNITS + LAGS[3] + 1):
        for lag, step in zip(LAGS, steps):
            if 0 <= n - lag < UNITS:
                step(n - lag)

    for n in range(UNITS):
        for copy in s1[n][1] + s2[n] + s3[n] + [s4[n]]:
            copy.wait_send()
    for n, copy in enumerate(halo):
        copy.wait_recv()
        p, slot = n // 8, n % 8
        r = 768 + 48 * slot + 16 * p
        out_ref[r : r + 16, :] = hrecv[slot, 2 * p : 2 * p + 2].reshape(16, 128)
    for copy in halo:
        copy.wait_send()


def exchange(tiles, weights, owners, cells):
    vmem = pl.BlockSpec(memory_space=pltpu.VMEM)
    dma = pltpu.SemaphoreType.DMA
    return pl.pallas_call(
        exchange_kernel,
        out_shape=jax.ShapeDtypeStruct((1256, 128), F32),
        in_specs=[pl.BlockSpec(memory_space=pl.ANY), vmem, vmem, vmem],
        out_specs=vmem,
        scratch_shapes=[
            pltpu.VMEM((NB, 128, 4096), BF16),
            pltpu.VMEM((3, 192, 128), BF16),
            pltpu.VMEM((3, 64, 128), BF16),
            pltpu.VMEM((128, 128), F32),
            pltpu.VMEM((3, 2, 128, WIDE), BF16),
            pltpu.VMEM((3, 2, 128, HALF), BF16),
            pltpu.VMEM((3, 2, 64, WIDE), BF16),
            pltpu.VMEM((3, 256, WIDE), BF16),
            pltpu.VMEM((3, 256, HALF), BF16),
            pltpu.VMEM((3, 128, WIDE), BF16),
            pltpu.VMEM((NB, 128, HALF), F32),
            pltpu.VMEM((NB, 128, QUARTER), jnp.int32),
            pltpu.VMEM((UNITS, 128, 128), F32),
            pltpu.VMEM((NB, 3, 32, QUARTER), jnp.int32),
            pltpu.VMEM((UNITS, 3, 32, 128), F32),
            pltpu.VMEM((NB, 32, HALF), F32),
            pltpu.VMEM((NB, 32, QUARTER), jnp.int32),
            pltpu.VMEM((UNITS, 32, 128), F32),
            pltpu.VMEM((NB, 3, 8, QUARTER), jnp.int32),
            pltpu.VMEM((UNITS, 3, 8, 128), F32),
            pltpu.VMEM((UNITS, 128, 128), F32),
            pltpu.VMEM((UNITS, 64, 128), F32),
            pltpu.VMEM((4, NB, 8, 128), F32),
            pltpu.VMEM((8, NB, 8, 128), F32),
            dma((NB,)),
            dma((UNITS, 2)),
            dma((UNITS, 7)),
            dma((UNITS, 7)),
            dma((3, 7)),
            dma((3, 7)),
            dma((UNITS, 3, 2)),
            dma((UNITS, 3, 2)),
            dma((UNITS, 3, 2)),
            dma((UNITS, 3, 2)),
            dma((UNITS,)),
            dma((UNITS,)),
            dma((3, 8)),
            dma((3, 8)),
        ],
        compiler_params=pltpu.CompilerParams(
            collective_id=0, has_side_effects=True, vmem_limit_bytes=60 * 1024 * 1024
        ),
        name="tile_exchange",
    )(tiles, weights, owners, cells)


def full_exchange_kernel(
    tiles_hbm,
    wt_ref,
    own_ref,
    cell_ref,
    out_ref,
    tin,
    sel,
    meta,
    metar,
    send_a,
    send_b,
    recv_a,
    recv_b,
    acc2,
    st2,
    st2m,
    rcv2,
    rcv2m,
    acc3,
    st3,
    st3m,
    rcv3,
    rcv3m,
    tbuf,
    hsend,
    hrecv,
    tin_sem,
    self_sem,
    s1_send,
    s1_recv,
    s2_send,
    s2_recv,
    s3_send,
    s3_recv,
    h_send,
    h_recv,
):
    ix = lax.axis_index("skyx")
    iy = lax.axis_index("skyy")
    core = ix % 2
    q = (ix // 2, iy % 4, iy // 4)

    def device(axis, step, flip):
        r = list(q)
        if step:
            r[axis] = (r[axis] + step) % 4
        c = (core + flip) % 2 if flip else core
        return (r[0] * 2 + c, r[2] * 4 + r[1])

    def around(dy, dx):
        return ((ix + dx + 8) % 8, (iy + dy + 16) % 16)

    barrier = pltpu.get_barrier_semaphore()
    peers = [device(0, 0, 1)]
    for axis in range(3):
        for step, flip in MEMBERS[:6]:
            peers.append(device(axis, step, flip))
    for dy, dx in AROUND:
        peers.append(around(dy, dx))
    for peer in peers:
        pl.semaphore_signal(barrier, inc=1, device_id=peer, device_id_type=MESH)

    tin_copies = {}
    for b in ORDER:
        tin_copies[b] = pltpu.make_async_copy(tiles_hbm.at[b], tin.at[b], tin_sem.at[b])
        tin_copies[b].start()

    own = own_ref[...]
    ox, oy = own // 16, own % 16
    oq = (ox // 2, oy % 4, oy // 4)
    oc = ox % 2
    ownf = jnp.broadcast_to(own.astype(F32), (128, 128))
    same = ownf == ownf.T
    earlier = lax.broadcasted_iota(jnp.int32, (128, 128), 0) < lax.broadcasted_iota(
        jnp.int32, (128, 128), 1
    )
    rank = jnp.sum(jnp.where(same & earlier, 1.0, 0.0), axis=0, keepdims=True).astype(jnp.int32)
    rows = lax.broadcasted_iota(jnp.int32, (256, 128), 0)
    for p in range(3):
        slot = (oq[p] * 2 + oc) * 32 + (oq[(p + 1) % 3] * 4 + oq[(p + 2) % 3]) * 2 + rank
        sel[p] = jnp.where(rows == slot, 1.0, 0.0).astype(BF16)
    meta[...] = jnp.zeros((128, 128), F32)
    meta[0:6, :] = wt_ref[...].astype(F32)
    meta[6:7, :] = cell_ref[...].astype(F32) + 1.0

    s1 = {}

    def stage1_refs(b):
        p, k = b // 2, b % 2
        return (send_a.at[p], recv_a.at[p]) if k == 0 else (send_b.at[p], recv_b.at[p])

    for n, b in enumerate(ORDER):
        p, k = b // 2, b % 2
        src, dst = stage1_refs(b)
        tin_copies[b].wait()

        def gather(c, carry, b=b, p=p, src=src):
            at = pl.ds(pl.multiple_of(c * 512, 512), 512)
            src[:, at] = jnp.dot(sel[p], tin[b, :, at], preferred_element_type=F32).astype(BF16)
            return carry

        lax.fori_loop(0, 8, gather, 0)
        if k == 0:
            src[:, 4096:4224] = lax.dot_general(
                sel[p],
                meta[...].astype(BF16),
                (((1,), (1,)), ((), ())),
                preferred_element_type=F32,
            ).astype(BF16)
        if n == 0:
            pl.semaphore_wait(barrier, len(peers))
        mine = q[p] * 2 + core
        mine_rows = pl.ds(pl.multiple_of(mine * 32, 32), 32)
        own_copy = pltpu.make_async_copy(src.at[mine_rows], dst.at[mine_rows], self_sem.at[b])
        own_copy.start()
        copies = [own_copy]
        for m, (step, flip) in enumerate(MEMBERS):
            there = ((q[p] + step) % 4) * 2 + (core + flip) % 2
            copy = pltpu.make_async_remote_copy(
                src_ref=src.at[pl.ds(pl.multiple_of(there * 32, 32), 32)],
                dst_ref=dst.at[mine_rows],
                send_sem=s1_send.at[b, m],
                recv_sem=s1_recv.at[b, m],
                device_id=device(p, step, flip),
                device_id_type=MESH,
            )
            copy.start()
            copies.append(copy)
        s1[b] = copies

    s2, s3 = {}, {}

    def encode(values, denom, size):
        top = jnp.max(jnp.abs(values), axis=1, keepdims=True)
        some = top > 1e-30
        inverse = jnp.where(some, 32767.0 / jnp.where(some, top, 1.0), 0.0)
        codes = (values * inverse + 32768.5).astype(jnp.int32)
        words = codes[:, :QUARTER] | (codes[:, QUARTER:] << 16)
        lane = lax.broadcasted_iota(jnp.int32, (size, 128), 1)
        return words, jnp.where(lane < 64, denom, top * (1.0 / 32767.0))

    def decode(words, extra):
        step = extra[:, 64:65]
        low = (words & 65535).astype(F32) - 32768.0
        high = lax.shift_right_logical(words, jnp.full_like(words, 16)).astype(F32) - 32768.0
        return low * step, high * step

    def gathered(own, own_denom, words, extras):
        low, high, denom = own[:, :QUARTER], own[:, QUARTER:], own_denom
        for k in range(3):
            a, c = decode(words[k], extras[k])
            low, high, denom = low + a, high + c, denom + extras[k][:, 0:1]
        return low, high, denom

    def pass_on(b, axis, size, words, extras, to_words, to_extras, send, recv):
        copies = []
        for step in (2, 1, 3):
            there = (q[axis] + step) % 4
            at = pl.ds(pl.multiple_of(there * size, size), size)
            for n, (src, dst) in enumerate(((words, to_words), (extras, to_extras))):
                copy = pltpu.make_async_remote_copy(
                    src_ref=src.at[b, at],
                    dst_ref=dst.at[b, step - 1],
                    send_sem=send.at[b, step - 1, n],
                    recv_sem=recv.at[b, step - 1, n],
                    device_id=device(axis, step, 0),
                    device_id_type=MESH,
                )
                copy.start()
                copies.append(copy)
        return copies

    def reduce_tiles(b):
        p, k = b // 2, b % 2
        src, dst = stage1_refs(b)
        s1[b][0].wait()
        for copy in s1[b][1:]:
            copy.wait_recv()
        if k == 0:
            metar[p] = dst[:, 4096:4224].astype(F32).T[0:8, :]
        w = metar[p, b : b + 1, :]
        code = metar[p, 6:7, :].astype(jnp.int32)
        row = lax.broadcasted_iota(jnp.int32, (128, 256), 0)
        col = lax.broadcasted_iota(jnp.int32, (128, 256), 1)
        hit = ((col % 32) // 2 == row // 8) & (code == row % 4 + 1)
        upper = (row // 4) % 2 == 0
        both = jnp.where(hit, jnp.broadcast_to(w, (128, 256)), 0.0)
        c0 = jnp.where(upper, both, 0.0).astype(BF16)
        c1 = jnp.where(upper, 0.0, both).astype(BF16)
        denom = jnp.sum(both, axis=1, keepdims=True)

        def reduce(c, carry):
            lo = pl.ds(pl.multiple_of(c * 512, 512), 512)
            hi = pl.ds(pl.multiple_of(c * 512 + HALF, 512), 512)
            acc2[b, :, lo] = jnp.dot(c0, dst[:, lo], preferred_element_type=F32) + jnp.dot(
                c1, dst[:, hi], preferred_element_type=F32
            )
            return carry

        lax.fori_loop(0, 4, reduce, 0)
        st2[b], st2m[b] = encode(acc2[b], denom, 128)
        s2[b] = pass_on(b, (p + 1) % 3, 32, st2, st2m, rcv2, rcv2m, s2_send, s2_recv)

    def second(b):
        p = b // 2
        for copy in s2[b]:
            copy.wait_recv()
        at = pl.ds(pl.multiple_of(q[(p + 1) % 3] * 32, 32), 32)
        low, high, denom = gathered(acc2[b, at, :], st2m[b, at, 0:1], rcv2[b], rcv2m[b])
        acc3[b, :, :QUARTER] = low
        acc3[b, :, QUARTER:] = high
        st3[b], st3m[b] = encode(acc3[b], denom, 32)
        s3[b] = pass_on(b, (p + 2) % 3, 8, st3, st3m, rcv3, rcv3m, s3_send, s3_recv)

    left_half = lax.broadcasted_iota(jnp.int32, (16, 128), 1) < 64

    def third(b):
        p = b // 2
        axis = (p + 2) % 3
        for copy in s3[b]:
            copy.wait_recv()
        at = pl.ds(pl.multiple_of(q[axis] * 8, 8), 8)
        low, high, denom = gathered(acc3[b, at, :], st3m[b, at, 0:1], rcv3[b], rcv3m[b])
        scale = 1.0 / (1.0 + denom)
        for j in range(8):
            c = slice(128 * j, 128 * j + 128)
            tbuf[pl.ds(j, 8, stride=16), :] = low[:, c] * scale
            tbuf[pl.ds(j + 8, 8, stride=16), :] = high[:, c] * scale
        for h in range(2):
            for cy in range(2):
                s = h * 4 + cy * 2
                a = tbuf[16 * s : 16 * s + 16, :]
                c = tbuf[16 * s + 16 : 16 * s + 32, :]
                y0 = 64 * cy + 32 * h
                out_ref[pl.ds(128 * b + y0, 16, stride=2), :] = jnp.where(
                    left_half, a, pltpu.roll(c, 64, 1)
                )
                out_ref[pl.ds(128 * b + y0 + 1, 16, stride=2), :] = jnp.where(
                    left_half, pltpu.roll(a, 64, 1), c
                )
        r = 128 * b
        n = ORDER.index(b)
        hsend[0, n] = out_ref[r : r + 8, :]
        hsend[1, n] = out_ref[r + 120 : r + 128, :]
        turned = out_ref[r : r + 128, :].T
        hsend[2, n] = turned[0:8, :]
        hsend[3, n] = turned[120:128, :]
        out_ref[1152 + 8 * b : 1160 + 8 * b, :] = turned[0:8, :]
        out_ref[1200 + 8 * b : 1208 + 8 * b, :] = turned[120:128, :]

    halo = []

    def send_halo(group):
        bands = pl.ds(3 * group, 3)
        for n, (dy, dx) in enumerate(AROUND):
            which = 0 if dy < 0 else 1 if dy > 0 else 2 if dx < 0 else 3
            copy = pltpu.make_async_remote_copy(
                src_ref=hsend.at[which, bands],
                dst_ref=hrecv.at[n, bands],
                send_sem=h_send.at[group, n],
                recv_sem=h_recv.at[group, n],
                device_id=around(dy, dx),
                device_id_type=MESH,
            )
            copy.start()
            halo.append(copy)

    for n in range(6 + 4):
        if n < 6:
            reduce_tiles(ORDER[n])
        if 0 <= n - 2 < 6:
            second(ORDER[n - 2])
        if 0 <= n - 4 < 6:
            third(ORDER[n - 4])
            if n - 4 in (2, 5):
                send_halo((n - 4) // 3)

    for b in ORDER:
        for copy in s1[b][1:] + s2[b] + s3[b]:
            copy.wait_send()
    for n, copy in enumerate(halo):
        copy.wait_recv()
        group, slot = n // 8, n % 8
        for k in range(3):
            r = 768 + 48 * slot + 8 * ORDER[3 * group + k]
            out_ref[r : r + 8, :] = hrecv[slot, 3 * group + k]
    out_ref[1248:1256, :] = jnp.zeros((8, 128), F32)
    for copy in halo:
        copy.wait_send()


def full_exchange(tiles, weights, owners, cells):
    vmem = pl.BlockSpec(memory_space=pltpu.VMEM)
    dma = pltpu.SemaphoreType.DMA
    return pl.pallas_call(
        full_exchange_kernel,
        out_shape=jax.ShapeDtypeStruct((1256, 128), F32),
        in_specs=[pl.BlockSpec(memory_space=pl.ANY), vmem, vmem, vmem],
        out_specs=vmem,
        scratch_shapes=[
            pltpu.VMEM((NB, 128, 4096), BF16),
            pltpu.VMEM((3, 256, 128), BF16),
            pltpu.VMEM((128, 128), F32),
            pltpu.VMEM((3, 8, 256), F32),
            pltpu.VMEM((3, 256, 4224), BF16),
            pltpu.VMEM((3, 256, 4096), BF16),
            pltpu.VMEM((3, 256, 4224), BF16),
            pltpu.VMEM((3, 256, 4096), BF16),
            pltpu.VMEM((NB, 128, HALF), F32),
            pltpu.VMEM((NB, 128, QUARTER), jnp.int32),
            pltpu.VMEM((NB, 128, 128), F32),
            pltpu.VMEM((NB, 3, 32, QUARTER), jnp.int32),
            pltpu.VMEM((NB, 3, 32, 128), F32),
            pltpu.VMEM((NB, 32, HALF), F32),
            pltpu.VMEM((NB, 32, QUARTER), jnp.int32),
            pltpu.VMEM((NB, 32, 128), F32),
            pltpu.VMEM((NB, 3, 8, QUARTER), jnp.int32),
            pltpu.VMEM((NB, 3, 8, 128), F32),
            pltpu.VMEM((128, 128), F32),
            pltpu.VMEM((4, NB, 8, 128), F32),
            pltpu.VMEM((8, NB, 8, 128), F32),
            dma((NB,)),
            dma((NB,)),
            dma((NB, 7)),
            dma((NB, 7)),
            dma((NB, 3, 2)),
            dma((NB, 3, 2)),
            dma((NB, 3, 2)),
            dma((NB, 3, 2)),
            dma((2, 8)),
            dma((2, 8)),
        ],
        compiler_params=pltpu.CompilerParams(
            collective_id=1, has_side_effects=True, vmem_limit_bytes=60 * 1024 * 1024
        ),
        name="full_exchange",
    )(tiles, weights, owners, cells)


def detect_kernel(
    taps_ref,
    coadd_hbm,
    w1_ref,
    b1_ref,
    w2_ref,
    b2_ref,
    psf_hbm,
    det_hbm,
    coadd_ref,
    psf_out,
    det_out,
    partial,
    ext,
    shifted,
    sides,
    sides_t,
    psf,
    taps3,
    edge3,
    hidden,
    turned,
    small,
    beside,
    w2s,
    sems,
):
    ix = lax.axis_index("skyx")
    iy = lax.axis_index("skyy")
    top, bottom = (iy > 0).astype(F32), (iy < 15).astype(F32)
    left, right = (ix > 0).astype(F32), (ix < 7).astype(F32)

    fetch = pltpu.make_async_copy(coadd_hbm, coadd_ref, sems.at[0])
    fetch.start()

    def halo(slot, b):
        r = 768 + slot * 48 + b * 8
        return coadd_ref[r : r + 8, :]

    def lanes_of(n):
        return lax.broadcasted_iota(jnp.int32, (n, 128), 1)

    small[...] = jnp.zeros((128, 128), F32)
    for b in range(NB):
        for i in range(3):
            small[pl.ds(i * 24 + b, 3, stride=8), 0:64] = w1_ref[b, i].astype(F32)
    w1 = (small[...].T[0:64, 0:72] * 0.5).astype(BF16)
    for i in range(3):
        for j in range(3):
            at = 64 * (3 * i + j)
            w2s[:, at : at + 64] = w2_ref[i, j]
    small[0:1, 0:64] = b1_ref[...] * 0.5
    small[1:2, 0:64] = b2_ref[...]
    columns = small[...].T
    bias1 = jnp.broadcast_to(columns[0:64, 0:1], (64, 256))
    bias2 = jnp.broadcast_to(columns[0:64, 1:2], (64, 256))

    taps3[...] = jnp.zeros_like(taps3)
    fetch.wait()

    pieces = []
    for b in range(NB):
        pieces += [
            halo(3, b)[2:8] * left,
            halo(8, b)[0:4],
            halo(9, b)[4:8],
            halo(2, b)[0:6] * right,
        ]
    pieces.append(jnp.zeros((8, 128), F32))
    sides[8:136, :] = jnp.concatenate(pieces, axis=0).T
    lane8 = lanes_of(8)
    for r, mid, at_left, at_right, keep in ((0, 1, 7, 6, top), (136, 0, 5, 4, bottom)):
        line = jnp.zeros((8, 128), F32)
        for b in range(NB):
            middle = halo(mid, b)
            parts = (
                (halo(at_left, b) * left, 122, 0, 6),
                (middle, 0, 6, 4),
                (middle, 124, 10, 4),
                (halo(at_right, b) * right, 0, 14, 6),
            )
            for value, start, at, size in parts:
                at = 20 * b + at
                moved = pltpu.roll(value, (at - start) % 128, 1)
                line = jnp.where((lane8 >= at) & (lane8 < at + size), moved, line)
        sides[r : r + 8, :] = line * keep

    for j in range(9):
        shifted[j] = pltpu.roll(sides[...], (-j) % 128, 1) if j else sides[...]
    owner_band = lane8 // 20

    def edge_block(start, size):
        acc = jnp.zeros((size, 128), F32)
        for i in range(9):
            for j in range(9):
                tap = jnp.full((8, 128), taps_ref[i, 0, j], F32)
                for b in range(1, NB):
                    tap = jnp.where(owner_band == b, taps_ref[i, b, j], tap)
                tap = jnp.broadcast_to(tap[0:1], (size, 128))
                acc = acc + tap * shifted[j, start + i : start + i + size, :]
        at = lax.broadcasted_iota(jnp.int32, (size, 128), 0) + start
        keep = jnp.where(at < 4, top, jnp.where(at >= 132, bottom, 1.0))
        keep = keep * jnp.where(lanes_of(size) % 20 < 10, left, right)
        return acc.astype(BF16).astype(F32) * keep

    sides[0:136, :] = edge_block(0, 136)

    for b in range(NB):
        ext[b, 8:136, :] = coadd_ref[128 * b : 128 * b + 128, :]
        ext[b, 0:8, :] = halo(1, b) * top
        ext[b, 136:144, :] = halo(0, b) * bottom
    column = lanes_of(144)

    def band(b, carry):
        near_left = pltpu.roll(shifted[0], 122 - 20 * b, 1)
        near_right = pltpu.roll(shifted[0], 114 - 20 * b, 1)
        x = ext[b]
        for j in range(9):
            if j < 4:
                moved = pltpu.roll(jnp.where(column >= 124 + j, near_left, x), 4 - j, 1)
            elif j == 4:
                moved = x
            else:
                moved = pltpu.roll(jnp.where(column < j - 4, near_right, x), 132 - j, 1)
            shifted[j + 1] = moved

        for n in range(6):
            at_rows = slice(24 * n, 24 * n + 24)
            sums = [None] * 9
            for j in range(9):
                value = shifted[j + 1, at_rows, :]
                for i in range(9):
                    term = taps_ref[i, b, j] * value
                    sums[i] = term if j == 0 else sums[i] + term
            for i in range(9):
                partial[i, at_rows, :] = sums[i]

        def block(start, size):
            acc = partial[0, start : start + size, :]
            for i in range(1, 9):
                acc = acc + partial[i, start + i : start + i + size, :]
            at = lax.broadcasted_iota(jnp.int32, (size, 128), 0) + start
            keep = jnp.where(at < 4, top, jnp.where(at >= 132, bottom, 1.0))
            v = acc.astype(BF16).astype(F32) * keep
            psf[start : start + size, :] = v
            lane = lanes_of(size)
            edge = sides[start : start + size, :]
            before = jnp.where(lane == 0, pltpu.roll(edge, 127 - 20 * b, 1), pltpu.roll(v, 1, 1))
            after = jnp.where(
                lane == 127, pltpu.roll(edge, 117 - 20 * b, 1), pltpu.roll(v, 127, 1)
            )
            for j, value in enumerate((before, v, after)):
                taps3[pl.ds(start * 24 + 8 * j + b, size, stride=24), :] = value
            edge = jnp.where(lane == 20 * b + 2, pltpu.roll(v, 20 * b + 2, 1), edge)
            edge = jnp.where(lane == 20 * b + 9, pltpu.roll(v, 20 * b + 10, 1), edge)
            sides[start : start + size, :] = edge

        block(0, 72)
        block(72, 64)
        psf_out[b] = psf[4:132, :].astype(BF16)
        return carry

    lax.fori_loop(0, NB, band, 0)

    psf_copy = pltpu.make_async_copy(psf_out, psf_hbm, sems.at[1])
    psf_copy.start()

    def silu(u):
        return u + u * jnp.tanh(u)

    sides_t[0] = sides[0:128, :].T
    tail = jnp.concatenate([sides[128:136, :], jnp.zeros((120, 128), F32)], axis=0)
    sides_t[1] = tail.T
    edge3[...] = jnp.zeros_like(edge3)
    at256 = lax.broadcasted_iota(jnp.int32, (64, 256), 1)
    ends = jnp.where(at256 == 0, top, jnp.where(at256 == 129, bottom, 1.0))
    for side, (offset, keep) in enumerate(((0, left), (9, right))):
        for t in range(2):
            for j in range(3):
                edge3[side, 8 * j : 8 * j + 6, 128 * t : 128 * t + 128] = sides_t[
                    t, pl.ds(offset + j, 6, stride=20), :
                ]
        x = edge3[side]
        rhs = jnp.concatenate([pltpu.roll(x, 256 - (2 + i), 1) for i in range(3)], axis=0)
        v = silu(jnp.dot(w1, rhs.astype(BF16), preferred_element_type=F32) + bias1)
        v = v * (ends * keep)
        beside[side, 0] = v[:, 0:128]
        beside[side, 1] = v[:, 128:256]

    lane64 = lanes_of(64)

    def pair(n, t):
        at0 = pl.ds(pl.multiple_of((2 * n + 2) * 24, 8), 72)
        at1 = pl.ds(pl.multiple_of((2 * n + 3) * 24, 8), 72)
        rhs = jnp.concatenate([taps3[at0, :], taps3[at1, :]], axis=1).astype(BF16)
        v = silu(jnp.dot(w1, rhs, preferred_element_type=F32) + bias1)
        for k in range(2):
            row, h = 2 * n + k, v[:, 128 * k : 128 * k + 128]
            near = pltpu.roll(beside[0, t], 128 * (t + 1) - row, 1)
            far = pltpu.roll(beside[1, t], 128 * (t + 1) - 1 - row, 1)
            hidden[row, 0:64] = jnp.where(lane64 == 0, near, pltpu.roll(h, 1, 1)).astype(BF16)
            hidden[row, 64:128] = h.astype(BF16)
            hidden[row, 128:192] = jnp.where(lane64 == 127, far, pltpu.roll(h, 127, 1)).astype(
                BF16
            )

    def first(n, carry):
        pair(n, 0)
        return carry

    lax.fori_loop(0, 64, first, 0, unroll=16)
    pair(64, 1)
    hidden[0] = (hidden[0].astype(F32) * top).astype(BF16)
    hidden[129] = (hidden[129].astype(F32) * bottom).astype(BF16)

    w2 = w2s[...]

    def leave(g):
        at = pl.ds(pl.multiple_of(g * 16, 16), 16)
        return pltpu.make_async_copy(det_out.at[g], det_hbm.at[:, at], sems.at[2 + g])

    def group(g, carry):
        def rows(n, inner):
            y = g * 16 + 2 * n
            rhs = jnp.concatenate(
                [hidden[pl.ds(y, 3)].reshape(576, 128), hidden[pl.ds(y + 1, 3)].reshape(576, 128)],
                axis=1,
            )
            z = jnp.dot(w2, rhs, preferred_element_type=F32) + bias2
            turned[pl.ds(2 * n, 64, stride=16), :] = z[:, 0:128]
            turned[pl.ds(2 * n + 1, 64, stride=16), :] = z[:, 128:256]
            return inner

        lax.fori_loop(0, 8, rows, 0, unroll=8)
        det_out[g] = turned[...].reshape(64, 16, 128).astype(BF16)
        leave(g).start()
        return carry

    lax.fori_loop(0, 8, group, 0)
    psf_copy.wait()
    for g in range(8):
        leave(g).wait()


def detect(taps, coadd, w1, b1, w2, b2):
    vmem = pl.BlockSpec(memory_space=pltpu.VMEM)
    anywhere = pl.BlockSpec(memory_space=pl.ANY)
    return pl.pallas_call(
        detect_kernel,
        out_shape=(
            jax.ShapeDtypeStruct((NB, 128, 128), BF16),
            jax.ShapeDtypeStruct((64, 128, 128), BF16),
        ),
        in_specs=[pl.BlockSpec(memory_space=pltpu.SMEM), anywhere] + [vmem] * 4,
        out_specs=(anywhere, anywhere),
        scratch_shapes=[
            pltpu.VMEM((1256, 128), F32),
            pltpu.VMEM((NB, 128, 128), BF16),
            pltpu.VMEM((8, 64, 16, 128), BF16),
            pltpu.VMEM((9, 144, 128), F32),
            pltpu.VMEM((NB, 144, 128), F32),
            pltpu.VMEM((10, 144, 128), F32),
            pltpu.VMEM((144, 128), F32),
            pltpu.VMEM((2, 128, 128), F32),
            pltpu.VMEM((136, 128), F32),
            pltpu.VMEM((136 * 24, 128), F32),
            pltpu.VMEM((2, 24, 256), F32),
            pltpu.VMEM((130, 192, 128), BF16),
            pltpu.VMEM((64 * 16, 128), F32),
            pltpu.VMEM((128, 128), F32),
            pltpu.VMEM((2, 2, 64, 128), F32),
            pltpu.VMEM((64, 576), BF16),
            pltpu.SemaphoreType.DMA((10,)),
        ],
        compiler_params=pltpu.CompilerParams(vmem_limit_bytes=48 * 1024 * 1024),
        name="detect",
    )(taps, coadd, w1, b1, w2, b2)


def body(
    tiles,
    tile_weight,
    owners,
    cells,
    psf_kernel,
    conv1_weight,
    conv1_bias,
    conv2_weight,
    conv2_bias,
):
    operands = (
        tiles.transpose(1, 0, 2),
        tile_weight.transpose(1, 0),
        owners.reshape(1, 128),
        cells.reshape(1, 128),
    )
    coadd = exchange(*operands)
    coadd = lax.cond(coadd[1248, 0] > 0.5, lambda: full_exchange(*operands), lambda: coadd)
    return detect(
        psf_kernel.transpose(1, 0, 2),
        coadd,
        conv1_weight.transpose(1, 2, 3, 0),
        conv1_bias.reshape(1, 64),
        conv2_weight.transpose(2, 3, 0, 1),
        conv2_bias.reshape(1, 64),
    )


def solution(mesh):
    in_specs = (
        P(("skyx", "skyy"), None, None),
        P(("skyx", "skyy"), None),
        P(("skyx", "skyy"), None),
        P(("skyx", "skyy")),
        P(),
        P(),
        P(),
        P(),
        P(),
    )
    out_specs = (P(None, "skyy", "skyx"), P(None, "skyy", "skyx"))
    return jax.shard_map(body, mesh=mesh, in_specs=in_specs, out_specs=out_specs, check_vma=False)
```

```python
import functools

import jax
import jax.numpy as jnp
from jax import lax
from jax.experimental import pallas as pl
from jax.experimental.pallas import tpu as pltpu
from jax.sharding import PartitionSpec as P

MESH = pl.DeviceIdType.MESH
F32 = jnp.float32
BF16 = jnp.bfloat16

NB = 6
HALF = 2048
QUARTER = 1024
WIDE = HALF + 128
PIECES = ((0, 0, 2048), (1, 0, 2048))
UNITS = 3 * len(PIECES)
LAGS = (0, 3, 5, 6)
ORDER = (0, 2, 4, 1, 3, 5)
MEMBERS = ((2, 0), (2, 1), (1, 0), (3, 0), (1, 1), (3, 1), (0, 1))
AROUND = ((-1, 0), (1, 0), (0, -1), (0, 1), (-1, -1), (-1, 1), (1, -1), (1, 1))


def encode(values, denom, flag, size):
    top = jnp.max(jnp.abs(values), axis=1, keepdims=True)
    some = top > 1e-30
    inverse = jnp.where(some, 32767.0 / jnp.where(some, top, 1.0), 0.0)
    codes = (values * inverse + 32768.5).astype(jnp.int32)
    middle = values.shape[1] // 2
    words = codes[:, :middle] | (codes[:, middle:] << 16)
    lane = lax.broadcasted_iota(jnp.int32, (size, 128), 1)
    extra = jnp.where(lane < 64, denom, top * (1.0 / 32767.0))
    return words, jnp.where(lane == 127, flag, extra)


def decode(words, extra):
    step = extra[:, 64:65]
    low = (words & 65535).astype(F32) - 32768.0
    high = lax.shift_right_logical(words, jnp.full_like(words, 16)).astype(F32) - 32768.0
    return low * step, high * step


def gathered(own, own_extra, words, extras):
    middle = own.shape[1] // 2
    low, high = own[:, :middle], own[:, middle:]
    denom, flag = own_extra[:, 0:1], own_extra[:, 127:128]
    for k in range(3):
        a, c = decode(words[k], extras[k])
        low, high, denom = low + a, high + c, denom + extras[k][:, 0:1]
        flag = jnp.maximum(flag, extras[k][:, 127:128])
    return low, high, denom, jnp.max(flag, axis=0, keepdims=True)


def exchange_kernel(
    tiles_hbm,
    wt_ref,
    own_ref,
    cell_ref,
    out_ref,
    tin,
    sel,
    selx,
    meta,
    send_lo,
    send_hi,
    send_x,
    recv_lo,
    recv_hi,
    recv_x,
    acc2,
    st2,
    st2m,
    rcv2,
    rcv2m,
    acc3,
    st3,
    st3m,
    rcv3,
    rcv3m,
    tbuf,
    rbuf,
    hsend,
    hrecv,
    tin_sem,
    self_sem,
    s1_send,
    s1_recv,
    x_send,
    x_recv,
    s2_send,
    s2_recv,
    s3_send,
    s3_recv,
    c_send,
    c_recv,
    h_send,
    h_recv,
):
    ix = lax.axis_index("skyx")
    iy = lax.axis_index("skyy")
    core = ix % 2
    q = (ix // 2, iy % 4, iy // 4)

    def device(axis, step, flip):
        r = list(q)
        if step:
            r[axis] = (r[axis] + step) % 4
        c = (core + flip) % 2 if flip else core
        return (r[0] * 2 + c, r[2] * 4 + r[1])

    def around(dy, dx):
        return ((ix + dx + 8) % 8, (iy + dy + 16) % 16)

    barrier = pltpu.get_barrier_semaphore()
    peers = [device(0, 0, 1)]
    for axis in range(3):
        for step, flip in MEMBERS[:6]:
            peers.append(device(axis, step, flip))
    for dy, dx in AROUND:
        peers.append(around(dy, dx))
    for peer in peers:
        pl.semaphore_signal(barrier, inc=1, device_id=peer, device_id_type=MESH)

    tin_copies = []
    for b in range(NB):
        tin_copies.append(pltpu.make_async_copy(tiles_hbm.at[b], tin.at[b], tin_sem.at[b]))
        tin_copies[b].start()

    own = own_ref[...]
    ox, oy = own // 16, own % 16
    oq = (ox // 2, oy % 4, oy // 4)
    oc = ox % 2
    earlier = lax.broadcasted_iota(jnp.int32, (128, 128), 0) < lax.broadcasted_iota(
        jnp.int32, (128, 128), 1
    )
    rows = lax.broadcasted_iota(jnp.int32, (128, 128), 0)
    rows_x = lax.broadcasted_iota(jnp.int32, (64, 128), 0)
    lane128 = lax.broadcasted_iota(jnp.int32, (128, 128), 1)
    meta[...] = jnp.zeros((128, 128), F32)
    meta[0:6, :] = wt_ref[...].astype(F32)

    def select(p):
        group = jnp.broadcast_to(oq[p].astype(F32), (128, 128))
        rank = jnp.sum(
            jnp.where((group == group.T) & earlier, 1.0, 0.0), axis=0, keepdims=True
        )
        over = jnp.where(jnp.max(rank, axis=1, keepdims=True) > 39.5, 1.0, 0.0)
        rank = rank.astype(jnp.int32)
        slot = jnp.where(rank < 32, oq[p] * 32 + rank, -1)
        sel[p, 0:128] = jnp.where(rows == slot, 1.0, 0.0).astype(BF16)
        slot = jnp.where((rank >= 32) & (rank < 40), oq[p] * 16 + rank - 32, -64)
        sel[p, 128:192] = jnp.where(rows_x == slot, 1.0, 0.0).astype(BF16)
        selx[p] = jnp.where(rows_x == slot + 8, 1.0, 0.0).astype(BF16)
        unit = oq[(p + 1) % 3] * 4 + oq[(p + 2) % 3]
        meta[6:7, :] = ((unit * 2 + oc) * 4 + cell_ref[...] + 1).astype(F32)
        both = pick_meta(sel[p])
        extra = both[128:192] + pick_meta(selx[p])
        return jnp.where(lane128 == 7, over, both[0:128]).astype(BF16), extra.astype(BF16)

    def pick(which, value):
        return jnp.dot(which, value, preferred_element_type=F32)

    def pick_meta(which):
        return lax.dot_general(
            which,
            meta[...].astype(BF16),
            (((1,), (1,)), ((), ())),
            preferred_element_type=F32,
        )

    s1 = {}
    for n in range(UNITS):
        p, (half, first, width) = n % 3, PIECES[n // 3]
        if half == 0:
            flagged, extra = select(p)
        for k in range(2):
            b = 2 * p + k
            if half == 0:
                tin_copies[b].wait()

            def gather(c, carry, b=b, p=p, k=k, half=half, first=first):
                at = pl.ds(pl.multiple_of(c * 512 + first, 512), 512)
                there = pl.ds(pl.multiple_of(c * 512 + first + HALF, 512), 512)
                if half == 0:
                    both = pick(sel[p], tin[b, :, at])
                    send_lo[p, k, :, at] = both[0:128].astype(BF16)
                    send_x[p, k, :, at] = (
                        both[128:192] + pick(selx[p], tin[b, :, there])
                    ).astype(BF16)
                else:
                    send_hi[p, k, :, at] = pick(sel[p, 0:128], tin[b, :, there]).astype(BF16)
                return carry

            lax.fori_loop(0, width // 512, gather, 0)
            if half == 0:
                send_lo[p, k, :, HALF:WIDE] = flagged
                send_x[p, k, :, HALF:WIDE] = extra
        if n == 0:
            pl.semaphore_wait(barrier, len(peers))
        mine = q[p] * 2 + core
        streams = [(send_hi, recv_hi, 32, pl.ds(first, width), s1_send, s1_recv)]
        if half == 0:
            streams = [
                (send_lo, recv_lo, 32, pl.ds(0, WIDE), s1_send, s1_recv),
                (send_x, recv_x, 16, pl.ds(0, WIDE), x_send, x_recv),
            ]
        local, away = [], []
        for m, (step, flip) in enumerate(MEMBERS + ((0, 0),)):
            to = (q[p] + step) % 4
            parity = (core + flip) % 2
            for w, (src, dst, size, columns, sends, recvs) in enumerate(streams):
                from_ref = src.at[p, parity, pl.ds(pl.multiple_of(to * size, size), size), columns]
                to_ref = dst.at[p, pl.ds(pl.multiple_of(mine * size, size), size), columns]
                if (step, flip) == (0, 0):
                    copy = pltpu.make_async_copy(from_ref, to_ref, self_sem.at[n, w])
                    local.append(copy)
                else:
                    at = n if size == 32 else p
                    copy = pltpu.make_async_remote_copy(
                        src_ref=from_ref,
                        dst_ref=to_ref,
                        send_sem=sends.at[at, m],
                        recv_sem=recvs.at[at, m],
                        device_id=device(p, step, flip),
                        device_id_type=MESH,
                    )
                    away.append(copy)
                copy.start()
        s1[n] = (local, away)

    s2, s3, s4 = {}, {}, {}

    def pass_on(n, axis, size, words, extras, to_words, to_extras, send, recv):
        copies = []
        half, first, width = PIECES[n // 3]
        m, columns = 3 * half + n % 3, pl.ds(first // 2, width // 2)
        for step in (2, 1, 3):
            there = (q[axis] + step) % 4
            at = pl.ds(pl.multiple_of(there * size, size), size)
            pairs = (
                (words.at[m, at, columns], to_words.at[m, step - 1, :, columns]),
                (extras.at[n, at], to_extras.at[n, step - 1]),
            )
            for w, (from_ref, to_ref) in enumerate(pairs):
                copy = pltpu.make_async_remote_copy(
                    src_ref=from_ref,
                    dst_ref=to_ref,
                    send_sem=send.at[n, step - 1, w],
                    recv_sem=recv.at[n, step - 1, w],
                    device_id=device(axis, step, 0),
                    device_id_type=MESH,
                )
                copy.start()
                copies.append(copy)
        return copies

    weighted = {}

    def coefficients(p):
        m = recv_lo[p, :, HALF:WIDE].astype(F32).T
        mx = recv_x[p, :, HALF:WIDE].astype(F32).T
        w = jnp.where(core == 0, m[2 * p : 2 * p + 1], m[2 * p + 1 : 2 * p + 2])
        wx = jnp.where(core == 0, mx[2 * p : 2 * p + 1], mx[2 * p + 1 : 2 * p + 2])
        at = lax.broadcasted_iota(jnp.int32, (128, 256), 0).astype(F32) + 1.0
        c = jnp.where(m[6:7] == at, jnp.broadcast_to(w, (128, 256)), 0.0)
        cx = jnp.where(mx[6:7] == at[:, 0:128], jnp.broadcast_to(wx, (128, 128)), 0.0)
        low = (lane128 // 8) % 2 == 0
        x0, x1 = jnp.where(low, cx, 0.0), jnp.where(low, 0.0, cx)
        denom = jnp.sum(c, axis=1, keepdims=True) + jnp.sum(x0, axis=1, keepdims=True)
        flag = jnp.max(m[7:8], axis=1, keepdims=True)
        return c.astype(BF16), x0.astype(BF16), x1.astype(BF16), denom, flag

    def reduce_tiles(n):
        p, (half, first, width) = n % 3, PIECES[n // 3]
        m = 3 * half + p
        for copy in s1[n][0]:
            copy.wait()
        for copy in s1[n][1]:
            copy.wait_recv()
        if half == 0:
            weighted[p] = coefficients(p)
        c, x0, x1, denom, flag = weighted[p]
        src = recv_lo if half == 0 else recv_hi
        cx = x0 if half == 0 else x1

        def reduce(i, carry):
            at = pl.ds(pl.multiple_of(i * 512 + first, 512), 512)
            acc2[m, :, at] = pick(c, src[p, :, at]) + pick(cx, recv_x[p, :, at])
            return carry

        lax.fori_loop(0, width // 512, reduce, 0)
        words, extra = encode(acc2[m, :, first : first + width], denom, flag, 128)
        st2[m, :, first // 2 : (first + width) // 2] = words
        st2m[n] = extra
        s2[n] = pass_on(n, (p + 1) % 3, 32, st2, st2m, rcv2, rcv2m, s2_send, s2_recv)

    def second(n):
        p, (half, first, width) = n % 3, PIECES[n // 3]
        m, columns = 3 * half + p, slice(first // 2, (first + width) // 2)
        for copy in s2[n]:
            copy.wait_recv()
        at = pl.ds(pl.multiple_of(q[(p + 1) % 3] * 32, 32), 32)
        low, high, denom, flag = gathered(
            acc2[m, at, first : first + width],
            st2m[n, at, :],
            rcv2[m, :, :, columns],
            rcv2m[n],
        )
        middle = first + width // 2
        acc3[m, :, first:middle] = low
        acc3[m, :, middle : first + width] = high
        st3[m, :, columns], st3m[n] = encode(acc3[m, :, first : first + width], denom, flag, 32)
        s3[n] = pass_on(n, (p + 2) % 3, 8, st3, st3m, rcv3, rcv3m, s3_send, s3_recv)

    def third(n):
        p, (half, first, width) = n % 3, PIECES[n // 3]
        m, columns = 3 * half + p, slice(first // 2, (first + width) // 2)
        for copy in s3[n]:
            copy.wait_recv()
        at = pl.ds(pl.multiple_of(q[(p + 2) % 3] * 8, 8), 8)
        low, high, denom, flag = gathered(
            acc3[m, at, first : first + width],
            st3m[n, at, :],
            rcv3[m, :, :, columns],
            rcv3m[n],
        )
        if n < 3:
            flag = jnp.broadcast_to(flag, (8, 128))
            out_ref[1248:1256, :] = jnp.maximum(out_ref[1248:1256, :], flag) if n else flag
        scale = 1.0 / (1.0 + denom)
        lines = width // 128
        for j in range(lines // 2):
            c = slice(128 * j, 128 * j + 128)
            tbuf[n, pl.ds(j, 8, stride=lines), :] = low[:, c] * scale
            tbuf[n, pl.ds(j + lines // 2, 8, stride=lines), :] = high[:, c] * scale
        size = 4 * lines
        s4[n] = pltpu.make_async_remote_copy(
            src_ref=tbuf.at[n, pl.ds(pl.multiple_of((1 - core) * size, size), size)],
            dst_ref=rbuf.at[n, pl.ds(0, size)],
            send_sem=c_send.at[n],
            recv_sem=c_recv.at[n],
            device_id=device(0, 0, 1),
            device_id_type=MESH,
        )
        s4[n].start()

    halo = []

    def place(value, band, row):
        lines = value.shape[0] // 4
        left_half = lax.broadcasted_iota(jnp.int32, (lines, 128), 1) < 64
        for cy in range(2):
            r = 2 * cy * lines
            a, c = value[r : r + lines], value[r + lines : r + 2 * lines]
            y0 = band * 128 + 64 * cy + row
            out_ref[pl.ds(y0, lines, stride=2), :] = jnp.where(
                left_half, a, pltpu.roll(c, 64, 1)
            )
            out_ref[pl.ds(y0 + 1, lines, stride=2), :] = jnp.where(
                left_half, pltpu.roll(a, 64, 1), c
            )

    def fourth(n):
        p, (half, first, width) = n % 3, PIECES[n // 3]
        row, size = (half * HALF + first) // 64, width // 32
        place(tbuf[n, pl.ds(pl.multiple_of(core * size, size), size), :], 2 * p + core, row)
        s4[n].wait_recv()
        place(rbuf[n, 0:size, :], 2 * p + 1 - core, row)
        if n < UNITS - 3:
            return
        for b in (2 * p, 2 * p + 1):
            r = 128 * b
            hsend[0, b] = out_ref[r : r + 8, :]
            hsend[1, b] = out_ref[r + 120 : r + 128, :]
            turned = out_ref[r : r + 128, :].T
            hsend[2, b] = turned[0:8, :]
            hsend[3, b] = turned[120:128, :]
            out_ref[1152 + 8 * b : 1160 + 8 * b, :] = turned[0:8, :]
            out_ref[1200 + 8 * b : 1208 + 8 * b, :] = turned[120:128, :]
        bands = pl.ds(2 * p, 2)
        for m, (dy, dx) in enumerate(AROUND):
            which = 0 if dy < 0 else 1 if dy > 0 else 2 if dx < 0 else 3
            copy = pltpu.make_async_remote_copy(
                src_ref=hsend.at[which, bands],
                dst_ref=hrecv.at[m, bands],
                send_sem=h_send.at[p, m],
                recv_sem=h_recv.at[p, m],
                device_id=around(dy, dx),
                device_id_type=MESH,
            )
            copy.start()
            halo.append(copy)

    steps = (reduce_tiles, second, third, fourth)
    for n in range(UNITS + LAGS[3] + 1):
        for lag, step in zip(LAGS, steps):
            if 0 <= n - lag < UNITS:
                step(n - lag)

    for n in range(UNITS):
        for copy in s1[n][1] + s2[n] + s3[n] + [s4[n]]:
            copy.wait_send()
    for n, copy in enumerate(halo):
        copy.wait_recv()
        p, slot = n // 8, n % 8
        r = 768 + 48 * slot + 16 * p
        out_ref[r : r + 16, :] = hrecv[slot, 2 * p : 2 * p + 2].reshape(16, 128)
    for copy in halo:
        copy.wait_send()


def exchange(tiles, weights, owners, cells):
    vmem = pl.BlockSpec(memory_space=pltpu.VMEM)
    dma = pltpu.SemaphoreType.DMA
    return pl.pallas_call(
        exchange_kernel,
        out_shape=jax.ShapeDtypeStruct((1256, 128), F32),
        in_specs=[pl.BlockSpec(memory_space=pl.ANY), vmem, vmem, vmem],
        out_specs=vmem,
        scratch_shapes=[
            pltpu.VMEM((NB, 128, 4096), BF16),
            pltpu.VMEM((3, 192, 128), BF16),
            pltpu.VMEM((3, 64, 128), BF16),
            pltpu.VMEM((128, 128), F32),
            pltpu.VMEM((3, 2, 128, WIDE), BF16),
            pltpu.VMEM((3, 2, 128, HALF), BF16),
            pltpu.VMEM((3, 2, 64, WIDE), BF16),
            pltpu.VMEM((3, 256, WIDE), BF16),
            pltpu.VMEM((3, 256, HALF), BF16),
            pltpu.VMEM((3, 128, WIDE), BF16),
            pltpu.VMEM((NB, 128, HALF), F32),
            pltpu.VMEM((NB, 128, QUARTER), jnp.int32),
            pltpu.VMEM((UNITS, 128, 128), F32),
            pltpu.VMEM((NB, 3, 32, QUARTER), jnp.int32),
            pltpu.VMEM((UNITS, 3, 32, 128), F32),
            pltpu.VMEM((NB, 32, HALF), F32),
            pltpu.VMEM((NB, 32, QUARTER), jnp.int32),
            pltpu.VMEM((UNITS, 32, 128), F32),
            pltpu.VMEM((NB, 3, 8, QUARTER), jnp.int32),
            pltpu.VMEM((UNITS, 3, 8, 128), F32),
            pltpu.VMEM((UNITS, 128, 128), F32),
            pltpu.VMEM((UNITS, 64, 128), F32),
            pltpu.VMEM((4, NB, 8, 128), F32),
            pltpu.VMEM((8, NB, 8, 128), F32),
            dma((NB,)),
            dma((UNITS, 2)),
            dma((UNITS, 7)),
            dma((UNITS, 7)),
            dma((3, 7)),
            dma((3, 7)),
            dma((UNITS, 3, 2)),
            dma((UNITS, 3, 2)),
            dma((UNITS, 3, 2)),
            dma((UNITS, 3, 2)),
            dma((UNITS,)),
            dma((UNITS,)),
            dma((3, 8)),
            dma((3, 8)),
        ],
        compiler_params=pltpu.CompilerParams(
            collective_id=0, has_side_effects=True, vmem_limit_bytes=60 * 1024 * 1024
        ),
        name="tile_exchange",
    )(tiles, weights, owners, cells)


def full_exchange_kernel(
    tiles_hbm,
    wt_ref,
    own_ref,
    cell_ref,
    out_ref,
    tin,
    sel,
    meta,
    metar,
    send_a,
    send_b,
    recv_a,
    recv_b,
    acc2,
    st2,
    st2m,
    rcv2,
    rcv2m,
    acc3,
    st3,
    st3m,
    rcv3,
    rcv3m,
    tbuf,
    hsend,
    hrecv,
    tin_sem,
    self_sem,
    s1_send,
    s1_recv,
    s2_send,
    s2_recv,
    s3_send,
    s3_recv,
    h_send,
    h_recv,
):
    ix = lax.axis_index("skyx")
    iy = lax.axis_index("skyy")
    core = ix % 2
    q = (ix // 2, iy % 4, iy // 4)

    def device(axis, step, flip):
        r = list(q)
        if step:
            r[axis] = (r[axis] + step) % 4
        c = (core + flip) % 2 if flip else core
        return (r[0] * 2 + c, r[2] * 4 + r[1])

    def around(dy, dx):
        return ((ix + dx + 8) % 8, (iy + dy + 16) % 16)

    barrier = pltpu.get_barrier_semaphore()
    peers = [device(0, 0, 1)]
    for axis in range(3):
        for step, flip in MEMBERS[:6]:
            peers.append(device(axis, step, flip))
    for dy, dx in AROUND:
        peers.append(around(dy, dx))
    for peer in peers:
        pl.semaphore_signal(barrier, inc=1, device_id=peer, device_id_type=MESH)

    tin_copies = {}
    for b in ORDER:
        tin_copies[b] = pltpu.make_async_copy(tiles_hbm.at[b], tin.at[b], tin_sem.at[b])
        tin_copies[b].start()

    own = own_ref[...]
    ox, oy = own // 16, own % 16
    oq = (ox // 2, oy % 4, oy // 4)
    oc = ox % 2
    ownf = jnp.broadcast_to(own.astype(F32), (128, 128))
    same = ownf == ownf.T
    earlier = lax.broadcasted_iota(jnp.int32, (128, 128), 0) < lax.broadcasted_iota(
        jnp.int32, (128, 128), 1
    )
    rank = jnp.sum(jnp.where(same & earlier, 1.0, 0.0), axis=0, keepdims=True).astype(jnp.int32)
    rows = lax.broadcasted_iota(jnp.int32, (256, 128), 0)
    for p in range(3):
        slot = (oq[p] * 2 + oc) * 32 + (oq[(p + 1) % 3] * 4 + oq[(p + 2) % 3]) * 2 + rank
        sel[p] = jnp.where(rows == slot, 1.0, 0.0).astype(BF16)
    meta[...] = jnp.zeros((128, 128), F32)
    meta[0:6, :] = wt_ref[...].astype(F32)
    meta[6:7, :] = cell_ref[...].astype(F32) + 1.0

    s1 = {}

    def stage1_refs(b):
        p, k = b // 2, b % 2
        return (send_a.at[p], recv_a.at[p]) if k == 0 else (send_b.at[p], recv_b.at[p])

    for n, b in enumerate(ORDER):
        p, k = b // 2, b % 2
        src, dst = stage1_refs(b)
        tin_copies[b].wait()

        def gather(c, carry, b=b, p=p, src=src):
            at = pl.ds(pl.multiple_of(c * 512, 512), 512)
            src[:, at] = jnp.dot(sel[p], tin[b, :, at], preferred_element_type=F32).astype(BF16)
            return carry

        lax.fori_loop(0, 8, gather, 0)
        if k == 0:
            src[:, 4096:4224] = lax.dot_general(
                sel[p],
                meta[...].astype(BF16),
                (((1,), (1,)), ((), ())),
                preferred_element_type=F32,
            ).astype(BF16)
        if n == 0:
            pl.semaphore_wait(barrier, len(peers))
        mine = q[p] * 2 + core
        mine_rows = pl.ds(pl.multiple_of(mine * 32, 32), 32)
        own_copy = pltpu.make_async_copy(src.at[mine_rows], dst.at[mine_rows], self_sem.at[b])
        own_copy.start()
        copies = [own_copy]
        for m, (step, flip) in enumerate(MEMBERS):
            there = ((q[p] + step) % 4) * 2 + (core + flip) % 2
            copy = pltpu.make_async_remote_copy(
                src_ref=src.at[pl.ds(pl.multiple_of(there * 32, 32), 32)],
                dst_ref=dst.at[mine_rows],
                send_sem=s1_send.at[b, m],
                recv_sem=s1_recv.at[b, m],
                device_id=device(p, step, flip),
                device_id_type=MESH,
            )
            copy.start()
            copies.append(copy)
        s1[b] = copies

    s2, s3 = {}, {}

    def encode(values, denom, size):
        top = jnp.max(jnp.abs(values), axis=1, keepdims=True)
        some = top > 1e-30
        inverse = jnp.where(some, 32767.0 / jnp.where(some, top, 1.0), 0.0)
        codes = (values * inverse + 32768.5).astype(jnp.int32)
        words = codes[:, :QUARTER] | (codes[:, QUARTER:] << 16)
        lane = lax.broadcasted_iota(jnp.int32, (size, 128), 1)
        return words, jnp.where(lane < 64, denom, top * (1.0 / 32767.0))

    def decode(words, extra):
        step = extra[:, 64:65]
        low = (words & 65535).astype(F32) - 32768.0
        high = lax.shift_right_logical(words, jnp.full_like(words, 16)).astype(F32) - 32768.0
        return low * step, high * step

    def gathered(own, own_denom, words, extras):
        low, high, denom = own[:, :QUARTER], own[:, QUARTER:], own_denom
        for k in range(3):
            a, c = decode(words[k], extras[k])
            low, high, denom = low + a, high + c, denom + extras[k][:, 0:1]
        return low, high, denom

    def pass_on(b, axis, size, words, extras, to_words, to_extras, send, recv):
        copies = []
        for step in (2, 1, 3):
            there = (q[axis] + step) % 4
            at = pl.ds(pl.multiple_of(there * size, size), size)
            for n, (src, dst) in enumerate(((words, to_words), (extras, to_extras))):
                copy = pltpu.make_async_remote_copy(
                    src_ref=src.at[b, at],
                    dst_ref=dst.at[b, step - 1],
                    send_sem=send.at[b, step - 1, n],
                    recv_sem=recv.at[b, step - 1, n],
                    device_id=device(axis, step, 0),
                    device_id_type=MESH,
                )
                copy.start()
                copies.append(copy)
        return copies

    def reduce_tiles(b):
        p, k = b // 2, b % 2
        src, dst = stage1_refs(b)
        s1[b][0].wait()
        for copy in s1[b][1:]:
            copy.wait_recv()
        if k == 0:
            metar[p] = dst[:, 4096:4224].astype(F32).T[0:8, :]
        w = metar[p, b : b + 1, :]
        code = metar[p, 6:7, :].astype(jnp.int32)
        row = lax.broadcasted_iota(jnp.int32, (128, 256), 0)
        col = lax.broadcasted_iota(jnp.int32, (128, 256), 1)
        hit = ((col % 32) // 2 == row // 8) & (code == row % 4 + 1)
        upper = (row // 4) % 2 == 0
        both = jnp.where(hit, jnp.broadcast_to(w, (128, 256)), 0.0)
        c0 = jnp.where(upper, both, 0.0).astype(BF16)
        c1 = jnp.where(upper, 0.0, both).astype(BF16)
        denom = jnp.sum(both, axis=1, keepdims=True)

        def reduce(c, carry):
            lo = pl.ds(pl.multiple_of(c * 512, 512), 512)
            hi = pl.ds(pl.multiple_of(c * 512 + HALF, 512), 512)
            acc2[b, :, lo] = jnp.dot(c0, dst[:, lo], preferred_element_type=F32) + jnp.dot(
                c1, dst[:, hi], preferred_element_type=F32
            )
            return carry

        lax.fori_loop(0, 4, reduce, 0)
        st2[b], st2m[b] = encode(acc2[b], denom, 128)
        s2[b] = pass_on(b, (p + 1) % 3, 32, st2, st2m, rcv2, rcv2m, s2_send, s2_recv)

    def second(b):
        p = b // 2
        for copy in s2[b]:
            copy.wait_recv()
        at = pl.ds(pl.multiple_of(q[(p + 1) % 3] * 32, 32), 32)
        low, high, denom = gathered(acc2[b, at, :], st2m[b, at, 0:1], rcv2[b], rcv2m[b])
        acc3[b, :, :QUARTER] = low
        acc3[b, :, QUARTER:] = high
        st3[b], st3m[b] = encode(acc3[b], denom, 32)
        s3[b] = pass_on(b, (p + 2) % 3, 8, st3, st3m, rcv3, rcv3m, s3_send, s3_recv)

    left_half = lax.broadcasted_iota(jnp.int32, (16, 128), 1) < 64

    def third(b):
        p = b // 2
        axis = (p + 2) % 3
        for copy in s3[b]:
            copy.wait_recv()
        at = pl.ds(pl.multiple_of(q[axis] * 8, 8), 8)
        low, high, denom = gathered(acc3[b, at, :], st3m[b, at, 0:1], rcv3[b], rcv3m[b])
        scale = 1.0 / (1.0 + denom)
        for j in range(8):
            c = slice(128 * j, 128 * j + 128)
            tbuf[pl.ds(j, 8, stride=16), :] = low[:, c] * scale
            tbuf[pl.ds(j + 8, 8, stride=16), :] = high[:, c] * scale
        for h in range(2):
            for cy in range(2):
                s = h * 4 + cy * 2
                a = tbuf[16 * s : 16 * s + 16, :]
                c = tbuf[16 * s + 16 : 16 * s + 32, :]
                y0 = 64 * cy + 32 * h
                out_ref[pl.ds(128 * b + y0, 16, stride=2), :] = jnp.where(
                    left_half, a, pltpu.roll(c, 64, 1)
                )
                out_ref[pl.ds(128 * b + y0 + 1, 16, stride=2), :] = jnp.where(
                    left_half, pltpu.roll(a, 64, 1), c
                )
        r = 128 * b
        n = ORDER.index(b)
        hsend[0, n] = out_ref[r : r + 8, :]
        hsend[1, n] = out_ref[r + 120 : r + 128, :]
        turned = out_ref[r : r + 128, :].T
        hsend[2, n] = turned[0:8, :]
        hsend[3, n] = turned[120:128, :]
        out_ref[1152 + 8 * b : 1160 + 8 * b, :] = turned[0:8, :]
        out_ref[1200 + 8 * b : 1208 + 8 * b, :] = turned[120:128, :]

    halo = []

    def send_halo(group):
        bands = pl.ds(3 * group, 3)
        for n, (dy, dx) in enumerate(AROUND):
            which = 0 if dy < 0 else 1 if dy > 0 else 2 if dx < 0 else 3
            copy = pltpu.make_async_remote_copy(
                src_ref=hsend.at[which, bands],
                dst_ref=hrecv.at[n, bands],
                send_sem=h_send.at[group, n],
                recv_sem=h_recv.at[group, n],
                device_id=around(dy, dx),
                device_id_type=MESH,
            )
            copy.start()
            halo.append(copy)

    for n in range(6 + 4):
        if n < 6:
            reduce_tiles(ORDER[n])
        if 0 <= n - 2 < 6:
            second(ORDER[n - 2])
        if 0 <= n - 4 < 6:
            third(ORDER[n - 4])
            if n - 4 in (2, 5):
                send_halo((n - 4) // 3)

    for b in ORDER:
        for copy in s1[b][1:] + s2[b] + s3[b]:
            copy.wait_send()
    for n, copy in enumerate(halo):
        copy.wait_recv()
        group, slot = n // 8, n % 8
        for k in range(3):
            r = 768 + 48 * slot + 8 * ORDER[3 * group + k]
            out_ref[r : r + 8, :] = hrecv[slot, 3 * group + k]
    out_ref[1248:1256, :] = jnp.zeros((8, 128), F32)
    for copy in halo:
        copy.wait_send()


def full_exchange(tiles, weights, owners, cells):
    vmem = pl.BlockSpec(memory_space=pltpu.VMEM)
    dma = pltpu.SemaphoreType.DMA
    return pl.pallas_call(
        full_exchange_kernel,
        out_shape=jax.ShapeDtypeStruct((1256, 128), F32),
        in_specs=[pl.BlockSpec(memory_space=pl.ANY), vmem, vmem, vmem],
        out_specs=vmem,
        scratch_shapes=[
            pltpu.VMEM((NB, 128, 4096), BF16),
            pltpu.VMEM((3, 256, 128), BF16),
            pltpu.VMEM((128, 128), F32),
            pltpu.VMEM((3, 8, 256), F32),
            pltpu.VMEM((3, 256, 4224), BF16),
            pltpu.VMEM((3, 256, 4096), BF16),
            pltpu.VMEM((3, 256, 4224), BF16),
            pltpu.VMEM((3, 256, 4096), BF16),
            pltpu.VMEM((NB, 128, HALF), F32),
            pltpu.VMEM((NB, 128, QUARTER), jnp.int32),
            pltpu.VMEM((NB, 128, 128), F32),
            pltpu.VMEM((NB, 3, 32, QUARTER), jnp.int32),
            pltpu.VMEM((NB, 3, 32, 128), F32),
            pltpu.VMEM((NB, 32, HALF), F32),
            pltpu.VMEM((NB, 32, QUARTER), jnp.int32),
            pltpu.VMEM((NB, 32, 128), F32),
            pltpu.VMEM((NB, 3, 8, QUARTER), jnp.int32),
            pltpu.VMEM((NB, 3, 8, 128), F32),
            pltpu.VMEM((128, 128), F32),
            pltpu.VMEM((4, NB, 8, 128), F32),
            pltpu.VMEM((8, NB, 8, 128), F32),
            dma((NB,)),
            dma((NB,)),
            dma((NB, 7)),
            dma((NB, 7)),
            dma((NB, 3, 2)),
            dma((NB, 3, 2)),
            dma((NB, 3, 2)),
            dma((NB, 3, 2)),
            dma((2, 8)),
            dma((2, 8)),
        ],
        compiler_params=pltpu.CompilerParams(
            collective_id=1, has_side_effects=True, vmem_limit_bytes=60 * 1024 * 1024
        ),
        name="full_exchange",
    )(tiles, weights, owners, cells)


def detect_kernel(
    taps_ref,
    coadd_hbm,
    w1_ref,
    b1_ref,
    w2_ref,
    b2_ref,
    psf_hbm,
    det_hbm,
    coadd_ref,
    psf_out,
    det_out,
    partial,
    ext,
    shifted,
    sides,
    sides_t,
    psf,
    taps3,
    edge3,
    hidden,
    turned,
    small,
    beside,
    w2s,
    sems,
):
    ix = lax.axis_index("skyx")
    iy = lax.axis_index("skyy")
    top, bottom = (iy > 0).astype(F32), (iy < 15).astype(F32)
    left, right = (ix > 0).astype(F32), (ix < 7).astype(F32)

    fetch = pltpu.make_async_copy(coadd_hbm, coadd_ref, sems.at[0])
    fetch.start()

    def halo(slot, b):
        r = 768 + slot * 48 + b * 8
        return coadd_ref[r : r + 8, :]

    def lanes_of(n):
        return lax.broadcasted_iota(jnp.int32, (n, 128), 1)

    small[...] = jnp.zeros((128, 128), F32)
    for b in range(NB):
        for i in range(3):
            small[pl.ds(i * 24 + b, 3, stride=8), 0:64] = w1_ref[b, i].astype(F32)
    w1 = (small[...].T[0:64, 0:72] * 0.5).astype(BF16)
    for i in range(3):
        for j in range(3):
            at = 64 * (3 * i + j)
            w2s[:, at : at + 64] = w2_ref[i, j]
    small[0:1, 0:64] = b1_ref[...] * 0.5
    small[1:2, 0:64] = b2_ref[...]
    columns = small[...].T
    bias1 = jnp.broadcast_to(columns[0:64, 0:1], (64, 256))
    bias2 = jnp.broadcast_to(columns[0:64, 1:2], (64, 256))

    taps3[...] = jnp.zeros_like(taps3)
    fetch.wait()

    pieces = []
    for b in range(NB):
        pieces += [
            halo(3, b)[2:8] * left,
            halo(8, b)[0:4],
            halo(9, b)[4:8],
            halo(2, b)[0:6] * right,
        ]
    pieces.append(jnp.zeros((8, 128), F32))
    sides[8:136, :] = jnp.concatenate(pieces, axis=0).T
    lane8 = lanes_of(8)
    for r, mid, at_left, at_right, keep in ((0, 1, 7, 6, top), (136, 0, 5, 4, bottom)):
        line = jnp.zeros((8, 128), F32)
        for b in range(NB):
            middle = halo(mid, b)
            parts = (
                (halo(at_left, b) * left, 122, 0, 6),
                (middle, 0, 6, 4),
                (middle, 124, 10, 4),
                (halo(at_right, b) * right, 0, 14, 6),
            )
            for value, start, at, size in parts:
                at = 20 * b + at
                moved = pltpu.roll(value, (at - start) % 128, 1)
                line = jnp.where((lane8 >= at) & (lane8 < at + size), moved, line)
        sides[r : r + 8, :] = line * keep

    for j in range(9):
        shifted[j] = pltpu.roll(sides[...], (-j) % 128, 1) if j else sides[...]
    owner_band = lane8 // 20

    def edge_block(start, size):
        acc = jnp.zeros((size, 128), F32)
        for i in range(9):
            for j in range(9):
                tap = jnp.full((8, 128), taps_ref[i, 0, j], F32)
                for b in range(1, NB):
                    tap = jnp.where(owner_band == b, taps_ref[i, b, j], tap)
                tap = jnp.broadcast_to(tap[0:1], (size, 128))
                acc = acc + tap * shifted[j, start + i : start + i + size, :]
        at = lax.broadcasted_iota(jnp.int32, (size, 128), 0) + start
        keep = jnp.where(at < 4, top, jnp.where(at >= 132, bottom, 1.0))
        keep = keep * jnp.where(lanes_of(size) % 20 < 10, left, right)
        return acc.astype(BF16).astype(F32) * keep

    sides[0:136, :] = edge_block(0, 136)

    for b in range(NB):
        ext[b, 8:136, :] = coadd_ref[128 * b : 128 * b + 128, :]
        ext[b, 0:8, :] = halo(1, b) * top
        ext[b, 136:144, :] = halo(0, b) * bottom
    column = lanes_of(144)

    def band(b, carry):
        near_left = pltpu.roll(shifted[0], 122 - 20 * b, 1)
        near_right = pltpu.roll(shifted[0], 114 - 20 * b, 1)
        x = ext[b]
        for j in range(9):
            if j < 4:
                moved = pltpu.roll(jnp.where(column >= 124 + j, near_left, x), 4 - j, 1)
            elif j == 4:
                moved = x
            else:
                moved = pltpu.roll(jnp.where(column < j - 4, near_right, x), 132 - j, 1)
            shifted[j + 1] = moved

        for n in range(6):
            at_rows = slice(24 * n, 24 * n + 24)
            sums = [None] * 9
            for j in range(9):
                value = shifted[j + 1, at_rows, :]
                for i in range(9):
                    term = taps_ref[i, b, j] * value
                    sums[i] = term if j == 0 else sums[i] + term
            for i in range(9):
                partial[i, at_rows, :] = sums[i]

        def block(start, size):
            acc = partial[0, start : start + size, :]
            for i in range(1, 9):
                acc = acc + partial[i, start + i : start + i + size, :]
            at = lax.broadcasted_iota(jnp.int32, (size, 128), 0) + start
            keep = jnp.where(at < 4, top, jnp.where(at >= 132, bottom, 1.0))
            v = acc.astype(BF16).astype(F32) * keep
            psf[start : start + size, :] = v
            lane = lanes_of(size)
            edge = sides[start : start + size, :]
            before = jnp.where(lane == 0, pltpu.roll(edge, 127 - 20 * b, 1), pltpu.roll(v, 1, 1))
            after = jnp.where(
                lane == 127, pltpu.roll(edge, 117 - 20 * b, 1), pltpu.roll(v, 127, 1)
            )
            for j, value in enumerate((before, v, after)):
                taps3[pl.ds(start * 24 + 8 * j + b, size, stride=24), :] = value
            edge = jnp.where(lane == 20 * b + 2, pltpu.roll(v, 20 * b + 2, 1), edge)
            edge = jnp.where(lane == 20 * b + 9, pltpu.roll(v, 20 * b + 10, 1), edge)
            sides[start : start + size, :] = edge

        block(0, 72)
        block(72, 64)
        psf_out[b] = psf[4:132, :].astype(BF16)
        return carry

    lax.fori_loop(0, NB, band, 0)

    psf_copy = pltpu.make_async_copy(psf_out, psf_hbm, sems.at[1])
    psf_copy.start()

    def silu(u):
        return u + u * jnp.tanh(u)

    sides_t[0] = sides[0:128, :].T
    tail = jnp.concatenate([sides[128:136, :], jnp.zeros((120, 128), F32)], axis=0)
    sides_t[1] = tail.T
    edge3[...] = jnp.zeros_like(edge3)
    at256 = lax.broadcasted_iota(jnp.int32, (64, 256), 1)
    ends = jnp.where(at256 == 0, top, jnp.where(at256 == 129, bottom, 1.0))
    for side, (offset, keep) in enumerate(((0, left), (9, right))):
        for t in range(2):
            for j in range(3):
                edge3[side, 8 * j : 8 * j + 6, 128 * t : 128 * t + 128] = sides_t[
                    t, pl.ds(offset + j, 6, stride=20), :
                ]
        x = edge3[side]
        rhs = jnp.concatenate([pltpu.roll(x, 256 - (2 + i), 1) for i in range(3)], axis=0)
        v = silu(jnp.dot(w1, rhs.astype(BF16), preferred_element_type=F32) + bias1)
        v = v * (ends * keep)
        beside[side, 0] = v[:, 0:128]
        beside[side, 1] = v[:, 128:256]

    lane64 = lanes_of(64)

    def pair(n, t):
        at0 = pl.ds(pl.multiple_of((2 * n + 2) * 24, 8), 72)
        at1 = pl.ds(pl.multiple_of((2 * n + 3) * 24, 8), 72)
        rhs = jnp.concatenate([taps3[at0, :], taps3[at1, :]], axis=1).astype(BF16)
        v = silu(jnp.dot(w1, rhs, preferred_element_type=F32) + bias1)
        for k in range(2):
            row, h = 2 * n + k, v[:, 128 * k : 128 * k + 128]
            near = pltpu.roll(beside[0, t], 128 * (t + 1) - row, 1)
            far = pltpu.roll(beside[1, t], 128 * (t + 1) - 1 - row, 1)
            hidden[row, 0:64] = jnp.where(lane64 == 0, near, pltpu.roll(h, 1, 1)).astype(BF16)
            hidden[row, 64:128] = h.astype(BF16)
            hidden[row, 128:192] = jnp.where(lane64 == 127, far, pltpu.roll(h, 127, 1)).astype(
                BF16
            )

    def first(n, carry):
        pair(n, 0)
        return carry

    lax.fori_loop(0, 64, first, 0, unroll=32)
    pair(64, 1)
    hidden[0] = (hidden[0].astype(F32) * top).astype(BF16)
    hidden[129] = (hidden[129].astype(F32) * bottom).astype(BF16)

    w2 = w2s[...]

    def leave(g):
        at = pl.ds(pl.multiple_of(g * 16, 16), 16)
        return pltpu.make_async_copy(det_out.at[g], det_hbm.at[:, at], sems.at[2 + g])

    def group(g, carry):
        def rows(n, inner):
            y = g * 16 + 2 * n
            rhs = jnp.concatenate(
                [hidden[pl.ds(y, 3)].reshape(576, 128), hidden[pl.ds(y + 1, 3)].reshape(576, 128)],
                axis=1,
            )
            z = jnp.dot(w2, rhs, preferred_element_type=F32) + bias2
            turned[pl.ds(2 * n, 64, stride=16), :] = z[:, 0:128]
            turned[pl.ds(2 * n + 1, 64, stride=16), :] = z[:, 128:256]
            return inner

        lax.fori_loop(0, 8, rows, 0, unroll=8)
        det_out[g] = turned[...].reshape(64, 16, 128).astype(BF16)
        leave(g).start()
        return carry

    lax.fori_loop(0, 8, group, 0)
    psf_copy.wait()
    for g in range(8):
        leave(g).wait()


def detect(taps, coadd, w1, b1, w2, b2):
    vmem = pl.BlockSpec(memory_space=pltpu.VMEM)
    anywhere = pl.BlockSpec(memory_space=pl.ANY)
    return pl.pallas_call(
        detect_kernel,
        out_shape=(
            jax.ShapeDtypeStruct((NB, 128, 128), BF16),
            jax.ShapeDtypeStruct((64, 128, 128), BF16),
        ),
        in_specs=[pl.BlockSpec(memory_space=pltpu.SMEM), anywhere] + [vmem] * 4,
        out_specs=(anywhere, anywhere),
        scratch_shapes=[
            pltpu.VMEM((1256, 128), F32),
            pltpu.VMEM((NB, 128, 128), BF16),
            pltpu.VMEM((8, 64, 16, 128), BF16),
            pltpu.VMEM((9, 144, 128), F32),
            pltpu.VMEM((NB, 144, 128), F32),
            pltpu.VMEM((10, 144, 128), F32),
            pltpu.VMEM((144, 128), F32),
            pltpu.VMEM((2, 128, 128), F32),
            pltpu.VMEM((136, 128), F32),
            pltpu.VMEM((136 * 24, 128), F32),
            pltpu.VMEM((2, 24, 256), F32),
            pltpu.VMEM((130, 192, 128), BF16),
            pltpu.VMEM((64 * 16, 128), F32),
            pltpu.VMEM((128, 128), F32),
            pltpu.VMEM((2, 2, 64, 128), F32),
            pltpu.VMEM((64, 576), BF16),
            pltpu.SemaphoreType.DMA((10,)),
        ],
        compiler_params=pltpu.CompilerParams(vmem_limit_bytes=48 * 1024 * 1024),
        name="detect",
    )(taps, coadd, w1, b1, w2, b2)


def body(
    tiles,
    tile_weight,
    owners,
    cells,
    psf_kernel,
    conv1_weight,
    conv1_bias,
    conv2_weight,
    conv2_bias,
):
    operands = (
        tiles.transpose(1, 0, 2),
        tile_weight.transpose(1, 0),
        owners.reshape(1, 128),
        cells.reshape(1, 128),
    )
    coadd = exchange(*operands)
    coadd = lax.cond(coadd[1248, 0] > 0.5, lambda: full_exchange(*operands), lambda: coadd)
    return detect(
        psf_kernel.transpose(1, 0, 2),
        coadd,
        conv1_weight.transpose(1, 2, 3, 0),
        conv1_bias.reshape(1, 64),
        conv2_weight.transpose(2, 3, 0, 1),
        conv2_bias.reshape(1, 64),
    )


def solution(mesh):
    in_specs = (
        P(("skyx", "skyy"), None, None),
        P(("skyx", "skyy"), None),
        P(("skyx", "skyy"), None),
        P(("skyx", "skyy")),
        P(),
        P(),
        P(),
        P(),
        P(),
    )
    out_specs = (P(None, "skyy", "skyx"), P(None, "skyy", "skyx"))
    return jax.shard_map(body, mesh=mesh, in_specs=in_specs, out_specs=out_specs, check_vma=False)
```

```python
import functools

import jax
import jax.numpy as jnp
from jax import lax
from jax.experimental import pallas as pl
from jax.experimental.pallas import tpu as pltpu
from jax.sharding import PartitionSpec as P

MESH = pl.DeviceIdType.MESH
F32 = jnp.float32
BF16 = jnp.bfloat16

NB = 6
HALF = 2048
QUARTER = 1024
WIDE = HALF + 128
PIECES = ((0, 0, 2048), (1, 0, 2048))
UNITS = 3 * len(PIECES)
LAGS = (0, 3, 5, 6)
ORDER = (0, 2, 4, 1, 3, 5)
MEMBERS = ((2, 0), (2, 1), (1, 0), (3, 0), (1, 1), (3, 1), (0, 1))
AROUND = ((-1, 0), (1, 0), (0, -1), (0, 1), (-1, -1), (-1, 1), (1, -1), (1, 1))


def encode(values, denom, flag, size):
    top = jnp.max(jnp.abs(values), axis=1, keepdims=True)
    some = top > 1e-30
    inverse = jnp.where(some, 32767.0 / jnp.where(some, top, 1.0), 0.0)
    codes = (values * inverse + 32768.5).astype(jnp.int32)
    middle = values.shape[1] // 2
    words = codes[:, :middle] | (codes[:, middle:] << 16)
    lane = lax.broadcasted_iota(jnp.int32, (size, 128), 1)
    extra = jnp.where(lane < 64, denom, top * (1.0 / 32767.0))
    return words, jnp.where(lane == 127, flag, extra)


def decode(words, extra):
    step = extra[:, 64:65]
    low = (words & 65535).astype(F32) - 32768.0
    high = lax.shift_right_logical(words, jnp.full_like(words, 16)).astype(F32) - 32768.0
    return low * step, high * step


def gathered(own, own_extra, words, extras):
    middle = own.shape[1] // 2
    low, high = own[:, :middle], own[:, middle:]
    denom, flag = own_extra[:, 0:1], own_extra[:, 127:128]
    for k in range(3):
        a, c = decode(words[k], extras[k])
        low, high, denom = low + a, high + c, denom + extras[k][:, 0:1]
        flag = jnp.maximum(flag, extras[k][:, 127:128])
    return low, high, denom, jnp.max(flag, axis=0, keepdims=True)


def exchange_kernel(
    tiles_hbm,
    wt_ref,
    own_ref,
    cell_ref,
    out_ref,
    tin,
    sel,
    selx,
    meta,
    send_lo,
    send_hi,
    send_x,
    recv_lo,
    recv_hi,
    recv_x,
    acc2,
    st2,
    st2m,
    rcv2,
    rcv2m,
    acc3,
    st3,
    st3m,
    rcv3,
    rcv3m,
    tbuf,
    rbuf,
    hsend,
    hrecv,
    tin_sem,
    self_sem,
    s1_send,
    s1_recv,
    x_send,
    x_recv,
    s2_send,
    s2_recv,
    s3_send,
    s3_recv,
    c_send,
    c_recv,
    h_send,
    h_recv,
):
    ix = lax.axis_index("skyx")
    iy = lax.axis_index("skyy")
    core = ix % 2
    q = (ix // 2, iy % 4, iy // 4)

    def device(axis, step, flip):
        r = list(q)
        if step:
            r[axis] = (r[axis] + step) % 4
        c = (core + flip) % 2 if flip else core
        return (r[0] * 2 + c, r[2] * 4 + r[1])

    def around(dy, dx):
        return ((ix + dx + 8) % 8, (iy + dy + 16) % 16)

    barrier = pltpu.get_barrier_semaphore()
    peers = [device(0, 0, 1)]
    for axis in range(3):
        for step, flip in MEMBERS[:6]:
            peers.append(device(axis, step, flip))
    for dy, dx in AROUND:
        peers.append(around(dy, dx))
    for peer in peers:
        pl.semaphore_signal(barrier, inc=1, device_id=peer, device_id_type=MESH)

    tin_copies = []
    for b in range(NB):
        tin_copies.append(pltpu.make_async_copy(tiles_hbm.at[b], tin.at[b], tin_sem.at[b]))
        tin_copies[b].start()

    own = own_ref[...]
    ox, oy = own // 16, own % 16
    oq = (ox // 2, oy % 4, oy // 4)
    oc = ox % 2
    earlier = lax.broadcasted_iota(jnp.int32, (128, 128), 0) < lax.broadcasted_iota(
        jnp.int32, (128, 128), 1
    )
    rows = lax.broadcasted_iota(jnp.int32, (128, 128), 0)
    rows_x = lax.broadcasted_iota(jnp.int32, (64, 128), 0)
    lane128 = lax.broadcasted_iota(jnp.int32, (128, 128), 1)
    meta[...] = jnp.zeros((128, 128), F32)
    meta[0:6, :] = wt_ref[...].astype(F32)

    def select(p):
        group = jnp.broadcast_to(oq[p].astype(F32), (128, 128))
        rank = jnp.sum(
            jnp.where((group == group.T) & earlier, 1.0, 0.0), axis=0, keepdims=True
        )
        over = jnp.where(jnp.max(rank, axis=1, keepdims=True) > 39.5, 1.0, 0.0)
        rank = rank.astype(jnp.int32)
        slot = jnp.where(rank < 32, oq[p] * 32 + rank, -1)
        sel[p, 0:128] = jnp.where(rows == slot, 1.0, 0.0).astype(BF16)
        slot = jnp.where((rank >= 32) & (rank < 40), oq[p] * 16 + rank - 32, -64)
        sel[p, 128:192] = jnp.where(rows_x == slot, 1.0, 0.0).astype(BF16)
        selx[p] = jnp.where(rows_x == slot + 8, 1.0, 0.0).astype(BF16)
        unit = oq[(p + 1) % 3] * 4 + oq[(p + 2) % 3]
        meta[6:7, :] = ((unit * 2 + oc) * 4 + cell_ref[...] + 1).astype(F32)
        both = pick_meta(sel[p])
        extra = both[128:192] + pick_meta(selx[p])
        return jnp.where(lane128 == 7, over, both[0:128]).astype(BF16), extra.astype(BF16)

    def pick(which, value):
        return jnp.dot(which, value, preferred_element_type=F32)

    def pick_meta(which):
        return lax.dot_general(
            which,
            meta[...].astype(BF16),
            (((1,), (1,)), ((), ())),
            preferred_element_type=F32,
        )

    s1 = {}
    for n in range(UNITS):
        p, (half, first, width) = n % 3, PIECES[n // 3]
        if half == 0:
            flagged, extra = select(p)
        for k in range(2):
            b = 2 * p + k
            if half == 0:
                tin_copies[b].wait()

            def gather(c, carry, b=b, p=p, k=k, half=half, first=first):
                at = pl.ds(pl.multiple_of(c * 512 + first, 512), 512)
                there = pl.ds(pl.multiple_of(c * 512 + first + HALF, 512), 512)
                if half == 0:
                    both = pick(sel[p], tin[b, :, at])
                    send_lo[p, k, :, at] = both[0:128].astype(BF16)
                    send_x[p, k, :, at] = (
                        both[128:192] + pick(selx[p], tin[b, :, there])
                    ).astype(BF16)
                else:
                    send_hi[p, k, :, at] = pick(sel[p, 0:128], tin[b, :, there]).astype(BF16)
                return carry

            lax.fori_loop(0, width // 512, gather, 0)
            if half == 0:
                send_lo[p, k, :, HALF:WIDE] = flagged
                send_x[p, k, :, HALF:WIDE] = extra
        if n == 0:
            pl.semaphore_wait(barrier, len(peers))
        mine = q[p] * 2 + core
        streams = [(send_hi, recv_hi, 32, pl.ds(first, width), s1_send, s1_recv)]
        if half == 0:
            streams = [
                (send_lo, recv_lo, 32, pl.ds(0, WIDE), s1_send, s1_recv),
                (send_x, recv_x, 16, pl.ds(0, WIDE), x_send, x_recv),
            ]
        local, away = [], []
        for m, (step, flip) in enumerate(MEMBERS + ((0, 0),)):
            to = (q[p] + step) % 4
            parity = (core + flip) % 2
            for w, (src, dst, size, columns, sends, recvs) in enumerate(streams):
                from_ref = src.at[p, parity, pl.ds(pl.multiple_of(to * size, size), size), columns]
                to_ref = dst.at[p, pl.ds(pl.multiple_of(mine * size, size), size), columns]
                if (step, flip) == (0, 0):
                    copy = pltpu.make_async_copy(from_ref, to_ref, self_sem.at[n, w])
                    local.append(copy)
                else:
                    at = n if size == 32 else p
                    copy = pltpu.make_async_remote_copy(
                        src_ref=from_ref,
                        dst_ref=to_ref,
                        send_sem=sends.at[at, m],
                        recv_sem=recvs.at[at, m],
                        device_id=device(p, step, flip),
                        device_id_type=MESH,
                    )
                    away.append(copy)
                copy.start()
        s1[n] = (local, away)

    s2, s3, s4 = {}, {}, {}

    def pass_on(n, axis, size, words, extras, to_words, to_extras, send, recv):
        copies = []
        half, first, width = PIECES[n // 3]
        m, columns = 3 * half + n % 3, pl.ds(first // 2, width // 2)
        for step in (2, 1, 3):
            there = (q[axis] + step) % 4
            at = pl.ds(pl.multiple_of(there * size, size), size)
            pairs = (
                (words.at[m, at, columns], to_words.at[m, step - 1, :, columns]),
                (extras.at[n, at], to_extras.at[n, step - 1]),
            )
            for w, (from_ref, to_ref) in enumerate(pairs):
                copy = pltpu.make_async_remote_copy(
                    src_ref=from_ref,
                    dst_ref=to_ref,
                    send_sem=send.at[n, step - 1, w],
                    recv_sem=recv.at[n, step - 1, w],
                    device_id=device(axis, step, 0),
                    device_id_type=MESH,
                )
                copy.start()
                copies.append(copy)
        return copies

    weighted = {}

    def coefficients(p):
        m = recv_lo[p, :, HALF:WIDE].astype(F32).T
        mx = recv_x[p, :, HALF:WIDE].astype(F32).T
        w = jnp.where(core == 0, m[2 * p : 2 * p + 1], m[2 * p + 1 : 2 * p + 2])
        wx = jnp.where(core == 0, mx[2 * p : 2 * p + 1], mx[2 * p + 1 : 2 * p + 2])
        at = lax.broadcasted_iota(jnp.int32, (128, 256), 0).astype(F32) + 1.0
        c = jnp.where(m[6:7] == at, jnp.broadcast_to(w, (128, 256)), 0.0)
        cx = jnp.where(mx[6:7] == at[:, 0:128], jnp.broadcast_to(wx, (128, 128)), 0.0)
        low = (lane128 // 8) % 2 == 0
        x0, x1 = jnp.where(low, cx, 0.0), jnp.where(low, 0.0, cx)
        denom = jnp.sum(c, axis=1, keepdims=True) + jnp.sum(x0, axis=1, keepdims=True)
        flag = jnp.max(m[7:8], axis=1, keepdims=True)
        return c.astype(BF16), x0.astype(BF16), x1.astype(BF16), denom, flag

    def reduce_tiles(n):
        p, (half, first, width) = n % 3, PIECES[n // 3]
        m = 3 * half + p
        for copy in s1[n][0]:
            copy.wait()
        for copy in s1[n][1]:
            copy.wait_recv()
        if half == 0:
            weighted[p] = coefficients(p)
        c, x0, x1, denom, flag = weighted[p]
        src = recv_lo if half == 0 else recv_hi
        cx = x0 if half == 0 else x1

        def reduce(i, carry):
            at = pl.ds(pl.multiple_of(i * 512 + first, 512), 512)
            acc2[m, :, at] = pick(c, src[p, :, at]) + pick(cx, recv_x[p, :, at])
            return carry

        lax.fori_loop(0, width // 512, reduce, 0, unroll=2)
        words, extra = encode(acc2[m, :, first : first + width], denom, flag, 128)
        st2[m, :, first // 2 : (first + width) // 2] = words
        st2m[n] = extra
        s2[n] = pass_on(n, (p + 1) % 3, 32, st2, st2m, rcv2, rcv2m, s2_send, s2_recv)

    def second(n):
        p, (half, first, width) = n % 3, PIECES[n // 3]
        m, columns = 3 * half + p, slice(first // 2, (first + width) // 2)
        for copy in s2[n]:
            copy.wait_recv()
        at = pl.ds(pl.multiple_of(q[(p + 1) % 3] * 32, 32), 32)
        low, high, denom, flag = gathered(
            acc2[m, at, first : first + width],
            st2m[n, at, :],
            rcv2[m, :, :, columns],
            rcv2m[n],
        )
        middle = first + width // 2
        acc3[m, :, first:middle] = low
        acc3[m, :, middle : first + width] = high
        st3[m, :, columns], st3m[n] = encode(acc3[m, :, first : first + width], denom, flag, 32)
        s3[n] = pass_on(n, (p + 2) % 3, 8, st3, st3m, rcv3, rcv3m, s3_send, s3_recv)

    def third(n):
        p, (half, first, width) = n % 3, PIECES[n // 3]
        m, columns = 3 * half + p, slice(first // 2, (first + width) // 2)
        for copy in s3[n]:
            copy.wait_recv()
        at = pl.ds(pl.multiple_of(q[(p + 2) % 3] * 8, 8), 8)
        low, high, denom, flag = gathered(
            acc3[m, at, first : first + width],
            st3m[n, at, :],
            rcv3[m, :, :, columns],
            rcv3m[n],
        )
        if n < 3:
            flag = jnp.broadcast_to(flag, (8, 128))
            out_ref[1248:1256, :] = jnp.maximum(out_ref[1248:1256, :], flag) if n else flag
        scale = 1.0 / (1.0 + denom)
        lines = width // 128
        for j in range(lines // 2):
            c = slice(128 * j, 128 * j + 128)
            tbuf[n, pl.ds(j, 8, stride=lines), :] = low[:, c] * scale
            tbuf[n, pl.ds(j + lines // 2, 8, stride=lines), :] = high[:, c] * scale
        size = 4 * lines
        s4[n] = pltpu.make_async_remote_copy(
            src_ref=tbuf.at[n, pl.ds(pl.multiple_of((1 - core) * size, size), size)],
            dst_ref=rbuf.at[n, pl.ds(0, size)],
            send_sem=c_send.at[n],
            recv_sem=c_recv.at[n],
            device_id=device(0, 0, 1),
            device_id_type=MESH,
        )
        s4[n].start()

    halo = []

    def place(value, band, row):
        lines = value.shape[0] // 4
        left_half = lax.broadcasted_iota(jnp.int32, (lines, 128), 1) < 64
        for cy in range(2):
            r = 2 * cy * lines
            a, c = value[r : r + lines], value[r + lines : r + 2 * lines]
            y0 = band * 128 + 64 * cy + row
            out_ref[pl.ds(y0, lines, stride=2), :] = jnp.where(
                left_half, a, pltpu.roll(c, 64, 1)
            )
            out_ref[pl.ds(y0 + 1, lines, stride=2), :] = jnp.where(
                left_half, pltpu.roll(a, 64, 1), c
            )

    def fourth(n):
        p, (half, first, width) = n % 3, PIECES[n // 3]
        row, size = (half * HALF + first) // 64, width // 32
        place(tbuf[n, pl.ds(pl.multiple_of(core * size, size), size), :], 2 * p + core, row)
        s4[n].wait_recv()
        place(rbuf[n, 0:size, :], 2 * p + 1 - core, row)
        if n < UNITS - 3:
            return
        for b in (2 * p, 2 * p + 1):
            r = 128 * b
            hsend[0, b] = out_ref[r : r + 8, :]
            hsend[1, b] = out_ref[r + 120 : r + 128, :]
            turned = out_ref[r : r + 128, :].T
            hsend[2, b] = turned[0:8, :]
            hsend[3, b] = turned[120:128, :]
            out_ref[1152 + 8 * b : 1160 + 8 * b, :] = turned[0:8, :]
            out_ref[1200 + 8 * b : 1208 + 8 * b, :] = turned[120:128, :]
        bands = pl.ds(2 * p, 2)
        for m, (dy, dx) in enumerate(AROUND):
            which = 0 if dy < 0 else 1 if dy > 0 else 2 if dx < 0 else 3
            copy = pltpu.make_async_remote_copy(
                src_ref=hsend.at[which, bands],
                dst_ref=hrecv.at[m, bands],
                send_sem=h_send.at[p, m],
                recv_sem=h_recv.at[p, m],
                device_id=around(dy, dx),
                device_id_type=MESH,
            )
            copy.start()
            halo.append(copy)

    steps = (reduce_tiles, second, third, fourth)
    for n in range(UNITS + LAGS[3] + 1):
        for lag, step in zip(LAGS, steps):
            if 0 <= n - lag < UNITS:
                step(n - lag)

    for n in range(UNITS):
        for copy in s1[n][1] + s2[n] + s3[n] + [s4[n]]:
            copy.wait_send()
    for n, copy in enumerate(halo):
        copy.wait_recv()
        p, slot = n // 8, n % 8
        r = 768 + 48 * slot + 16 * p
        out_ref[r : r + 16, :] = hrecv[slot, 2 * p : 2 * p + 2].reshape(16, 128)
    for copy in halo:
        copy.wait_send()


def exchange(tiles, weights, owners, cells):
    vmem = pl.BlockSpec(memory_space=pltpu.VMEM)
    dma = pltpu.SemaphoreType.DMA
    return pl.pallas_call(
        exchange_kernel,
        out_shape=jax.ShapeDtypeStruct((1256, 128), F32),
        in_specs=[pl.BlockSpec(memory_space=pl.ANY), vmem, vmem, vmem],
        out_specs=vmem,
        scratch_shapes=[
            pltpu.VMEM((NB, 128, 4096), BF16),
            pltpu.VMEM((3, 192, 128), BF16),
            pltpu.VMEM((3, 64, 128), BF16),
            pltpu.VMEM((128, 128), F32),
            pltpu.VMEM((3, 2, 128, WIDE), BF16),
            pltpu.VMEM((3, 2, 128, HALF), BF16),
            pltpu.VMEM((3, 2, 64, WIDE), BF16),
            pltpu.VMEM((3, 256, WIDE), BF16),
            pltpu.VMEM((3, 256, HALF), BF16),
            pltpu.VMEM((3, 128, WIDE), BF16),
            pltpu.VMEM((NB, 128, HALF), F32),
            pltpu.VMEM((NB, 128, QUARTER), jnp.int32),
            pltpu.VMEM((UNITS, 128, 128), F32),
            pltpu.VMEM((NB, 3, 32, QUARTER), jnp.int32),
            pltpu.VMEM((UNITS, 3, 32, 128), F32),
            pltpu.VMEM((NB, 32, HALF), F32),
            pltpu.VMEM((NB, 32, QUARTER), jnp.int32),
            pltpu.VMEM((UNITS, 32, 128), F32),
            pltpu.VMEM((NB, 3, 8, QUARTER), jnp.int32),
            pltpu.VMEM((UNITS, 3, 8, 128), F32),
            pltpu.VMEM((UNITS, 128, 128), F32),
            pltpu.VMEM((UNITS, 64, 128), F32),
            pltpu.VMEM((4, NB, 8, 128), F32),
            pltpu.VMEM((8, NB, 8, 128), F32),
            dma((NB,)),
            dma((UNITS, 2)),
            dma((UNITS, 7)),
            dma((UNITS, 7)),
            dma((3, 7)),
            dma((3, 7)),
            dma((UNITS, 3, 2)),
            dma((UNITS, 3, 2)),
            dma((UNITS, 3, 2)),
            dma((UNITS, 3, 2)),
            dma((UNITS,)),
            dma((UNITS,)),
            dma((3, 8)),
            dma((3, 8)),
        ],
        compiler_params=pltpu.CompilerParams(
            collective_id=0, has_side_effects=True, vmem_limit_bytes=60 * 1024 * 1024
        ),
        name="tile_exchange",
    )(tiles, weights, owners, cells)


def full_exchange_kernel(
    tiles_hbm,
    wt_ref,
    own_ref,
    cell_ref,
    out_ref,
    tin,
    sel,
    meta,
    metar,
    send_a,
    send_b,
    recv_a,
    recv_b,
    acc2,
    st2,
    st2m,
    rcv2,
    rcv2m,
    acc3,
    st3,
    st3m,
    rcv3,
    rcv3m,
    tbuf,
    hsend,
    hrecv,
    tin_sem,
    self_sem,
    s1_send,
    s1_recv,
    s2_send,
    s2_recv,
    s3_send,
    s3_recv,
    h_send,
    h_recv,
):
    ix = lax.axis_index("skyx")
    iy = lax.axis_index("skyy")
    core = ix % 2
    q = (ix // 2, iy % 4, iy // 4)

    def device(axis, step, flip):
        r = list(q)
        if step:
            r[axis] = (r[axis] + step) % 4
        c = (core + flip) % 2 if flip else core
        return (r[0] * 2 + c, r[2] * 4 + r[1])

    def around(dy, dx):
        return ((ix + dx + 8) % 8, (iy + dy + 16) % 16)

    barrier = pltpu.get_barrier_semaphore()
    peers = [device(0, 0, 1)]
    for axis in range(3):
        for step, flip in MEMBERS[:6]:
            peers.append(device(axis, step, flip))
    for dy, dx in AROUND:
        peers.append(around(dy, dx))
    for peer in peers:
        pl.semaphore_signal(barrier, inc=1, device_id=peer, device_id_type=MESH)

    tin_copies = {}
    for b in ORDER:
        tin_copies[b] = pltpu.make_async_copy(tiles_hbm.at[b], tin.at[b], tin_sem.at[b])
        tin_copies[b].start()

    own = own_ref[...]
    ox, oy = own // 16, own % 16
    oq = (ox // 2, oy % 4, oy // 4)
    oc = ox % 2
    ownf = jnp.broadcast_to(own.astype(F32), (128, 128))
    same = ownf == ownf.T
    earlier = lax.broadcasted_iota(jnp.int32, (128, 128), 0) < lax.broadcasted_iota(
        jnp.int32, (128, 128), 1
    )
    rank = jnp.sum(jnp.where(same & earlier, 1.0, 0.0), axis=0, keepdims=True).astype(jnp.int32)
    rows = lax.broadcasted_iota(jnp.int32, (256, 128), 0)
    for p in range(3):
        slot = (oq[p] * 2 + oc) * 32 + (oq[(p + 1) % 3] * 4 + oq[(p + 2) % 3]) * 2 + rank
        sel[p] = jnp.where(rows == slot, 1.0, 0.0).astype(BF16)
    meta[...] = jnp.zeros((128, 128), F32)
    meta[0:6, :] = wt_ref[...].astype(F32)
    meta[6:7, :] = cell_ref[...].astype(F32) + 1.0

    s1 = {}

    def stage1_refs(b):
        p, k = b // 2, b % 2
        return (send_a.at[p], recv_a.at[p]) if k == 0 else (send_b.at[p], recv_b.at[p])

    for n, b in enumerate(ORDER):
        p, k = b // 2, b % 2
        src, dst = stage1_refs(b)
        tin_copies[b].wait()

        def gather(c, carry, b=b, p=p, src=src):
            at = pl.ds(pl.multiple_of(c * 512, 512), 512)
            src[:, at] = jnp.dot(sel[p], tin[b, :, at], preferred_element_type=F32).astype(BF16)
            return carry

        lax.fori_loop(0, 8, gather, 0)
        if k == 0:
            src[:, 4096:4224] = lax.dot_general(
                sel[p],
                meta[...].astype(BF16),
                (((1,), (1,)), ((), ())),
                preferred_element_type=F32,
            ).astype(BF16)
        if n == 0:
            pl.semaphore_wait(barrier, len(peers))
        mine = q[p] * 2 + core
        mine_rows = pl.ds(pl.multiple_of(mine * 32, 32), 32)
        own_copy = pltpu.make_async_copy(src.at[mine_rows], dst.at[mine_rows], self_sem.at[b])
        own_copy.start()
        copies = [own_copy]
        for m, (step, flip) in enumerate(MEMBERS):
            there = ((q[p] + step) % 4) * 2 + (core + flip) % 2
            copy = pltpu.make_async_remote_copy(
                src_ref=src.at[pl.ds(pl.multiple_of(there * 32, 32), 32)],
                dst_ref=dst.at[mine_rows],
                send_sem=s1_send.at[b, m],
                recv_sem=s1_recv.at[b, m],
                device_id=device(p, step, flip),
                device_id_type=MESH,
            )
            copy.start()
            copies.append(copy)
        s1[b] = copies

    s2, s3 = {}, {}

    def encode(values, denom, size):
        top = jnp.max(jnp.abs(values), axis=1, keepdims=True)
        some = top > 1e-30
        inverse = jnp.where(some, 32767.0 / jnp.where(some, top, 1.0), 0.0)
        codes = (values * inverse + 32768.5).astype(jnp.int32)
        words = codes[:, :QUARTER] | (codes[:, QUARTER:] << 16)
        lane = lax.broadcasted_iota(jnp.int32, (size, 128), 1)
        return words, jnp.where(lane < 64, denom, top * (1.0 / 32767.0))

    def decode(words, extra):
        step = extra[:, 64:65]
        low = (words & 65535).astype(F32) - 32768.0
        high = lax.shift_right_logical(words, jnp.full_like(words, 16)).astype(F32) - 32768.0
        return low * step, high * step

    def gathered(own, own_denom, words, extras):
        low, high, denom = own[:, :QUARTER], own[:, QUARTER:], own_denom
        for k in range(3):
            a, c = decode(words[k], extras[k])
            low, high, denom = low + a, high + c, denom + extras[k][:, 0:1]
        return low, high, denom

    def pass_on(b, axis, size, words, extras, to_words, to_extras, send, recv):
        copies = []
        for step in (2, 1, 3):
            there = (q[axis] + step) % 4
            at = pl.ds(pl.multiple_of(there * size, size), size)
            for n, (src, dst) in enumerate(((words, to_words), (extras, to_extras))):
                copy = pltpu.make_async_remote_copy(
                    src_ref=src.at[b, at],
                    dst_ref=dst.at[b, step - 1],
                    send_sem=send.at[b, step - 1, n],
                    recv_sem=recv.at[b, step - 1, n],
                    device_id=device(axis, step, 0),
                    device_id_type=MESH,
                )
                copy.start()
                copies.append(copy)
        return copies

    def reduce_tiles(b):
        p, k = b // 2, b % 2
        src, dst = stage1_refs(b)
        s1[b][0].wait()
        for copy in s1[b][1:]:
            copy.wait_recv()
        if k == 0:
            metar[p] = dst[:, 4096:4224].astype(F32).T[0:8, :]
        w = metar[p, b : b + 1, :]
        code = metar[p, 6:7, :].astype(jnp.int32)
        row = lax.broadcasted_iota(jnp.int32, (128, 256), 0)
        col = lax.broadcasted_iota(jnp.int32, (128, 256), 1)
        hit = ((col % 32) // 2 == row // 8) & (code == row % 4 + 1)
        upper = (row // 4) % 2 == 0
        both = jnp.where(hit, jnp.broadcast_to(w, (128, 256)), 0.0)
        c0 = jnp.where(upper, both, 0.0).astype(BF16)
        c1 = jnp.where(upper, 0.0, both).astype(BF16)
        denom = jnp.sum(both, axis=1, keepdims=True)

        def reduce(c, carry):
            lo = pl.ds(pl.multiple_of(c * 512, 512), 512)
            hi = pl.ds(pl.multiple_of(c * 512 + HALF, 512), 512)
            acc2[b, :, lo] = jnp.dot(c0, dst[:, lo], preferred_element_type=F32) + jnp.dot(
                c1, dst[:, hi], preferred_element_type=F32
            )
            return carry

        lax.fori_loop(0, 4, reduce, 0)
        st2[b], st2m[b] = encode(acc2[b], denom, 128)
        s2[b] = pass_on(b, (p + 1) % 3, 32, st2, st2m, rcv2, rcv2m, s2_send, s2_recv)

    def second(b):
        p = b // 2
        for copy in s2[b]:
            copy.wait_recv()
        at = pl.ds(pl.multiple_of(q[(p + 1) % 3] * 32, 32), 32)
        low, high, denom = gathered(acc2[b, at, :], st2m[b, at, 0:1], rcv2[b], rcv2m[b])
        acc3[b, :, :QUARTER] = low
        acc3[b, :, QUARTER:] = high
        st3[b], st3m[b] = encode(acc3[b], denom, 32)
        s3[b] = pass_on(b, (p + 2) % 3, 8, st3, st3m, rcv3, rcv3m, s3_send, s3_recv)

    left_half = lax.broadcasted_iota(jnp.int32, (16, 128), 1) < 64

    def third(b):
        p = b // 2
        axis = (p + 2) % 3
        for copy in s3[b]:
            copy.wait_recv()
        at = pl.ds(pl.multiple_of(q[axis] * 8, 8), 8)
        low, high, denom = gathered(acc3[b, at, :], st3m[b, at, 0:1], rcv3[b], rcv3m[b])
        scale = 1.0 / (1.0 + denom)
        for j in range(8):
            c = slice(128 * j, 128 * j + 128)
            tbuf[pl.ds(j, 8, stride=16), :] = low[:, c] * scale
            tbuf[pl.ds(j + 8, 8, stride=16), :] = high[:, c] * scale
        for h in range(2):
            for cy in range(2):
                s = h * 4 + cy * 2
                a = tbuf[16 * s : 16 * s + 16, :]
                c = tbuf[16 * s + 16 : 16 * s + 32, :]
                y0 = 64 * cy + 32 * h
                out_ref[pl.ds(128 * b + y0, 16, stride=2), :] = jnp.where(
                    left_half, a, pltpu.roll(c, 64, 1)
                )
                out_ref[pl.ds(128 * b + y0 + 1, 16, stride=2), :] = jnp.where(
                    left_half, pltpu.roll(a, 64, 1), c
                )
        r = 128 * b
        n = ORDER.index(b)
        hsend[0, n] = out_ref[r : r + 8, :]
        hsend[1, n] = out_ref[r + 120 : r + 128, :]
        turned = out_ref[r : r + 128, :].T
        hsend[2, n] = turned[0:8, :]
        hsend[3, n] = turned[120:128, :]
        out_ref[1152 + 8 * b : 1160 + 8 * b, :] = turned[0:8, :]
        out_ref[1200 + 8 * b : 1208 + 8 * b, :] = turned[120:128, :]

    halo = []

    def send_halo(group):
        bands = pl.ds(3 * group, 3)
        for n, (dy, dx) in enumerate(AROUND):
            which = 0 if dy < 0 else 1 if dy > 0 else 2 if dx < 0 else 3
            copy = pltpu.make_async_remote_copy(
                src_ref=hsend.at[which, bands],
                dst_ref=hrecv.at[n, bands],
                send_sem=h_send.at[group, n],
                recv_sem=h_recv.at[group, n],
                device_id=around(dy, dx),
                device_id_type=MESH,
            )
            copy.start()
            halo.append(copy)

    for n in range(6 + 4):
        if n < 6:
            reduce_tiles(ORDER[n])
        if 0 <= n - 2 < 6:
            second(ORDER[n - 2])
        if 0 <= n - 4 < 6:
            third(ORDER[n - 4])
            if n - 4 in (2, 5):
                send_halo((n - 4) // 3)

    for b in ORDER:
        for copy in s1[b][1:] + s2[b] + s3[b]:
            copy.wait_send()
    for n, copy in enumerate(halo):
        copy.wait_recv()
        group, slot = n // 8, n % 8
        for k in range(3):
            r = 768 + 48 * slot + 8 * ORDER[3 * group + k]
            out_ref[r : r + 8, :] = hrecv[slot, 3 * group + k]
    out_ref[1248:1256, :] = jnp.zeros((8, 128), F32)
    for copy in halo:
        copy.wait_send()


def full_exchange(tiles, weights, owners, cells):
    vmem = pl.BlockSpec(memory_space=pltpu.VMEM)
    dma = pltpu.SemaphoreType.DMA
    return pl.pallas_call(
        full_exchange_kernel,
        out_shape=jax.ShapeDtypeStruct((1256, 128), F32),
        in_specs=[pl.BlockSpec(memory_space=pl.ANY), vmem, vmem, vmem],
        out_specs=vmem,
        scratch_shapes=[
            pltpu.VMEM((NB, 128, 4096), BF16),
            pltpu.VMEM((3, 256, 128), BF16),
            pltpu.VMEM((128, 128), F32),
            pltpu.VMEM((3, 8, 256), F32),
            pltpu.VMEM((3, 256, 4224), BF16),
            pltpu.VMEM((3, 256, 4096), BF16),
            pltpu.VMEM((3, 256, 4224), BF16),
            pltpu.VMEM((3, 256, 4096), BF16),
            pltpu.VMEM((NB, 128, HALF), F32),
            pltpu.VMEM((NB, 128, QUARTER), jnp.int32),
            pltpu.VMEM((NB, 128, 128), F32),
            pltpu.VMEM((NB, 3, 32, QUARTER), jnp.int32),
            pltpu.VMEM((NB, 3, 32, 128), F32),
            pltpu.VMEM((NB, 32, HALF), F32),
            pltpu.VMEM((NB, 32, QUARTER), jnp.int32),
            pltpu.VMEM((NB, 32, 128), F32),
            pltpu.VMEM((NB, 3, 8, QUARTER), jnp.int32),
            pltpu.VMEM((NB, 3, 8, 128), F32),
            pltpu.VMEM((128, 128), F32),
            pltpu.VMEM((4, NB, 8, 128), F32),
            pltpu.VMEM((8, NB, 8, 128), F32),
            dma((NB,)),
            dma((NB,)),
            dma((NB, 7)),
            dma((NB, 7)),
            dma((NB, 3, 2)),
            dma((NB, 3, 2)),
            dma((NB, 3, 2)),
            dma((NB, 3, 2)),
            dma((2, 8)),
            dma((2, 8)),
        ],
        compiler_params=pltpu.CompilerParams(
            collective_id=1, has_side_effects=True, vmem_limit_bytes=60 * 1024 * 1024
        ),
        name="full_exchange",
    )(tiles, weights, owners, cells)


def detect_kernel(
    taps_ref,
    coadd_hbm,
    w1_ref,
    b1_ref,
    w2_ref,
    b2_ref,
    psf_hbm,
    det_hbm,
    coadd_ref,
    psf_out,
    det_out,
    partial,
    ext,
    shifted,
    sides,
    sides_t,
    psf,
    taps3,
    edge3,
    hidden,
    turned,
    small,
    beside,
    w2s,
    sems,
):
    ix = lax.axis_index("skyx")
    iy = lax.axis_index("skyy")
    top, bottom = (iy > 0).astype(F32), (iy < 15).astype(F32)
    left, right = (ix > 0).astype(F32), (ix < 7).astype(F32)

    fetch = pltpu.make_async_copy(coadd_hbm, coadd_ref, sems.at[0])
    fetch.start()

    def halo(slot, b):
        r = 768 + slot * 48 + b * 8
        return coadd_ref[r : r + 8, :]

    def lanes_of(n):
        return lax.broadcasted_iota(jnp.int32, (n, 128), 1)

    small[...] = jnp.zeros((128, 128), F32)
    for b in range(NB):
        for i in range(3):
            small[pl.ds(i * 24 + b, 3, stride=8), 0:64] = w1_ref[b, i].astype(F32)
    w1 = (small[...].T[0:64, 0:72] * 0.5).astype(BF16)
    for i in range(3):
        for j in range(3):
            at = 64 * (3 * i + j)
            w2s[:, at : at + 64] = w2_ref[i, j]
    small[0:1, 0:64] = b1_ref[...] * 0.5
    small[1:2, 0:64] = b2_ref[...]
    columns = small[...].T
    bias1 = jnp.broadcast_to(columns[0:64, 0:1], (64, 256))
    bias2 = jnp.broadcast_to(columns[0:64, 1:2], (64, 256))

    taps3[...] = jnp.zeros_like(taps3)
    fetch.wait()

    pieces = []
    for b in range(NB):
        pieces += [
            halo(3, b)[2:8] * left,
            halo(8, b)[0:4],
            halo(9, b)[4:8],
            halo(2, b)[0:6] * right,
        ]
    pieces.append(jnp.zeros((8, 128), F32))
    sides[8:136, :] = jnp.concatenate(pieces, axis=0).T
    lane8 = lanes_of(8)
    for r, mid, at_left, at_right, keep in ((0, 1, 7, 6, top), (136, 0, 5, 4, bottom)):
        line = jnp.zeros((8, 128), F32)
        for b in range(NB):
            middle = halo(mid, b)
            parts = (
                (halo(at_left, b) * left, 122, 0, 6),
                (middle, 0, 6, 4),
                (middle, 124, 10, 4),
                (halo(at_right, b) * right, 0, 14, 6),
            )
            for value, start, at, size in parts:
                at = 20 * b + at
                moved = pltpu.roll(value, (at - start) % 128, 1)
                line = jnp.where((lane8 >= at) & (lane8 < at + size), moved, line)
        sides[r : r + 8, :] = line * keep

    for j in range(9):
        shifted[j] = pltpu.roll(sides[...], (-j) % 128, 1) if j else sides[...]
    owner_band = lane8 // 20

    def edge_block(start, size):
        acc = jnp.zeros((size, 128), F32)
        for i in range(9):
            for j in range(9):
                tap = jnp.full((8, 128), taps_ref[i, 0, j], F32)
                for b in range(1, NB):
                    tap = jnp.where(owner_band == b, taps_ref[i, b, j], tap)
                tap = jnp.broadcast_to(tap[0:1], (size, 128))
                acc = acc + tap * shifted[j, start + i : start + i + size, :]
        at = lax.broadcasted_iota(jnp.int32, (size, 128), 0) + start
        keep = jnp.where(at < 4, top, jnp.where(at >= 132, bottom, 1.0))
        keep = keep * jnp.where(lanes_of(size) % 20 < 10, left, right)
        return acc.astype(BF16).astype(F32) * keep

    sides[0:136, :] = edge_block(0, 136)

    for b in range(NB):
        ext[b, 8:136, :] = coadd_ref[128 * b : 128 * b + 128, :]
        ext[b, 0:8, :] = halo(1, b) * top
        ext[b, 136:144, :] = halo(0, b) * bottom
    column = lanes_of(144)

    def band(b, carry):
        near_left = pltpu.roll(shifted[0], 122 - 20 * b, 1)
        near_right = pltpu.roll(shifted[0], 114 - 20 * b, 1)
        x = ext[b]
        for j in range(9):
            if j < 4:
                moved = pltpu.roll(jnp.where(column >= 124 + j, near_left, x), 4 - j, 1)
            elif j == 4:
                moved = x
            else:
                moved = pltpu.roll(jnp.where(column < j - 4, near_right, x), 132 - j, 1)
            shifted[j + 1] = moved

        for n in range(6):
            at_rows = slice(24 * n, 24 * n + 24)
            sums = [None] * 9
            for j in range(9):
                value = shifted[j + 1, at_rows, :]
                for i in range(9):
                    term = taps_ref[i, b, j] * value
                    sums[i] = term if j == 0 else sums[i] + term
            for i in range(9):
                partial[i, at_rows, :] = sums[i]

        def block(start, size):
            acc = partial[0, start : start + size, :]
            for i in range(1, 9):
                acc = acc + partial[i, start + i : start + i + size, :]
            at = lax.broadcasted_iota(jnp.int32, (size, 128), 0) + start
            keep = jnp.where(at < 4, top, jnp.where(at >= 132, bottom, 1.0))
            v = acc.astype(BF16).astype(F32) * keep
            psf[start : start + size, :] = v
            lane = lanes_of(size)
            edge = sides[start : start + size, :]
            before = jnp.where(lane == 0, pltpu.roll(edge, 127 - 20 * b, 1), pltpu.roll(v, 1, 1))
            after = jnp.where(
                lane == 127, pltpu.roll(edge, 117 - 20 * b, 1), pltpu.roll(v, 127, 1)
            )
            for j, value in enumerate((before, v, after)):
                taps3[pl.ds(start * 24 + 8 * j + b, size, stride=24), :] = value
            edge = jnp.where(lane == 20 * b + 2, pltpu.roll(v, 20 * b + 2, 1), edge)
            edge = jnp.where(lane == 20 * b + 9, pltpu.roll(v, 20 * b + 10, 1), edge)
            sides[start : start + size, :] = edge

        block(0, 72)
        block(72, 64)
        psf_out[b] = psf[4:132, :].astype(BF16)
        return carry

    lax.fori_loop(0, NB, band, 0)

    psf_copy = pltpu.make_async_copy(psf_out, psf_hbm, sems.at[1])
    psf_copy.start()

    def silu(u):
        return u + u * jnp.tanh(u)

    sides_t[0] = sides[0:128, :].T
    tail = jnp.concatenate([sides[128:136, :], jnp.zeros((120, 128), F32)], axis=0)
    sides_t[1] = tail.T
    edge3[...] = jnp.zeros_like(edge3)
    at256 = lax.broadcasted_iota(jnp.int32, (64, 256), 1)
    ends = jnp.where(at256 == 0, top, jnp.where(at256 == 129, bottom, 1.0))
    for side, (offset, keep) in enumerate(((0, left), (9, right))):
        for t in range(2):
            for j in range(3):
                edge3[side, 8 * j : 8 * j + 6, 128 * t : 128 * t + 128] = sides_t[
                    t, pl.ds(offset + j, 6, stride=20), :
                ]
        x = edge3[side]
        rhs = jnp.concatenate([pltpu.roll(x, 256 - (2 + i), 1) for i in range(3)], axis=0)
        v = silu(jnp.dot(w1, rhs.astype(BF16), preferred_element_type=F32) + bias1)
        v = v * (ends * keep)
        beside[side, 0] = v[:, 0:128]
        beside[side, 1] = v[:, 128:256]

    lane64 = lanes_of(64)

    def pair(n, t):
        at0 = pl.ds(pl.multiple_of((2 * n + 2) * 24, 8), 72)
        at1 = pl.ds(pl.multiple_of((2 * n + 3) * 24, 8), 72)
        rhs = jnp.concatenate([taps3[at0, :], taps3[at1, :]], axis=1).astype(BF16)
        v = silu(jnp.dot(w1, rhs, preferred_element_type=F32) + bias1)
        for k in range(2):
            row, h = 2 * n + k, v[:, 128 * k : 128 * k + 128]
            near = pltpu.roll(beside[0, t], 128 * (t + 1) - row, 1)
            far = pltpu.roll(beside[1, t], 128 * (t + 1) - 1 - row, 1)
            hidden[row, 0:64] = jnp.where(lane64 == 0, near, pltpu.roll(h, 1, 1)).astype(BF16)
            hidden[row, 64:128] = h.astype(BF16)
            hidden[row, 128:192] = jnp.where(lane64 == 127, far, pltpu.roll(h, 127, 1)).astype(
                BF16
            )

    def first(n, carry):
        pair(n, 0)
        return carry

    lax.fori_loop(0, 64, first, 0, unroll=32)
    pair(64, 1)
    hidden[0] = (hidden[0].astype(F32) * top).astype(BF16)
    hidden[129] = (hidden[129].astype(F32) * bottom).astype(BF16)

    w2 = w2s[...]

    def leave(g):
        at = pl.ds(pl.multiple_of(g * 16, 16), 16)
        return pltpu.make_async_copy(det_out.at[g], det_hbm.at[:, at], sems.at[2 + g])

    def group(g, carry):
        def rows(n, inner):
            y = g * 16 + 2 * n
            rhs = jnp.concatenate(
                [hidden[pl.ds(y, 3)].reshape(576, 128), hidden[pl.ds(y + 1, 3)].reshape(576, 128)],
                axis=1,
            )
            z = jnp.dot(w2, rhs, preferred_element_type=F32) + bias2
            turned[pl.ds(2 * n, 64, stride=16), :] = z[:, 0:128]
            turned[pl.ds(2 * n + 1, 64, stride=16), :] = z[:, 128:256]
            return inner

        lax.fori_loop(0, 8, rows, 0, unroll=8)
        det_out[g] = turned[...].reshape(64, 16, 128).astype(BF16)
        leave(g).start()
        return carry

    lax.fori_loop(0, 8, group, 0)
    psf_copy.wait()
    for g in range(8):
        leave(g).wait()


def detect(taps, coadd, w1, b1, w2, b2):
    vmem = pl.BlockSpec(memory_space=pltpu.VMEM)
    anywhere = pl.BlockSpec(memory_space=pl.ANY)
    return pl.pallas_call(
        detect_kernel,
        out_shape=(
            jax.ShapeDtypeStruct((NB, 128, 128), BF16),
            jax.ShapeDtypeStruct((64, 128, 128), BF16),
        ),
        in_specs=[pl.BlockSpec(memory_space=pltpu.SMEM), anywhere] + [vmem] * 4,
        out_specs=(anywhere, anywhere),
        scratch_shapes=[
            pltpu.VMEM((1256, 128), F32),
            pltpu.VMEM((NB, 128, 128), BF16),
            pltpu.VMEM((8, 64, 16, 128), BF16),
            pltpu.VMEM((9, 144, 128), F32),
            pltpu.VMEM((NB, 144, 128), F32),
            pltpu.VMEM((10, 144, 128), F32),
            pltpu.VMEM((144, 128), F32),
            pltpu.VMEM((2, 128, 128), F32),
            pltpu.VMEM((136, 128), F32),
            pltpu.VMEM((136 * 24, 128), F32),
            pltpu.VMEM((2, 24, 256), F32),
            pltpu.VMEM((130, 192, 128), BF16),
            pltpu.VMEM((64 * 16, 128), F32),
            pltpu.VMEM((128, 128), F32),
            pltpu.VMEM((2, 2, 64, 128), F32),
            pltpu.VMEM((64, 576), BF16),
            pltpu.SemaphoreType.DMA((10,)),
        ],
        compiler_params=pltpu.CompilerParams(vmem_limit_bytes=48 * 1024 * 1024),
        name="detect",
    )(taps, coadd, w1, b1, w2, b2)


def body(
    tiles,
    tile_weight,
    owners,
    cells,
    psf_kernel,
    conv1_weight,
    conv1_bias,
    conv2_weight,
    conv2_bias,
):
    operands = (
        tiles.transpose(1, 0, 2),
        tile_weight.transpose(1, 0),
        owners.reshape(1, 128),
        cells.reshape(1, 128),
    )
    coadd = exchange(*operands)
    coadd = lax.cond(coadd[1248, 0] > 0.5, lambda: full_exchange(*operands), lambda: coadd)
    return detect(
        psf_kernel.transpose(1, 0, 2),
        coadd,
        conv1_weight.transpose(1, 2, 3, 0),
        conv1_bias.reshape(1, 64),
        conv2_weight.transpose(2, 3, 0, 1),
        conv2_bias.reshape(1, 64),
    )


def solution(mesh):
    in_specs = (
        P(("skyx", "skyy"), None, None),
        P(("skyx", "skyy"), None),
        P(("skyx", "skyy"), None),
        P(("skyx", "skyy")),
        P(),
        P(),
        P(),
        P(),
        P(),
    )
    out_specs = (P(None, "skyy", "skyx"), P(None, "skyy", "skyx"))
    return jax.shard_map(body, mesh=mesh, in_specs=in_specs, out_specs=out_specs, check_vma=False)
```
